512 devices in a mesh: lat: 64 (over y, z), lev: 8 (over x, core).
Axes of the slice: x: 4, y: 8, z: 8, core: 2. Of those that a mesh axis runs over, the one named last changes fastest.
Arguments:
- winds: float32 [2, 32, 2048, 1440], P(None, 'lev', 'lat'), may hold values from -6 to 6
- thickness: float32 [32, 2048, 1440], P('lev', 'lat'), may hold values from 0.5 to 2
- cutoff: int32 [2048], P('lat'), may hold values from 1 to 720, as said below
Outputs:
- new_winds: float32 [2, 32, 2048, 1440], P(None, 'lev', 'lat')
- new_thickness: float32 [32, 2048, 1440], P('lev', 'lat')
The draws below stay inside these ranges and needn't reach their ends.
Inputs may be any that keep to these rules, and one draw needn't show every extreme that they name: Rows outside the 384 latitudes nearest each pole have a cutoff of half of 1440; rows inside have smaller cutoffs.
All inputs are finite; a program needn't handle non-finite values.
Results may differ from the reference program's by a relative error of at most 0.0003.
Values sent between devices are 32-bit elements; how exact they have to be, the bound alone decides.
A program may use at most 64 MiB of HBM per device.

```python
import math
import jax
import jax.numpy as jnp
from jax import lax

NLON = 1440
NLAT = 2048
NLEV = 32
NPOLE = 384


def draw_cutoff(key, part):
    latitude = jnp.arange(NLAT).astype(jnp.int32)
    distance = jnp.minimum(latitude, NLAT - 1 - latitude)
    highest = NLON * 4 // 9
    jitter = jax.random.randint(key, (NLAT,), 0, max(2, NLON // 90)).astype(jnp.int32)
    polar_cut = 1 + (2 * distance + 1) * highest // (2 * NPOLE) + jitter
    return jnp.where(distance < NPOLE, polar_cut, NLON // 2).astype(jnp.int32)


def steps_of(own_key, shape, cuts, least, top_value):
    factor_of = 1.0
    for axis_at, shards_of in cuts:
        draws = jax.random.uniform(jax.random.fold_in(jax.random.fold_in(own_key, 6), axis_at), (shards_of,), jnp.float32, least / len(cuts), top_value / len(cuts))
        factor_of = factor_of * jnp.repeat(jnp.exp(draws), shape[axis_at] // shards_of).reshape((-1,) + (1,) * (len(shape) - 1 - axis_at))
    return factor_of


def centred(key, shape, width, most, shards=(), dtype=jnp.bfloat16):
    level = steps_of(key, shape, shards, -0.22, 0.18) if shards else 1.0
    values = jax.random.normal(key, shape, jnp.float32) * width * level
    return jnp.minimum(jnp.maximum(values, -most), most).astype(dtype)


def setup_inputs(seed: int = 0) -> dict:
    key_of = jax.random.split(jax.random.key(seed), 4)
    winds = centred(key_of[0], (2, NLEV, NLAT, NLON), 1.0, 6.0, ((1, 8), (2, 64)), jnp.float32)
    thickness = jnp.clip(jnp.exp(math.log(2.0) - 1.3862944 * jax.random.uniform(key_of[1], (NLEV, NLAT, NLON), jnp.float32) ** steps_of(key_of[1], (NLEV, NLAT, NLON), ((0, 8), (1, 64)), -0.2, 0.2)), 0.5, 2.0)
    cutoff = draw_cutoff(jax.random.fold_in(key_of[3], 71), 0)
    return dict(winds=winds, thickness=thickness, cutoff=cutoff)


time_step = 0.2
coriolis = 1.0

def fourier_table(lon_count):
    column = jnp.arange(lon_count).astype(jnp.int32)
    middle = lon_count // 2
    wavenumber = jnp.where(column <= middle, column, column - middle).astype(jnp.int32)
    points = jnp.arange(lon_count).astype(jnp.int32)
    phase = points[:, None] * wavenumber[None, :] % lon_count
    angle = phase.astype(jnp.float32) * (2.0 * math.pi / lon_count)
    single = (wavenumber == 0) | (wavenumber == middle)
    weight = jnp.where(single, 1.0 / math.sqrt(lon_count), math.sqrt(2.0 / lon_count)).astype(jnp.float32)
    values = jnp.where((column <= middle)[None, :], jnp.cos(angle), jnp.sin(angle)) * weight[None, :]
    return (values, wavenumber.astype(jnp.float32))

def remove_high(vectors, cuts, fourier, wavenumber):
    coeffs = jnp.dot(vectors, fourier, precision=lax.Precision.HIGHEST)
    coeffs = jnp.where(wavenumber[None, :] > cuts[:, None], coeffs, 0.0)
    return vectors - jnp.dot(coeffs, fourier.T, precision=lax.Precision.HIGHEST)

def filter_band(block, cuts, fourier, wavenumber):
    band_rows = block.shape[2]
    rows_first = jnp.transpose(block, (2, 0, 1, 3)).reshape(band_rows, -1, NLON)

    def one_row(pair):
        row_data, row_cut = pair
        return remove_high(row_data, jnp.full((row_data.shape[0],), row_cut, jnp.float32), fourier, wavenumber)
    result = lax.map(one_row, (rows_first, cuts.astype(jnp.float32)))
    return jnp.transpose(result.reshape(band_rows, 3, NLEV, NLON), (1, 2, 0, 3))

def step_fields(zonal, merid, depth, geo_pad, depth_pad, merid_pad, first_row, lat_total):
    lat_rows = depth.shape[1]
    row_index = (first_row + jnp.arange(lat_rows)).astype(jnp.float32)
    center = (row_index + 0.5) * (math.pi / lat_total) - 0.5 * math.pi
    cos_center = jnp.cos(center)[None, :, None]
    sin_center = jnp.sin(center)[None, :, None]
    edge_index = (first_row + jnp.arange(lat_rows + 1)).astype(jnp.float32)
    edge = jnp.sin(edge_index * (math.pi / lat_total))[None, :, None]
    zonal_flux = 0.25 * (depth + jnp.roll(depth, -1, axis=2)) * (zonal + jnp.roll(zonal, -1, axis=2))
    merid_flux = 0.25 * (depth_pad[:, :-1] + depth_pad[:, 1:]) * (merid_pad[:, :-1] + merid_pad[:, 1:]) * edge
    new_depth = depth - time_step * (zonal_flux - jnp.roll(zonal_flux, 1, axis=2) + (merid_flux[:, 1:] - merid_flux[:, :-1]))
    geo = geo_pad[:, 1:-1]
    new_zonal = zonal - time_step * (0.5 * (jnp.roll(geo, -1, axis=2) - jnp.roll(geo, 1, axis=2)) - coriolis * sin_center * merid)
    new_merid = merid - time_step * (0.5 * cos_center * (geo_pad[:, 2:] - geo_pad[:, :-2]) + coriolis * sin_center * zonal)
    return (new_zonal, new_merid, new_depth)

def reference(winds, thickness, cutoff):
    fields = jnp.concatenate([winds, thickness[None]], axis=0)
    fourier, wavenumber = fourier_table(NLON)
    north = filter_band(fields[:, :, :NPOLE], cutoff[:NPOLE], fourier, wavenumber)
    south = filter_band(fields[:, :, NLAT - NPOLE:], cutoff[NLAT - NPOLE:], fourier, wavenumber)
    fields = jnp.concatenate([north, fields[:, :, NPOLE:NLAT - NPOLE], south], axis=2)
    zonal, merid, depth = (fields[0], fields[1], fields[2])
    within = jnp.cumsum(depth[::-1], axis=0)[::-1] - depth
    geo = within + 0.5 * depth
    widths = ((0, 0), (1, 1), (0, 0))
    new_zonal, new_merid, new_depth = step_fields(zonal, merid, depth, jnp.pad(geo, widths), jnp.pad(depth, widths), jnp.pad(merid, widths), 0, NLAT)
    return (jnp.stack([new_zonal, new_merid], axis=0), new_depth)
```

```python
import functools
import math

import jax
import jax.numpy as jnp
import numpy as np
from jax import lax
from jax.experimental import pallas as pl
from jax.experimental.pallas import tpu as pltpu
from jax.sharding import PartitionSpec as P

MESH = pl.DeviceIdType.MESH
time_step = 0.2
coriolis = 1.0
RADIX = 12
HALO = 4
WIDE = 128
HALF3 = 0.5 * math.sqrt(3.0)


def filter_tables(lon):
    seg = lon // RADIX
    points = np.arange(WIDE) - HALO
    scale = math.sqrt(2.0 / lon)
    table = np.zeros((6, 2 * WIDE, 2 * WIDE))
    wave = np.full((6, 2 * WIDE), float(lon))
    turn = 2.0 * math.pi / lon
    j = np.arange(seg)
    for k in range(1, 6):
        m = RADIX * j + k
        angle = turn * ((points[:, None] * m[None, :]) % lon)
        table[k, :WIDE, :seg] = np.cos(angle) * scale
        table[k, :WIDE, WIDE : WIDE + seg] = np.sin(angle) * scale
        table[k, WIDE:, :seg] = -np.sin(angle) * scale
        table[k, WIDE:, WIDE : WIDE + seg] = np.cos(angle) * scale
        wave[k, :seg] = wave[k, WIDE : WIDE + seg] = np.minimum(m, lon - m)
    half = seg // 2
    m = RADIX * np.arange(half + 1)
    weight = np.where((m == 0) | (m == lon // 2), scale / math.sqrt(2.0), scale)
    angle = turn * ((points[:, None] * m[None, :]) % lon)
    table[0, :WIDE, : half + 1] = np.cos(angle) * weight
    table[0, :WIDE, half + 1 : seg] = np.sin(angle[:, 1:half]) * scale
    wave[0, : half + 1] = m
    wave[0, half + 1 : seg] = m[1:half]
    m = RADIX * np.arange(half) + RADIX // 2
    angle = turn * ((points[:, None] * m[None, :]) % lon)
    table[0, WIDE:, WIDE : WIDE + half] = np.cos(angle) * scale
    table[0, WIDE:, WIDE + half : WIDE + seg] = np.sin(angle) * scale
    wave[0, WIDE : WIDE + half] = wave[0, WIDE + half : WIDE + seg] = m
    table = table.astype(np.float32)
    high = table.astype(jnp.bfloat16)
    low = (table - high.astype(np.float32)).astype(jnp.bfloat16)
    return high, low, wave.astype(np.float32).reshape(1, 12 * WIDE)


def split(x):
    high = x.astype(jnp.bfloat16)
    return high, (x - high.astype(jnp.float32)).astype(jnp.bfloat16)


def forward12(x):
    e = [x[s] + x[s + 6] for s in range(6)]
    o = [x[s] - x[s + 6] for s in range(6)]
    ee = [e[s] + e[s + 3] for s in range(3)]
    eo = [e[s] - e[s + 3] for s in range(3)]
    sum12 = ee[1] + ee[2]
    d15, s15, d24, s24 = o[1] - o[5], o[1] + o[5], o[2] - o[4], o[2] + o[4]
    a, b = o[0] + 0.5 * d24, HALF3 * d15
    c, d = 0.5 * s15 + o[3], HALF3 * s24
    return [
        (ee[0] + sum12, eo[0] - eo[1] + eo[2]),
        (a + b, c + d),
        (eo[0] + 0.5 * (eo[1] - eo[2]), HALF3 * (eo[1] + eo[2])),
        (o[0] - d24, s15 - o[3]),
        (ee[0] - 0.5 * sum12, HALF3 * (ee[1] - ee[2])),
        (a - b, c - d),
    ]


def inverse12(z):
    (z0, z6), (r1, n1), (r2, n2), (r3, n3), (r4, n4), (r5, n5) = z
    a, b = HALF3 * (r1 - r5), 0.5 * (n1 + n5) + n3
    c, d = 0.5 * (r1 + r5) - r3, HALF3 * (n1 - n5)
    odd = [r1 + r3 + r5, b + a, c + d, n1 - n3 + n5, d - c, b - a]
    low, h4 = z0 - 0.5 * r4, HALF3 * n4
    ee = [z0 + r4, low + h4, low - h4]
    h2, hr = HALF3 * n2, 0.5 * r2
    eo = [z6 + r2, hr + h2 - z6, z6 - hr + h2]
    even = [ee[s] + eo[s] for s in range(3)] + [ee[s] - eo[s] for s in range(3)]
    return [even[s] + odd[s] for s in range(6)] + [even[s] - odd[s] for s in range(6)]


def lanes_of(shape):
    return lax.broadcasted_iota(jnp.int32, shape, len(shape) - 1)


def segments(tiles):
    lane = lanes_of(tiles[0].shape)
    out = [pltpu.roll(tiles[0], HALO, 1)]
    for s in range(1, RADIX):
        shift = 8 * s + HALO
        out.append(pltpu.roll(jnp.where(lane >= WIDE - shift, tiles[s - 1], tiles[s]), shift, 1))
    return out


def joined(segs):
    lane = lanes_of(segs[0].shape)
    out = []
    for t in range(RADIX):
        tile = pltpu.roll(segs[t], WIDE - (8 * t + HALO), 1)
        if t + 1 < RADIX:
            later = pltpu.roll(segs[t + 1], 116 - 8 * t, 1)
            tile = jnp.where(lane < 120 - 8 * t, tile, later)
        out.append(tile)
    return out


def forward_rows(tiles, y_high, y_low, row):
    lane = lanes_of((16, WIDE))
    inside = (lane >= HALO) & (lane < WIDE - HALO)
    classes = forward12(segments(tiles))
    for k, parts in enumerate(classes):
        for at, part in enumerate(parts):
            high, low = split(jnp.where(inside, part, 0.0))
            y_high[k, pl.ds(row, 16), at * WIDE : (at + 1) * WIDE] = high
            y_low[k, pl.ds(row, 16), at * WIDE : (at + 1) * WIDE] = low


def tiles_of(load):
    return [load(pl.ds(t * WIDE, WIDE)) for t in range(RADIX)]


def compute_kernel(
    lat_total,
    winds,
    thick,
    cutoff,
    below,
    edge_below,
    pack_minus,
    pack_plus,
    wave,
    f_high,
    f_low,
    new_winds,
    new_thick,
    y_high,
    y_low,
    z,
    field,
    result,
    cut,
):
    levels, rows = thick.shape[0], thick.shape[1]
    fields = 3 * levels
    main = fields * rows

    row8 = lax.broadcasted_iota(jnp.int32, (rows, WIDE), 0)
    column = jnp.zeros((rows, WIDE), jnp.float32)
    for r in range(rows):
        column = jnp.where(row8 == r, cutoff[r].astype(jnp.float32), column)
    for unit in range(fields + 1):
        cut[pl.ds(unit * rows, rows), :] = column
    at = main + rows
    minus_cut = pack_minus[:, pl.ds(1408, WIDE)][:, 64:65]
    plus_cut = pack_plus[:, pl.ds(1408, WIDE)][:, 64:65]
    cut[pl.ds(at, 8), :] = jnp.broadcast_to(minus_cut, (8, WIDE))
    cut[pl.ds(at + 8, 8), :] = jnp.broadcast_to(plus_cut, (8, WIDE))
    first = lax.broadcasted_iota(jnp.int32, (16, WIDE), 0) == 0
    cut[pl.ds(at + 16, 16), :] = jnp.where(first, minus_cut[0:1], plus_cut[0:1])

    def filter_unit(index, carry):
        base = index * rows
        for half in range(rows // 16):
            @pl.when(index < 2 * levels)
            def _():
                side, level = index // levels, index % levels
                forward_rows(tiles_of(lambda c: winds[side, level, pl.ds(half * 16, 16), c]), y_high, y_low, base + half * 16)
            @pl.when((index >= 2 * levels) & (index < fields))
            def _():
                forward_rows(tiles_of(lambda c: thick[index - 2 * levels, pl.ds(half * 16, 16), c]), y_high, y_low, base + half * 16)
        return carry

    lax.fori_loop(0, fields, filter_unit, 0)
    for half in range(rows // 16):
        forward_rows(tiles_of(lambda c: below[pl.ds(half * 16, 16), c]), y_high, y_low, main + half * 16)
    forward_rows(tiles_of(lambda c: jnp.concatenate([pack_minus[:, c], pack_plus[:, c]], axis=0)), y_high, y_low, at)
    forward_rows(tiles_of(lambda c: jnp.concatenate([edge_below[:, c], jnp.zeros((8, WIDE), jnp.float32)], axis=0)), y_high, y_low, at + 16)

    for k in range(6):
        high, low = f_high[k], f_low[k]
        yh, yl = y_high[k], y_low[k]
        coeffs = jnp.dot(
            jnp.concatenate([yh, yl, yh], axis=1),
            jnp.concatenate([high, high, low], axis=0),
            preferred_element_type=jnp.float32,
        )
        limit = cut[...]
        wanted = wave[:, pl.ds(k * 2 * WIDE, 2 * WIDE)]
        keep = jnp.concatenate([limit >= wanted[:, :WIDE], limit >= wanted[:, WIDE:]], axis=1)
        xh, xl = split(jnp.where(keep, coeffs, 0.0))
        z[k] = lax.dot_general(
            jnp.concatenate([xh, xl, xh], axis=1),
            jnp.concatenate([high, high, low], axis=1),
            (((1,), (1,)), ((), ())),
            preferred_element_type=jnp.float32,
        )

    def back(index, carry):
        for half in range(rows // 16):
            here = pl.ds(index * rows + half * 16, 16)
            parts = [(z[k, here, :WIDE], z[k, here, WIDE:]) for k in range(6)]
            for s, value in enumerate(inverse12(parts)):
                field[index, s, pl.ds(half * 16, 16), :] = value
        return carry

    lax.fori_loop(0, fields + 2, back, 0)

    lat = lax.axis_index("lat")
    row_index = (lat * rows + row8).astype(jnp.float32)
    center = (row_index + 0.5) * (math.pi / lat_total) - 0.5 * math.pi
    sin_center = (time_step * coriolis) * jnp.sin(center)
    cos_center = (0.5 * time_step) * jnp.cos(center)
    edge = (0.25 * time_step) * jnp.sin(row_index * (math.pi / lat_total))
    last_index = (lat * rows + rows + jnp.zeros((1, WIDE), jnp.int32)).astype(jnp.float32)
    last_edge = (0.25 * time_step) * jnp.sin(last_index * (math.pi / lat_total))
    top, bottom = row8 == 0, row8 == rows - 1

    def down(x, halo):
        return jnp.where(top, halo, pltpu.roll(x, 1, 0))

    def up(x, halo):
        return jnp.where(bottom, halo, pltpu.roll(x, rows - 1, 0))

    def east(x):
        return pltpu.roll(x, WIDE - 1, 1)

    def west(x):
        return pltpu.roll(x, 1, 1)

    def stencil(s, carry):
        total = field[fields, s]
        outside = field[fields + 1, s]
        minus_total, plus_total = outside[16:17], outside[17:18]
        for level in reversed(range(levels)):
            u, v, h = field[level, s], field[levels + level, s], field[2 * levels + level, s]
            hm, vm = outside[level : level + 1], outside[levels + level : levels + level + 1]
            hp, vp = outside[8 + level : 9 + level], outside[8 + levels + level : 9 + levels + level]
            geo = total + 0.5 * h
            geo_minus, geo_plus = minus_total + 0.5 * hm, plus_total + 0.5 * hp
            total, minus_total, plus_total = total + h, minus_total + hm, plus_total + hp
            zonal = (0.25 * time_step) * (h + east(h)) * (u + east(u))
            merid = (h + down(h, hm)) * (v + down(v, vm)) * edge
            beyond = (h[rows - 1 :] + hp) * (v[rows - 1 :] + vp) * last_edge
            result[2 * levels + level, s] = h - ((zonal - west(zonal)) + (up(merid, beyond) - merid))
            result[level, s] = u - (0.5 * time_step) * (east(geo) - west(geo)) + sin_center * v
            result[levels + level, s] = v - cos_center * (up(geo, geo_plus) - down(geo, geo_minus)) - sin_center * u
        return carry

    lax.fori_loop(0, RADIX, stencil, 0)

    def write(index, carry):
        for part in range(rows // 8):
            here = pl.ds(part * 8, 8)
            tiles = joined([result[index, s, here, :] for s in range(RADIX)])
            @pl.when(index < 2 * levels)
            def _():
                for t in range(RADIX):
                    new_winds[index // levels, index % levels, here, t * WIDE : (t + 1) * WIDE] = tiles[t]
            @pl.when(index >= 2 * levels)
            def _():
                for t in range(RADIX):
                    new_thick[index - 2 * levels, here, t * WIDE : (t + 1) * WIDE] = tiles[t]
        return carry

    lax.fori_loop(0, fields, write, 0)


def compute(lat_total, winds, thick, cutoff, below, edge_below, pack_minus, pack_plus):
    levels, rows, lon = thick.shape
    high, low, wave = filter_tables(lon)
    full = RADIX * WIDE
    units = (3 * levels + 2) * rows
    whole = lambda shape: pl.BlockSpec(shape, lambda i: (0,) * len(shape), pipeline_mode=pl.Buffered(1))
    return pl.pallas_call(
        functools.partial(compute_kernel, lat_total),
        grid=(1,),
        out_shape=(
            jax.ShapeDtypeStruct(winds.shape, jnp.float32),
            jax.ShapeDtypeStruct(thick.shape, jnp.float32),
        ),
        in_specs=[
            whole((2, levels, rows, full)),
            whole((levels, rows, full)),
            pl.BlockSpec(memory_space=pltpu.SMEM),
            whole((rows, full)),
            whole((8, full)),
            whole((8, full)),
            whole((8, full)),
            whole((1, full)),
            whole(high.shape),
            whole(low.shape),
        ],
        out_specs=(whole((2, levels, rows, full)), whole((levels, rows, full))),
        scratch_shapes=[
            pltpu.VMEM((6, units, 2 * WIDE), jnp.bfloat16),
            pltpu.VMEM((6, units, 2 * WIDE), jnp.bfloat16),
            pltpu.VMEM((6, units, 2 * WIDE), jnp.float32),
            pltpu.VMEM((3 * levels + 2, RADIX, rows, WIDE), jnp.float32),
            pltpu.VMEM((3 * levels, RADIX, rows, WIDE), jnp.float32),
            pltpu.VMEM((units, WIDE), jnp.float32),
        ],
        compiler_params=pltpu.CompilerParams(vmem_limit_bytes=56 << 20),
    )(winds, thick, cutoff, below, edge_below, pack_minus, pack_plus, jnp.asarray(wave), jnp.asarray(high), jnp.asarray(low))


def exchange_kernel(
    lat_count,
    lev_count,
    thick,
    winds,
    cutoff,
    below,
    edge_below,
    out_minus,
    out_plus,
    merid,
    send_minus,
    send_plus,
    from_minus,
    from_plus,
    column,
    pair,
    sums,
    chained,
    shared,
    row_column,
    row_pair,
    row_sums,
    row_chained,
    row_shared,
    local_sem,
    send_sem,
    recv_sem,
):
    levels, rows, lon = thick.shape
    full = RADIX * WIDE
    part = rows // 2
    lat, lev = lax.axis_index("lat"), lax.axis_index("lev")
    x, core = lev // 2, lev % 2
    chips = lev_count // 2
    lat_up, lat_down = (lat + 1) % lat_count, (lat + lat_count - 1) % lat_count
    partner = x * 2 + (1 - core)
    x_up, x_down = ((x + 1) % chips) * 2 + core, ((x + chips - 1) % chips) * 2 + core

    barrier = pltpu.get_barrier_semaphore()
    around = [(lat_up, lev), (lat_down, lev), (lat, partner), (lat, x_up), (lat, x_down)]
    for device in around:
        pl.semaphore_signal(barrier, inc=1, device_id=device, device_id_type=MESH)

    loads = [
        pltpu.make_async_copy(winds.at[1, :, pl.ds(at, 8), :], merid.at[i], local_sem.at[i])
        for i, at in enumerate((0, rows - 8))
    ]
    for load in loads:
        load.start()

    def remote(source, target, at, device):
        return pltpu.make_async_remote_copy(
            src_ref=source,
            dst_ref=target,
            send_sem=send_sem.at[at],
            recv_sem=recv_sem.at[at],
            device_id=device,
            device_id_type=MESH,
        )

    total = thick[0]
    for level in range(1, levels):
        total = total + thick[level]
    column[:, pl.ds(full - WIDE, WIDE)] = jnp.zeros((rows, WIDE), jnp.float32)
    column[:, pl.ds(0, lon)] = total
    for load in loads:
        load.wait()
    lane8 = lanes_of((8, WIDE))
    row8 = lax.broadcasted_iota(jnp.int32, (8, lon), 0)
    for which, (pack, row) in enumerate(((send_minus, 0), (send_plus, rows - 1))):
        inner = row % 8
        value = jnp.zeros((8, lon), jnp.float32)
        for level in range(levels):
            value = jnp.where(row8 == level, thick[level, row : row + 1, :], value)
            value = jnp.where(row8 == levels + level, merid[which, level, inner : inner + 1, :], value)
        limit = cutoff[row].astype(jnp.float32)
        pack[:, pl.ds(full - WIDE, WIDE)] = jnp.broadcast_to(limit, (8, WIDE))
        pack[:, pl.ds(0, lon)] = value

    pl.semaphore_wait(barrier, len(around))
    mine, theirs = pl.multiple_of(core * part, part), pl.multiple_of((1 - core) * part, part)
    to_minus = remote(send_minus, from_plus, 0, (lat_down, lev))
    to_plus = remote(send_plus, from_minus, 1, (lat_up, lev))
    to_pair = remote(column.at[pl.ds(theirs, part), :], pair, 2, (lat, partner))
    to_pair.start()
    to_minus.start()
    to_plus.start()

    to_pair.wait()
    own = column[pl.ds(mine, part), :]
    sums[...] = own + pair[...]
    links = [remote(sums.at[pl.ds(8 * i, 8), :], chained.at[pl.ds(8 * i, 8), :], 3 + i, (lat, x_down)) for i in range(2)]
    row_link = remote(row_sums, row_chained, 5, (lat, x_down))

    @pl.when(x == chips - 1)
    def _():
        chained[...] = jnp.zeros_like(chained)
        row_chained[...] = jnp.zeros_like(row_chained)
        for link in links:
            link.start()

    to_minus.wait()
    to_plus.wait()
    keep_minus = jnp.where(lat == 0, 0.0, 1.0)
    keep_plus = jnp.where(lat == lat_count - 1, 0.0, 1.0)
    value_minus, value_plus = from_minus[...] * keep_minus, from_plus[...] * keep_plus
    out_minus[...] = value_minus
    out_plus[...] = value_plus
    sum_minus, sum_plus = value_minus[0:1], value_plus[0:1]
    for level in range(1, levels):
        sum_minus = sum_minus + value_minus[level : level + 1]
        sum_plus = sum_plus + value_plus[level : level + 1]
    row_column[0] = jnp.where(core == 0, sum_minus, sum_plus)
    row_column[1] = jnp.where(core == 0, sum_plus, sum_minus)
    to_row_pair = remote(row_column.at[1], row_pair, 6, (lat, partner))
    to_row_pair.start()

    for i, link in enumerate(links):
        @pl.when(x < chips - 1)
        def _():
            link.wait_recv()
        @pl.when((x < chips - 1) & (x > 0))
        def _():
            sums[pl.ds(8 * i, 8), :] = sums[pl.ds(8 * i, 8), :] + chained[pl.ds(8 * i, 8), :]
            link.start()

    to_row_pair.wait()
    row_sums[...] = row_column[0] + row_pair[...]

    @pl.when(x == chips - 1)
    def _():
        row_link.start()

    upper = jnp.where(core == 0, 0.0, 1.0)
    column[pl.ds(mine, part), :] = chained[...] + upper * own
    share = remote(column.at[pl.ds(mine, part), :], shared, 7, (lat, partner))
    share.start()

    @pl.when(x < chips - 1)
    def _():
        row_link.wait_recv()

    @pl.when((x < chips - 1) & (x > 0))
    def _():
        row_sums[...] = row_sums[...] + row_chained[...]
        row_link.start()

    row_column[0] = row_chained[...] + upper * row_column[0]
    row_share = remote(row_column.at[0], row_shared, 8, (lat, partner))
    row_share.start()

    lower = 1.0 - upper
    share.wait_recv()
    below[pl.ds(mine, part), :] = (chained[...] + lower * pair[...])[:, :lon]
    below[pl.ds(theirs, part), :] = shared[...][:, :lon]
    row_share.wait_recv()
    first = (row_chained[...] + lower * row_pair[...])[:, :lon]
    second = row_shared[...][:, :lon]
    edge_below[...] = jnp.zeros_like(edge_below)
    edge_below[0:1, :] = jnp.where(core == 0, first, second)
    edge_below[1:2, :] = jnp.where(core == 0, second, first)

    share.wait_send()
    row_share.wait_send()

    @pl.when(x > 0)
    def _():
        for link in links:
            link.wait_send()
        row_link.wait_send()


def exchange(mesh_shape, winds, thick, cutoff):
    levels, rows, lon = thick.shape
    full = RADIX * WIDE
    part = rows // 2
    vmem = pl.BlockSpec(memory_space=pltpu.VMEM)
    return pl.pallas_call(
        functools.partial(exchange_kernel, mesh_shape["lat"], mesh_shape["lev"]),
        out_shape=(
            jax.ShapeDtypeStruct((rows, lon), jnp.float32),
            jax.ShapeDtypeStruct((8, lon), jnp.float32),
            jax.ShapeDtypeStruct((8, full), jnp.float32),
            jax.ShapeDtypeStruct((8, full), jnp.float32),
        ),
        in_specs=[vmem, pl.BlockSpec(memory_space=pl.ANY), pl.BlockSpec(memory_space=pltpu.SMEM)],
        out_specs=(vmem, vmem, vmem, vmem),
        scratch_shapes=[
            pltpu.VMEM((2, levels, 8, lon), jnp.float32),
            pltpu.VMEM((8, full), jnp.float32),
            pltpu.VMEM((8, full), jnp.float32),
            pltpu.VMEM((8, full), jnp.float32),
            pltpu.VMEM((8, full), jnp.float32),
            pltpu.VMEM((rows, full), jnp.float32),
            pltpu.VMEM((part, full), jnp.float32),
            pltpu.VMEM((part, full), jnp.float32),
            pltpu.VMEM((part, full), jnp.float32),
            pltpu.VMEM((part, full), jnp.float32),
            pltpu.VMEM((2, 1, full), jnp.float32),
            pltpu.VMEM((1, full), jnp.float32),
            pltpu.VMEM((1, full), jnp.float32),
            pltpu.VMEM((1, full), jnp.float32),
            pltpu.VMEM((1, full), jnp.float32),
            pltpu.SemaphoreType.DMA((2,)),
            pltpu.SemaphoreType.DMA((9,)),
            pltpu.SemaphoreType.DMA((9,)),
        ],
        compiler_params=pltpu.CompilerParams(collective_id=0, has_side_effects=True),
    )(thick, winds, cutoff)


def solution(mesh):
    shape = dict(mesh.shape)

    def per_device(winds, thickness, cutoff):
        below, edge_below, pack_minus, pack_plus = exchange(shape, winds, thickness, cutoff)
        lat_total = thickness.shape[1] * shape["lat"]
        return compute(lat_total, winds, thickness, cutoff, below, edge_below, pack_minus, pack_plus)

    return jax.shard_map(
        per_device,
        mesh=mesh,
        in_specs=(P(None, "lev", "lat", None), P("lev", "lat", None), P("lat")),
        out_specs=(P(None, "lev", "lat", None), P("lev", "lat", None)),
        check_vma=False,
    )
```

```python
import functools
import math

import jax
import jax.numpy as jnp
import numpy as np
from jax import lax
from jax.experimental import pallas as pl
from jax.experimental.pallas import tpu as pltpu
from jax.sharding import PartitionSpec as P

MESH = pl.DeviceIdType.MESH
time_step = 0.2
coriolis = 1.0
RADIX = 12
HALO = 4
WIDE = 128
HALF3 = 0.5 * math.sqrt(3.0)


def filter_tables(lon):
    seg = lon // RADIX
    points = np.arange(WIDE) - HALO
    scale = math.sqrt(2.0 / lon)
    table = np.zeros((6, 2 * WIDE, 2 * WIDE))
    wave = np.full((6, 2 * WIDE), float(lon))
    turn = 2.0 * math.pi / lon
    j = np.arange(seg)
    for k in range(1, 6):
        m = RADIX * j + k
        angle = turn * ((points[:, None] * m[None, :]) % lon)
        table[k, :WIDE, :seg] = np.cos(angle) * scale
        table[k, :WIDE, WIDE : WIDE + seg] = np.sin(angle) * scale
        table[k, WIDE:, :seg] = -np.sin(angle) * scale
        table[k, WIDE:, WIDE : WIDE + seg] = np.cos(angle) * scale
        wave[k, :seg] = wave[k, WIDE : WIDE + seg] = np.minimum(m, lon - m)
    half = seg // 2
    m = RADIX * np.arange(half + 1)
    weight = np.where((m == 0) | (m == lon // 2), scale / math.sqrt(2.0), scale)
    angle = turn * ((points[:, None] * m[None, :]) % lon)
    table[0, :WIDE, : half + 1] = np.cos(angle) * weight
    table[0, :WIDE, half + 1 : seg] = np.sin(angle[:, 1:half]) * scale
    wave[0, : half + 1] = m
    wave[0, half + 1 : seg] = m[1:half]
    m = RADIX * np.arange(half) + RADIX // 2
    angle = turn * ((points[:, None] * m[None, :]) % lon)
    table[0, WIDE:, WIDE : WIDE + half] = np.cos(angle) * scale
    table[0, WIDE:, WIDE + half : WIDE + seg] = np.sin(angle) * scale
    wave[0, WIDE : WIDE + half] = wave[0, WIDE + half : WIDE + seg] = m
    table = table.astype(np.float32)
    high = table.astype(jnp.bfloat16)
    low = (table - high.astype(np.float32)).astype(jnp.bfloat16)
    return high, low, wave.astype(np.float32).reshape(1, 12 * WIDE)


def split(x):
    high = x.astype(jnp.bfloat16)
    return high, (x - high.astype(jnp.float32)).astype(jnp.bfloat16)


def forward12(x):
    e = [x[s] + x[s + 6] for s in range(6)]
    o = [x[s] - x[s + 6] for s in range(6)]
    ee = [e[s] + e[s + 3] for s in range(3)]
    eo = [e[s] - e[s + 3] for s in range(3)]
    sum12 = ee[1] + ee[2]
    d15, s15, d24, s24 = o[1] - o[5], o[1] + o[5], o[2] - o[4], o[2] + o[4]
    a, b = o[0] + 0.5 * d24, HALF3 * d15
    c, d = 0.5 * s15 + o[3], HALF3 * s24
    return [
        (ee[0] + sum12, eo[0] - eo[1] + eo[2]),
        (a + b, c + d),
        (eo[0] + 0.5 * (eo[1] - eo[2]), HALF3 * (eo[1] + eo[2])),
        (o[0] - d24, s15 - o[3]),
        (ee[0] - 0.5 * sum12, HALF3 * (ee[1] - ee[2])),
        (a - b, c - d),
    ]


def inverse12(z):
    (z0, z6), (r1, n1), (r2, n2), (r3, n3), (r4, n4), (r5, n5) = z
    a, b = HALF3 * (r1 - r5), 0.5 * (n1 + n5) + n3
    c, d = 0.5 * (r1 + r5) - r3, HALF3 * (n1 - n5)
    odd = [r1 + r3 + r5, b + a, c + d, n1 - n3 + n5, d - c, b - a]
    low, h4 = z0 - 0.5 * r4, HALF3 * n4
    ee = [z0 + r4, low + h4, low - h4]
    h2, hr = HALF3 * n2, 0.5 * r2
    eo = [z6 + r2, hr + h2 - z6, z6 - hr + h2]
    even = [ee[s] + eo[s] for s in range(3)] + [ee[s] - eo[s] for s in range(3)]
    return [even[s] + odd[s] for s in range(6)] + [even[s] - odd[s] for s in range(6)]


def lanes_of(shape):
    return lax.broadcasted_iota(jnp.int32, shape, len(shape) - 1)


def segments(tiles):
    lane = lanes_of(tiles[0].shape)
    out = [pltpu.roll(tiles[0], HALO, 1)]
    for s in range(1, RADIX):
        shift = 8 * s + HALO
        out.append(pltpu.roll(jnp.where(lane >= WIDE - shift, tiles[s - 1], tiles[s]), shift, 1))
    return out


def joined(segs):
    lane = lanes_of(segs[0].shape)
    out = []
    for t in range(RADIX):
        tile = pltpu.roll(segs[t], WIDE - (8 * t + HALO), 1)
        if t + 1 < RADIX:
            later = pltpu.roll(segs[t + 1], 116 - 8 * t, 1)
            tile = jnp.where(lane < 120 - 8 * t, tile, later)
        out.append(tile)
    return out


def forward_rows(tiles, y_high, y_low, row):
    lane = lanes_of((16, WIDE))
    inside = (lane >= HALO) & (lane < WIDE - HALO)
    classes = forward12(segments(tiles))
    for k, parts in enumerate(classes):
        for at, part in enumerate(parts):
            high, low = split(jnp.where(inside, part, 0.0))
            y_high[k, pl.ds(row, 16), at * WIDE : (at + 1) * WIDE] = high
            y_low[k, pl.ds(row, 16), at * WIDE : (at + 1) * WIDE] = low


def tiles_of(load):
    return [load(pl.ds(t * WIDE, WIDE)) for t in range(RADIX)]


def narrow_tiles(load, lon):
    last = lon - (RADIX - 1) * WIDE
    tiles = [load(pl.ds(t * WIDE, WIDE)) for t in range(RADIX - 1)]
    end = load(pl.ds((RADIX - 1) * WIDE, last))
    return tiles + [jnp.concatenate([end, jnp.zeros((end.shape[0], WIDE - last), jnp.float32)], axis=1)]


def filter_class(k, y_high, y_low, z, cut, wave, f_high, f_low):
    high, low = f_high[k], f_low[k]
    yh, yl = y_high[k], y_low[k]
    coeffs = jnp.dot(
        jnp.concatenate([yh, yl, yh], axis=1),
        jnp.concatenate([high, high, low], axis=0),
        preferred_element_type=jnp.float32,
    )
    limit = cut[...]
    wanted = wave[:, pl.ds(k * 2 * WIDE, 2 * WIDE)]
    keep = jnp.concatenate([limit >= wanted[:, :WIDE], limit >= wanted[:, WIDE:]], axis=1)
    xh, xl = split(jnp.where(keep, coeffs, 0.0))
    z[k] = lax.dot_general(
        jnp.concatenate([xh, xl, xh], axis=1),
        jnp.concatenate([high, high, low], axis=1),
        (((1,), (1,)), ((), ())),
        preferred_element_type=jnp.float32,
    )


def step_kernel(
    lat_count,
    lev_count,
    early_count,
    thick,
    winds,
    cutoff,
    wave,
    table_high,
    table_low,
    part_winds,
    new_thick,
    delta,
    h_in,
    w_in,
    f_high,
    f_low,
    y_high,
    y_low,
    z,
    field,
    result,
    cut,
    y2_high,
    y2_low,
    z2,
    outer,
    grad,
    cut2,
    out,
    out_delta,
    send_minus,
    send_plus,
    from_minus,
    from_plus,
    column,
    below,
    pair,
    sums,
    from_upper,
    from_lower,
    relay,
    shared,
    row_column,
    row_pair,
    row_sums,
    row_upper,
    row_lower,
    row_relay,
    load_sem,
    store_sem,
    send_sem,
    recv_sem,
):
    levels, rows, lon = thick.shape
    full = RADIX * WIDE
    part = rows // 2
    fields = 3 * levels
    lat, lev = lax.axis_index("lat"), lax.axis_index("lev")
    x, core = lev // 2, lev % 2
    chips = lev_count // 2
    partner = x * 2 + (1 - core)
    x_up, x_down = ((x + 1) % chips) * 2 + core, ((x + chips - 1) % chips) * 2 + core
    has_minus, has_plus = lat > 0, lat < lat_count - 1
    lat_minus, lat_plus = jnp.maximum(lat - 1, 0), jnp.minimum(lat + 1, lat_count - 1)
    early = lat % 8 < early_count

    barrier = pltpu.get_barrier_semaphore()
    for device in ((lat, partner), (lat, x_up), (lat, x_down)):
        pl.semaphore_signal(barrier, inc=1, device_id=device, device_id_type=MESH)

    @pl.when(has_minus)
    def _():
        pl.semaphore_signal(barrier, inc=1, device_id=(lat_minus, lev), device_id_type=MESH)

    @pl.when(has_plus)
    def _():
        pl.semaphore_signal(barrier, inc=1, device_id=(lat_plus, lev), device_id_type=MESH)

    loads = [
        pltpu.make_async_copy(source, target, load_sem.at[i])
        for i, (source, target) in enumerate(
            (
                (thick, h_in),
                (winds.at[1], w_in.at[1]),
                (table_high, f_high),
                (table_low, f_low),
                (winds.at[0], w_in.at[0]),
            )
        )
    ]
    for load in loads:
        load.start()

    def remote(source, target, at, device):
        return pltpu.make_async_remote_copy(
            src_ref=source,
            dst_ref=target,
            send_sem=send_sem.at[at],
            recv_sem=recv_sem.at[at],
            device_id=device,
            device_id_type=MESH,
        )

    row32 = lax.broadcasted_iota(jnp.int32, (rows, WIDE), 0)

    def limits():
        limit = jnp.zeros((rows, WIDE), jnp.float32)
        for r in range(rows):
            limit = jnp.where(row32 == r, cutoff[r].astype(jnp.float32), limit)
        for unit in range(fields):
            cut[pl.ds(unit * rows, rows), :] = limit
        cut2[pl.ds(0, rows), :] = limit

    def forward_thick():
        def unit(level, carry):
            for half in range(rows // 16):
                here = pl.ds(half * 16, 16)
                tiles = narrow_tiles(lambda c: h_in[level, here, c], lon)
                forward_rows(tiles, y_high, y_low, (2 * levels + level) * rows + half * 16)
            return carry

        lax.fori_loop(0, levels, unit, 0)

    def forward_winds():
        def unit(index, carry):
            for half in range(rows // 16):
                here = pl.ds(half * 16, 16)
                tiles = narrow_tiles(lambda c: w_in[index // levels, index % levels, here, c], lon)
                forward_rows(tiles, y_high, y_low, index * rows + half * 16)
            return carry

        lax.fori_loop(0, 2 * levels, unit, 0)

    def products(classes):
        for k in classes:
            filter_class(k, y_high, y_low, z, cut, wave, f_high, f_low)

    def inverse():
        def unit(index, carry):
            for half in range(rows // 16):
                here = pl.ds(index * rows + half * 16, 16)
                parts = [(z[k, here, :WIDE], z[k, here, WIDE:]) for k in range(6)]
                for s, value in enumerate(inverse12(parts)):
                    field[index, s, pl.ds(half * 16, 16), :] = value
            return carry

        lax.fori_loop(0, fields, unit, 0)

    def late(stage, *args):
        @pl.when(jnp.logical_not(early))
        def _():
            stage(*args)

    loads[0].wait()
    total = h_in[0]
    for level in range(1, levels):
        total = total + h_in[level]
    column[:, pl.ds(full - WIDE, WIDE)] = jnp.zeros((rows, WIDE), jnp.float32)
    column[:, pl.ds(0, lon)] = total
    loads[1].wait()
    row8 = lax.broadcasted_iota(jnp.int32, (8, lon), 0)
    for pack, row in ((send_minus, 0), (send_plus, rows - 1)):
        value = jnp.zeros((8, lon), jnp.float32)
        for level in range(levels):
            value = jnp.where(row8 == level, h_in[level, row : row + 1, :], value)
            value = jnp.where(row8 == levels + level, w_in[1, level, row : row + 1, :], value)
        pack[:, pl.ds(full - WIDE, WIDE)] = jnp.broadcast_to(cutoff[row].astype(jnp.float32), (8, WIDE))
        pack[:, pl.ds(0, lon)] = value

    @pl.when(early)
    def _():
        for load in loads[2:]:
            load.wait()
        limits()
        forward_thick()
        forward_winds()
        products(range(6))
        inverse()

    one = lambda flag: jnp.where(flag, 1, 0)
    pl.semaphore_wait(barrier, 3 + one(has_minus) + one(has_plus))
    mine, theirs = pl.multiple_of(core * part, part), pl.multiple_of((1 - core) * part, part)
    to_pair = remote(column.at[pl.ds(theirs, part), :], pair, 0, (lat, partner))
    to_minus = remote(send_minus, from_plus, 1, (lat_minus, lev))
    to_plus = remote(send_plus, from_minus, 2, (lat_plus, lev))
    to_pair.start()

    @pl.when(has_minus)
    def _():
        to_minus.start()

    @pl.when(has_plus)
    def _():
        to_plus.start()

    late(limits)
    late(forward_thick)

    to_pair.wait()
    own = column[pl.ds(mine, part), :]
    sums[...] = own + pair[...]

    @pl.when(x == chips - 1)
    def _():
        from_upper[...] = jnp.zeros_like(from_upper)
        row_upper[...] = jnp.zeros_like(row_upper)

    @pl.when(x >= chips - 2)
    def _():
        from_lower[...] = jnp.zeros_like(from_lower)
        row_lower[...] = jnp.zeros_like(row_lower)

    pieces = [pl.ds(8 * i, 8) for i in range(2)]
    down_first = [remote(sums.at[c, :], from_upper.at[c, :], 3 + i, (lat, x_down)) for i, c in enumerate(pieces)]
    down_later = [remote(relay.at[c, :], from_upper.at[c, :], 3 + i, (lat, x_down)) for i, c in enumerate(pieces)]
    up_first = [remote(sums.at[c, :], from_lower.at[c, :], 5 + i, (lat, x_up)) for i, c in enumerate(pieces)]
    up_later = [remote(from_lower.at[c, :], from_lower.at[c, :], 5 + i, (lat, x_up)) for i, c in enumerate(pieces)]
    row_pairing = remote(row_column, row_pair, 7, (lat, partner))
    row_down_first = remote(row_sums, row_upper, 8, (lat, x_down))
    row_down_later = remote(row_relay, row_upper, 8, (lat, x_down))
    row_up_first = remote(row_sums, row_lower, 9, (lat, x_up))
    row_up_later = remote(row_lower, row_lower, 9, (lat, x_up))

    for i in range(2):
        @pl.when(x >= 2)
        def _():
            down_first[i].start()

        @pl.when(x == 3)
        def _():
            up_first[i].start()

    @pl.when(jnp.logical_not(early))
    def _():
        for load in loads[2:]:
            load.wait()
        forward_winds()

    @pl.when(has_minus)
    def _():
        to_minus.wait_send()
        to_plus.wait_recv()

    @pl.when(jnp.logical_not(has_minus))
    def _():
        from_minus[...] = jnp.zeros_like(from_minus)

    @pl.when(has_plus)
    def _():
        to_plus.wait_send()
        to_minus.wait_recv()

    @pl.when(jnp.logical_not(has_plus))
    def _():
        from_plus[...] = jnp.zeros_like(from_plus)

    for at, source in enumerate((from_minus, from_plus)):
        outside = source[0:1, :]
        for level in range(1, levels):
            outside = outside + source[level : level + 1, :]
        row_column[at] = outside
    row_pairing.start()

    for i, c in enumerate(pieces):
        @pl.when((x == 1) | (x == 2))
        def _():
            down_first[i].wait_recv()

        @pl.when(x == 1)
        def _():
            relay[c, :] = sums[c, :] + from_upper[c, :]
            down_later[i].start()

        @pl.when(x == 0)
        def _():
            up_first[i].wait_recv()
            up_later[i].start()

    late(products, range(3))

    row_pairing.wait()
    row_sums[...] = row_column[...] + row_pair[...]

    @pl.when(x >= 2)
    def _():
        row_down_first.start()

    @pl.when(x == 3)
    def _():
        row_up_first.start()

    upper = jnp.where(core == 0, 0.0, 1.0)
    lower = 1.0 - upper
    shares = []
    for i, c in enumerate(pieces):
        @pl.when(x == 0)
        def _():
            down_first[i].wait_recv()

        @pl.when(x == 1)
        def _():
            up_first[i].wait_recv()

        here = pl.ds(pl.multiple_of(mine + 8 * i, 8), 8)
        above = from_upper[c, :] + from_lower[c, :]
        below[here, :] = above + lower * pair[c, :]
        column[here, :] = above + upper * column[here, :]
        shares.append(remote(column.at[here, :], shared.at[c, :], 10 + i, (lat, partner)))
        shares[i].start()

    late(products, range(3, 6))

    @pl.when((x == 1) | (x == 2))
    def _():
        row_down_first.wait_recv()

    @pl.when(x == 1)
    def _():
        row_relay[...] = row_sums[...] + row_upper[...]
        row_down_later.start()

    @pl.when(x == 0)
    def _():
        row_up_first.wait_recv()
        row_up_later.start()

    late(inverse)

    row_index = (lat * rows + row32).astype(jnp.float32)
    lat_total = lat_count * rows
    center = (row_index + 0.5) * (math.pi / lat_total) - 0.5 * math.pi
    sin_center = (time_step * coriolis) * jnp.sin(center)
    cos_center = (0.5 * time_step) * jnp.cos(center)
    edge = (0.25 * time_step) * jnp.sin(row_index * (math.pi / lat_total))
    last_index = (lat * rows + rows + jnp.zeros((8, WIDE), jnp.int32)).astype(jnp.float32)
    last_edge = (0.25 * time_step) * jnp.sin(last_index * (math.pi / lat_total))
    top, bottom = row32 == 0, row32 == rows - 1

    def down(x, halo):
        return jnp.where(top, halo, pltpu.roll(x, 1, 0))

    def up(x, halo):
        return jnp.where(bottom, halo, pltpu.roll(x, rows - 1, 0))

    def east(x):
        return pltpu.roll(x, WIDE - 1, 1)

    def west(x):
        return pltpu.roll(x, 1, 1)

    def stencil(s, carry):
        total = jnp.zeros((rows, WIDE), jnp.float32)
        for level in reversed(range(levels)):
            u, v, h = field[level, s], field[levels + level, s], field[2 * levels + level, s]
            geo = total + 0.5 * h
            total = total + h
            zonal = (0.25 * time_step) * (h + east(h)) * (u + east(u))
            merid = jnp.where(top, 0.0, (h + pltpu.roll(h, 1, 0)) * (v + pltpu.roll(v, 1, 0)) * edge)
            result[2 * levels + level, s] = h - ((zonal - west(zonal)) + (up(merid, 0.0) - merid))
            result[level, s] = u - (0.5 * time_step) * (east(geo) - west(geo)) + sin_center * v
            result[levels + level, s] = v - cos_center * (up(geo, 0.0) - down(geo, 0.0)) - sin_center * u
        return carry

    lax.fori_loop(0, RADIX, stencil, 0)

    def write_rows(target, source, parts):
        for p in parts:
            here = pl.ds(p * 8, 8)
            tiles = joined([source(s, here) for s in range(RADIX)])
            for t in range(RADIX - 1):
                target[here, t * WIDE : (t + 1) * WIDE] = tiles[t]
            target[here, (RADIX - 1) * WIDE : lon] = tiles[RADIX - 1][:, : lon - (RADIX - 1) * WIDE]

    def write_units(first, parts):
        def unit(level, carry):
            index = first + level
            write_rows(out.at[index], lambda s, here: result[index, s, here, :], parts)
            return carry

        lax.fori_loop(0, levels, unit, 0)

    write_units(0, range(4))
    stores = [
        pltpu.make_async_copy(out.at[pl.ds(0, levels)], part_winds.at[0], store_sem.at[0]),
        pltpu.make_async_copy(out.at[pl.ds(levels, levels)], part_winds.at[1], store_sem.at[1]),
        pltpu.make_async_copy(out.at[pl.ds(2 * levels, levels)], new_thick, store_sem.at[2]),
        pltpu.make_async_copy(out_delta, delta, store_sem.at[3]),
    ]
    stores[0].start()
    write_units(levels, (1, 2))
    write_units(2 * levels, (1, 2))

    for i, c in enumerate(pieces):
        shares[i].wait()
        below[pl.ds(pl.multiple_of(theirs + 8 * i, 8), 8), :] = shared[c, :]

    @pl.when(x == 0)
    def _():
        row_down_first.wait_recv()

    @pl.when(x == 1)
    def _():
        row_up_first.wait_recv()

    minus_cut = from_minus[:, full - WIDE :][:, WIDE - 1 :]
    plus_cut = from_plus[:, full - WIDE :][:, WIDE - 1 :]
    cut2[pl.ds(rows, 8), :] = jnp.broadcast_to(minus_cut, (8, WIDE))
    cut2[pl.ds(rows + 8, 8), :] = jnp.broadcast_to(plus_cut, (8, WIDE))
    row16 = lax.broadcasted_iota(jnp.int32, (16, WIDE), 0)
    cut2[pl.ds(rows + 16, 16), :] = jnp.where(row16 == 0, minus_cut[0:1], plus_cut[0:1])
    for half in range(rows // 16):
        forward_rows(tiles_of(lambda c: below[pl.ds(half * 16, 16), c]), y2_high, y2_low, half * 16)
    forward_rows(tiles_of(lambda c: jnp.concatenate([from_minus[:, c], from_plus[:, c]], axis=0)), y2_high, y2_low, rows)
    for at in range(2):
        row_column[at] = row_upper[at] + row_lower[at] + lower * row_pair[at]

    def edge_tile(c):
        return jnp.where(row16 == 0, row_column[0, :, c], jnp.where(row16 == 1, row_column[1, :, c], 0.0))

    forward_rows(tiles_of(edge_tile), y2_high, y2_low, rows + 16)
    for k in range(6):
        filter_class(k, y2_high, y2_low, z2, cut2, wave, f_high, f_low)
    for group in range((rows + 32) // 16):
        here = pl.ds(group * 16, 16)
        parts = [(z2[k, here, :WIDE], z2[k, here, WIDE:]) for k in range(6)]
        for s, value in enumerate(inverse12(parts)):
            outer[s, here, :] = value

    eight = lax.broadcasted_iota(jnp.int32, (8, WIDE), 0)
    at_top, at_bottom = eight == 0, eight == 7
    head, tail = pl.ds(0, 8), pl.ds(rows - 8, 8)

    def patch(s, carry):
        total = outer[s, pl.ds(0, rows), :]
        sides = outer[s, pl.ds(rows, 32), :]
        grad[0, s] = -(0.5 * time_step) * (east(total) - west(total))
        grad[1, s] = -cos_center * (up(total, sides[17:18]) - down(total, sides[16:17]))
        minus_total = plus_total = jnp.zeros((1, WIDE), jnp.float32)
        for level in reversed(range(levels)):
            hm, vm = sides[level : level + 1], sides[levels + level : levels + level + 1]
            hp, vp = sides[8 + level : 9 + level], sides[8 + levels + level : 9 + levels + level]
            vi, hi = levels + level, 2 * levels + level
            geo_minus, geo_plus = minus_total + 0.5 * hm, plus_total + 0.5 * hp
            minus_total, plus_total = minus_total + hm, plus_total + hp
            result[vi, s, head, :] += jnp.where(at_top, cos_center[:8] * geo_minus, 0.0)
            result[vi, s, tail, :] -= jnp.where(at_bottom, cos_center[rows - 8 :] * geo_plus, 0.0)
            first = (field[hi, s, head, :] + hm) * (field[vi, s, head, :] + vm) * edge[:8]
            final = (field[hi, s, tail, :] + hp) * (field[vi, s, tail, :] + vp) * last_edge
            result[hi, s, head, :] += jnp.where(at_top, first, 0.0)
            result[hi, s, tail, :] -= jnp.where(at_bottom, final, 0.0)
        return carry

    lax.fori_loop(0, RADIX, patch, 0)
    write_units(levels, (0, 3))
    stores[1].start()
    write_units(2 * levels, (0, 3))
    stores[2].start()
    for which in range(2):
        write_rows(out_delta.at[which], lambda s, here: grad[which, s, here, :], range(4))
    stores[3].start()

    @pl.when(x >= 1)
    def _():
        for link in down_first:
            link.wait_send()
        row_down_first.wait_send()

    @pl.when((x == 0) | (x == 3))
    def _():
        for link in up_first:
            link.wait_send()
        row_up_first.wait_send()

    for store in stores:
        store.wait()


def step(shape, winds, thick, cutoff):
    levels, rows, lon = thick.shape
    high, low, wave = filter_tables(lon)
    full = RADIX * WIDE
    part = rows // 2
    units = 3 * levels * rows
    more = rows + 32
    f32 = lambda *dims: pltpu.VMEM(dims, jnp.float32)
    bf16 = lambda *dims: pltpu.VMEM(dims, jnp.bfloat16)
    hbm = pl.BlockSpec(memory_space=pl.ANY)
    return pl.pallas_call(
        functools.partial(step_kernel, shape["lat"], shape["lev"], 2 if shape["lat"] == 64 else 1),
        out_shape=(
            jax.ShapeDtypeStruct(winds.shape, jnp.float32),
            jax.ShapeDtypeStruct(thick.shape, jnp.float32),
            jax.ShapeDtypeStruct((2, rows, lon), jnp.float32),
        ),
        in_specs=[hbm, hbm, pl.BlockSpec(memory_space=pltpu.SMEM), pl.BlockSpec(memory_space=pltpu.VMEM), hbm, hbm],
        out_specs=(hbm, hbm, hbm),
        scratch_shapes=[
            f32(levels, rows, lon),
            f32(2, levels, rows, lon),
            bf16(*high.shape),
            bf16(*low.shape),
            bf16(6, units, 2 * WIDE),
            bf16(6, units, 2 * WIDE),
            f32(6, units, 2 * WIDE),
            f32(3 * levels, RADIX, rows, WIDE),
            f32(3 * levels, RADIX, rows, WIDE),
            f32(units, WIDE),
            bf16(6, more, 2 * WIDE),
            bf16(6, more, 2 * WIDE),
            f32(6, more, 2 * WIDE),
            f32(RADIX, more, WIDE),
            f32(2, RADIX, rows, WIDE),
            f32(more, WIDE),
            f32(3 * levels, rows, lon),
            f32(2, rows, lon),
            f32(8, full),
            f32(8, full),
            f32(8, full),
            f32(8, full),
            f32(rows, full),
            f32(rows, full),
            f32(part, full),
            f32(part, full),
            f32(part, full),
            f32(part, full),
            f32(part, full),
            f32(part, full),
            f32(2, 1, full),
            f32(2, 1, full),
            f32(2, 1, full),
            f32(2, 1, full),
            f32(2, 1, full),
            f32(2, 1, full),
            pltpu.SemaphoreType.DMA((5,)),
            pltpu.SemaphoreType.DMA((4,)),
            pltpu.SemaphoreType.DMA((12,)),
            pltpu.SemaphoreType.DMA((12,)),
        ],
        compiler_params=pltpu.CompilerParams(collective_id=0, has_side_effects=True, vmem_limit_bytes=56 << 20),
    )(thick, winds, cutoff, jnp.asarray(wave), jnp.asarray(high), jnp.asarray(low))


def solution(mesh):
    shape = dict(mesh.shape)

    def per_device(winds, thickness, cutoff):
        part_winds, new_thick, delta = step(shape, winds, thickness, cutoff)
        return part_winds + delta[:, None], new_thick

    return jax.shard_map(
        per_device,
        mesh=mesh,
        in_specs=(P(None, "lev", "lat", None), P("lev", "lat", None), P("lat")),
        out_specs=(P(None, "lev", "lat", None), P("lev", "lat", None)),
        check_vma=False,
    )
```

```python
import functools
import math

import jax
import jax.numpy as jnp
import numpy as np
from jax import lax
from jax.experimental import pallas as pl
from jax.experimental.pallas import tpu as pltpu
from jax.sharding import PartitionSpec as P

MESH = pl.DeviceIdType.MESH
time_step = 0.2
coriolis = 1.0
RADIX = 12
HALO = 4
WIDE = 128
HALF3 = 0.5 * math.sqrt(3.0)


def filter_tables(lon):
    seg = lon // RADIX
    points = np.arange(WIDE) - HALO
    scale = math.sqrt(2.0 / lon)
    table = np.zeros((6, 2 * WIDE, 2 * WIDE))
    wave = np.full((6, 2 * WIDE), float(lon))
    turn = 2.0 * math.pi / lon
    j = np.arange(seg)
    for k in range(1, 6):
        m = RADIX * j + k
        angle = turn * ((points[:, None] * m[None, :]) % lon)
        table[k, :WIDE, :seg] = np.cos(angle) * scale
        table[k, :WIDE, WIDE : WIDE + seg] = np.sin(angle) * scale
        table[k, WIDE:, :seg] = -np.sin(angle) * scale
        table[k, WIDE:, WIDE : WIDE + seg] = np.cos(angle) * scale
        wave[k, :seg] = wave[k, WIDE : WIDE + seg] = np.minimum(m, lon - m)
    half = seg // 2
    m = RADIX * np.arange(half + 1)
    weight = np.where((m == 0) | (m == lon // 2), scale / math.sqrt(2.0), scale)
    angle = turn * ((points[:, None] * m[None, :]) % lon)
    table[0, :WIDE, : half + 1] = np.cos(angle) * weight
    table[0, :WIDE, half + 1 : seg] = np.sin(angle[:, 1:half]) * scale
    wave[0, : half + 1] = m
    wave[0, half + 1 : seg] = m[1:half]
    m = RADIX * np.arange(half) + RADIX // 2
    angle = turn * ((points[:, None] * m[None, :]) % lon)
    table[0, WIDE:, WIDE : WIDE + half] = np.cos(angle) * scale
    table[0, WIDE:, WIDE + half : WIDE + seg] = np.sin(angle) * scale
    wave[0, WIDE : WIDE + half] = wave[0, WIDE + half : WIDE + seg] = m
    table = table.astype(np.float32)
    high = table.astype(jnp.bfloat16)
    low = (table - high.astype(np.float32)).astype(jnp.bfloat16)
    return high, low, wave.astype(np.float32).reshape(1, 12 * WIDE)


def split(x):
    high = x.astype(jnp.bfloat16)
    return high, (x - high.astype(jnp.float32)).astype(jnp.bfloat16)


def forward12(x):
    e = [x[s] + x[s + 6] for s in range(6)]
    o = [x[s] - x[s + 6] for s in range(6)]
    ee = [e[s] + e[s + 3] for s in range(3)]
    eo = [e[s] - e[s + 3] for s in range(3)]
    sum12 = ee[1] + ee[2]
    d15, s15, d24, s24 = o[1] - o[5], o[1] + o[5], o[2] - o[4], o[2] + o[4]
    a, b = o[0] + 0.5 * d24, HALF3 * d15
    c, d = 0.5 * s15 + o[3], HALF3 * s24
    return [
        (ee[0] + sum12, eo[0] - eo[1] + eo[2]),
        (a + b, c + d),
        (eo[0] + 0.5 * (eo[1] - eo[2]), HALF3 * (eo[1] + eo[2])),
        (o[0] - d24, s15 - o[3]),
        (ee[0] - 0.5 * sum12, HALF3 * (ee[1] - ee[2])),
        (a - b, c - d),
    ]


def inverse12(z):
    (z0, z6), (r1, n1), (r2, n2), (r3, n3), (r4, n4), (r5, n5) = z
    a, b = HALF3 * (r1 - r5), 0.5 * (n1 + n5) + n3
    c, d = 0.5 * (r1 + r5) - r3, HALF3 * (n1 - n5)
    odd = [r1 + r3 + r5, b + a, c + d, n1 - n3 + n5, d - c, b - a]
    low, h4 = z0 - 0.5 * r4, HALF3 * n4
    ee = [z0 + r4, low + h4, low - h4]
    h2, hr = HALF3 * n2, 0.5 * r2
    eo = [z6 + r2, hr + h2 - z6, z6 - hr + h2]
    even = [ee[s] + eo[s] for s in range(3)] + [ee[s] - eo[s] for s in range(3)]
    return [even[s] + odd[s] for s in range(6)] + [even[s] - odd[s] for s in range(6)]


def lanes_of(shape):
    return lax.broadcasted_iota(jnp.int32, shape, len(shape) - 1)


def segments(tiles):
    lane = lanes_of(tiles[0].shape)
    out = [pltpu.roll(tiles[0], HALO, 1)]
    for s in range(1, RADIX):
        shift = 8 * s + HALO
        out.append(pltpu.roll(jnp.where(lane >= WIDE - shift, tiles[s - 1], tiles[s]), shift, 1))
    return out


def joined(segs):
    lane = lanes_of(segs[0].shape)
    out = []
    for t in range(RADIX):
        tile = pltpu.roll(segs[t], WIDE - (8 * t + HALO), 1)
        if t + 1 < RADIX:
            later = pltpu.roll(segs[t + 1], 116 - 8 * t, 1)
            tile = jnp.where(lane < 120 - 8 * t, tile, later)
        out.append(tile)
    return out


def forward_rows(tiles, y_high, y_low, row):
    lane = lanes_of((16, WIDE))
    inside = (lane >= HALO) & (lane < WIDE - HALO)
    classes = forward12(segments(tiles))
    for k, parts in enumerate(classes):
        for at, part in enumerate(parts):
            high, low = split(jnp.where(inside, part, 0.0))
            y_high[k, pl.ds(row, 16), at * WIDE : (at + 1) * WIDE] = high
            y_low[k, pl.ds(row, 16), at * WIDE : (at + 1) * WIDE] = low


def tiles_of(load):
    return [load(pl.ds(t * WIDE, WIDE)) for t in range(RADIX)]


def narrow_tiles(load, lon):
    last = lon - (RADIX - 1) * WIDE
    tiles = [load(pl.ds(t * WIDE, WIDE)) for t in range(RADIX - 1)]
    end = load(pl.ds((RADIX - 1) * WIDE, last))
    return tiles + [jnp.concatenate([end, jnp.zeros((end.shape[0], WIDE - last), jnp.float32)], axis=1)]


def filter_class(k, y_high, y_low, z, cut, wave, f_high, f_low):
    high, low = f_high[k], f_low[k]
    yh, yl = y_high[k], y_low[k]
    coeffs = jnp.dot(
        jnp.concatenate([yh, yl, yh], axis=1),
        jnp.concatenate([high, high, low], axis=0),
        preferred_element_type=jnp.float32,
    )
    limit = cut[...]
    wanted = wave[:, pl.ds(k * 2 * WIDE, 2 * WIDE)]
    keep = jnp.concatenate([limit >= wanted[:, :WIDE], limit >= wanted[:, WIDE:]], axis=1)
    xh, xl = split(jnp.where(keep, coeffs, 0.0))
    z[k] = lax.dot_general(
        jnp.concatenate([xh, xl, xh], axis=1),
        jnp.concatenate([high, high, low], axis=1),
        (((1,), (1,)), ((), ())),
        preferred_element_type=jnp.float32,
    )


def step_kernel(
    lat_count,
    lev_count,
    early_count,
    thick,
    winds,
    cutoff,
    wave,
    table_high,
    table_low,
    part_winds,
    new_thick,
    delta,
    h_in,
    w_in,
    f_high,
    f_low,
    y_high,
    y_low,
    z,
    field,
    result,
    cut,
    y2_high,
    y2_low,
    z2,
    outer,
    grad,
    cut2,
    out,
    out_delta,
    trig,
    send_minus,
    send_plus,
    from_minus,
    from_plus,
    column,
    below,
    pair,
    sums,
    from_upper,
    from_lower,
    relay,
    shared,
    row_column,
    row_pair,
    row_sums,
    row_upper,
    row_lower,
    row_relay,
    load_sem,
    store_sem,
    send_sem,
    recv_sem,
):
    levels, rows, lon = thick.shape
    full = RADIX * WIDE
    part = rows // 2
    fields = 3 * levels
    lat, lev = lax.axis_index("lat"), lax.axis_index("lev")
    x, core = lev // 2, lev % 2
    chips = lev_count // 2
    partner = x * 2 + (1 - core)
    x_up, x_down = ((x + 1) % chips) * 2 + core, ((x + chips - 1) % chips) * 2 + core
    has_minus, has_plus = lat > 0, lat < lat_count - 1
    lat_minus, lat_plus = jnp.maximum(lat - 1, 0), jnp.minimum(lat + 1, lat_count - 1)
    early = lat % 8 < early_count

    barrier = pltpu.get_barrier_semaphore()
    for device in ((lat, partner), (lat, x_up), (lat, x_down)):
        pl.semaphore_signal(barrier, inc=1, device_id=device, device_id_type=MESH)

    @pl.when(has_minus)
    def _():
        pl.semaphore_signal(barrier, inc=1, device_id=(lat_minus, lev), device_id_type=MESH)

    @pl.when(has_plus)
    def _():
        pl.semaphore_signal(barrier, inc=1, device_id=(lat_plus, lev), device_id_type=MESH)

    loads = [
        pltpu.make_async_copy(source, target, load_sem.at[i])
        for i, (source, target) in enumerate(
            (
                (thick, h_in),
                (winds.at[1], w_in.at[1]),
                (table_high, f_high),
                (table_low, f_low),
                (winds.at[0], w_in.at[0]),
            )
        )
    ]
    for load in loads:
        load.start()

    def remote(source, target, at, device):
        return pltpu.make_async_remote_copy(
            src_ref=source,
            dst_ref=target,
            send_sem=send_sem.at[at],
            recv_sem=recv_sem.at[at],
            device_id=device,
            device_id_type=MESH,
        )

    row32 = lax.broadcasted_iota(jnp.int32, (rows, WIDE), 0)

    def limits():
        limit = jnp.zeros((rows, WIDE), jnp.float32)
        for r in range(rows):
            limit = jnp.where(row32 == r, cutoff[r].astype(jnp.float32), limit)
        for unit in range(fields):
            cut[pl.ds(unit * rows, rows), :] = limit
        cut2[pl.ds(0, rows), :] = limit

    def forward_thick():
        def unit(level, carry):
            for half in range(rows // 16):
                here = pl.ds(half * 16, 16)
                tiles = narrow_tiles(lambda c: h_in[level, here, c], lon)
                forward_rows(tiles, y_high, y_low, (2 * levels + level) * rows + half * 16)
            return carry

        lax.fori_loop(0, levels, unit, 0)

    def forward_winds():
        def unit(index, carry):
            for half in range(rows // 16):
                here = pl.ds(half * 16, 16)
                tiles = narrow_tiles(lambda c: w_in[index // levels, index % levels, here, c], lon)
                forward_rows(tiles, y_high, y_low, index * rows + half * 16)
            return carry

        lax.fori_loop(0, 2 * levels, unit, 0)

    def products(classes):
        for k in classes:
            filter_class(k, y_high, y_low, z, cut, wave, f_high, f_low)

    def inverse():
        def unit(index, carry):
            for half in range(rows // 16):
                here = pl.ds(index * rows + half * 16, 16)
                parts = [(z[k, here, :WIDE], z[k, here, WIDE:]) for k in range(6)]
                for s, value in enumerate(inverse12(parts)):
                    field[index, s, pl.ds(half * 16, 16), :] = value
            return carry

        lax.fori_loop(0, fields, unit, 0)

    loads[0].wait()
    total = h_in[0]
    for level in range(1, levels):
        total = total + h_in[level]
    column[:, pl.ds(full - WIDE, WIDE)] = jnp.zeros((rows, WIDE), jnp.float32)
    column[:, pl.ds(0, lon)] = total
    loads[1].wait()
    row8 = lax.broadcasted_iota(jnp.int32, (8, lon), 0)
    for pack, row in ((send_minus, 0), (send_plus, rows - 1)):
        value = jnp.zeros((8, lon), jnp.float32)
        for level in range(levels):
            value = jnp.where(row8 == level, h_in[level, row : row + 1, :], value)
            value = jnp.where(row8 == levels + level, w_in[1, level, row : row + 1, :], value)
        pack[:, pl.ds(full - WIDE, WIDE)] = jnp.broadcast_to(cutoff[row].astype(jnp.float32), (8, WIDE))
        pack[:, pl.ds(0, lon)] = value

    one = lambda flag: jnp.where(flag, 1, 0)
    mine, theirs = pl.multiple_of(core * part, part), pl.multiple_of((1 - core) * part, part)
    upper = jnp.where(core == 0, 0.0, 1.0)
    lower = 1.0 - upper
    pieces = [pl.ds(8 * i, 8) for i in range(2)]
    places = [pl.ds(pl.multiple_of(mine + 8 * i, 8), 8) for i in range(2)]
    to_pair = remote(column.at[pl.ds(theirs, part), :], pair, 0, (lat, partner))
    to_minus = remote(send_minus, from_plus, 1, (lat_minus, lev))
    to_plus = remote(send_plus, from_minus, 2, (lat_plus, lev))
    down_first = [remote(sums.at[c, :], from_upper.at[c, :], 3 + i, (lat, x_down)) for i, c in enumerate(pieces)]
    down_later = [remote(relay.at[c, :], from_upper.at[c, :], 3 + i, (lat, x_down)) for i, c in enumerate(pieces)]
    up_first = [remote(sums.at[c, :], from_lower.at[c, :], 5 + i, (lat, x_up)) for i, c in enumerate(pieces)]
    up_later = [remote(from_lower.at[c, :], from_lower.at[c, :], 5 + i, (lat, x_up)) for i, c in enumerate(pieces)]
    row_pairing = remote(row_column, row_pair, 7, (lat, partner))
    row_down_first = remote(row_sums, row_upper, 8, (lat, x_down))
    row_down_later = remote(row_relay, row_upper, 8, (lat, x_down))
    row_up_first = remote(row_sums, row_lower, 9, (lat, x_up))
    row_up_later = remote(row_lower, row_lower, 9, (lat, x_up))
    shares = [remote(column.at[p, :], shared.at[c, :], 10 + i, (lat, partner)) for i, (p, c) in enumerate(zip(places, pieces))]

    def enter():
        pl.semaphore_wait(barrier, 3 + one(has_minus) + one(has_plus))
        to_pair.start()

        @pl.when(has_minus)
        def _():
            to_minus.start()

        @pl.when(has_plus)
        def _():
            to_plus.start()

    def first_step():
        to_pair.wait()
        sums[...] = column[pl.ds(mine, part), :] + pair[...]
        for i in range(2):
            @pl.when(x >= 2)
            def _():
                down_first[i].start()

            @pl.when(x == 3)
            def _():
                up_first[i].start()

        @pl.when(x == chips - 1)
        def _():
            from_upper[...] = jnp.zeros_like(from_upper)
            row_upper[...] = jnp.zeros_like(row_upper)

        @pl.when(x >= chips - 2)
        def _():
            from_lower[...] = jnp.zeros_like(from_lower)
            row_lower[...] = jnp.zeros_like(row_lower)

    def second_step():
        for i, c in enumerate(pieces):
            @pl.when((x == 1) | (x == 2))
            def _():
                down_first[i].wait_recv()

            @pl.when(x == 1)
            def _():
                relay[c, :] = sums[c, :] + from_upper[c, :]
                down_later[i].start()

            @pl.when(x == 0)
            def _():
                up_first[i].wait_recv()
                up_later[i].start()

    def share():
        for i, (p, c) in enumerate(zip(places, pieces)):
            @pl.when(x == 0)
            def _():
                down_first[i].wait_recv()

            @pl.when(x == 1)
            def _():
                up_first[i].wait_recv()

            above = from_upper[c, :] + from_lower[c, :]
            below[p, :] = above + lower * pair[c, :]
            column[p, :] = above + upper * column[p, :]
            shares[i].start()

    def neighbours():
        @pl.when(has_minus)
        def _():
            to_minus.wait_send()
            to_plus.wait_recv()

        @pl.when(jnp.logical_not(has_minus))
        def _():
            from_minus[...] = jnp.zeros_like(from_minus)

        @pl.when(has_plus)
        def _():
            to_plus.wait_send()
            to_minus.wait_recv()

        @pl.when(jnp.logical_not(has_plus))
        def _():
            from_plus[...] = jnp.zeros_like(from_plus)

        for at, source in enumerate((from_minus, from_plus)):
            outside = source[0:1, :]
            for level in range(1, levels):
                outside = outside + source[level : level + 1, :]
            row_column[at] = outside
        row_pairing.start()

    def row_first():
        row_pairing.wait()
        row_sums[...] = row_column[...] + row_pair[...]

        @pl.when(x >= 2)
        def _():
            row_down_first.start()

        @pl.when(x == 3)
        def _():
            row_up_first.start()

    def row_second():
        @pl.when((x == 1) | (x == 2))
        def _():
            row_down_first.wait_recv()

        @pl.when(x == 1)
        def _():
            row_relay[...] = row_sums[...] + row_upper[...]
            row_down_later.start()

        @pl.when(x == 0)
        def _():
            row_up_first.wait_recv()
            row_up_later.start()

    row_index = (lat * rows + row32).astype(jnp.float32)
    lat_total = lat_count * rows
    center = (row_index + 0.5) * (math.pi / lat_total) - 0.5 * math.pi
    trig[0] = (time_step * coriolis) * jnp.sin(center)
    trig[1] = (0.5 * time_step) * jnp.cos(center)
    trig[2] = (0.25 * time_step) * jnp.sin(row_index * (math.pi / lat_total))
    top, bottom = row32 == 0, row32 == rows - 1

    def down(x, halo):
        return jnp.where(top, halo, pltpu.roll(x, 1, 0))

    def up(x, halo):
        return jnp.where(bottom, halo, pltpu.roll(x, rows - 1, 0))

    def east(x):
        return pltpu.roll(x, WIDE - 1, 1)

    def west(x):
        return pltpu.roll(x, 1, 1)

    def inside(first, last):
        sin_center, cos_center, edge = trig[0], trig[1], trig[2]

        def one_segment(s, carry):
            total = jnp.zeros((rows, WIDE), jnp.float32)
            for level in reversed(range(levels)):
                u, v, h = field[level, s], field[levels + level, s], field[2 * levels + level, s]
                geo = total + 0.5 * h
                total = total + h
                zonal = (0.25 * time_step) * (h + east(h)) * (u + east(u))
                merid = jnp.where(top, 0.0, (h + pltpu.roll(h, 1, 0)) * (v + pltpu.roll(v, 1, 0)) * edge)
                result[2 * levels + level, s] = h - ((zonal - west(zonal)) + (up(merid, 0.0) - merid))
                result[level, s] = u - (0.5 * time_step) * (east(geo) - west(geo)) + sin_center * v
                result[levels + level, s] = v - cos_center * (up(geo, 0.0) - down(geo, 0.0)) - sin_center * u
            return carry

        lax.fori_loop(first, last, one_segment, 0)

    def write_rows(target, source, parts):
        for p in parts:
            here = pl.ds(p * 8, 8)
            tiles = joined([source(s, here) for s in range(RADIX)])
            for t in range(RADIX - 1):
                target[here, t * WIDE : (t + 1) * WIDE] = tiles[t]
            target[here, (RADIX - 1) * WIDE : lon] = tiles[RADIX - 1][:, : lon - (RADIX - 1) * WIDE]

    def write_units(first, parts):
        def unit(level, carry):
            index = first + level
            write_rows(out.at[index], lambda s, here: result[index, s, here, :], parts)
            return carry

        lax.fori_loop(0, levels, unit, 0)

    stores = [
        pltpu.make_async_copy(out.at[pl.ds(0, levels)], part_winds.at[0], store_sem.at[0]),
        pltpu.make_async_copy(out.at[pl.ds(levels, levels)], part_winds.at[1], store_sem.at[1]),
        pltpu.make_async_copy(out.at[pl.ds(2 * levels, levels)], new_thick, store_sem.at[2]),
        pltpu.make_async_copy(out_delta, delta, store_sem.at[3]),
    ]

    def write_first():
        write_units(0, range(4))
        stores[0].start()

    def write_middle():
        write_units(levels, (1, 2))
        write_units(2 * levels, (1, 2))

    def rest_of_loads():
        for load in loads[2:]:
            load.wait()

    def run(*stages):
        for stage in stages:
            stage()

    half_way = RADIX // 2
    some = lambda stage, *args: functools.partial(stage, *args)

    @pl.when(early)
    def _():
        run(rest_of_loads, limits, forward_thick, forward_winds, some(products, range(6)), inverse)
        run(enter, first_step, neighbours, some(inside, 0, half_way), row_first, second_step)
        run(some(inside, half_way, RADIX), row_second, share, write_first, write_middle)

    @pl.when(jnp.logical_not(early))
    def _():
        run(enter, limits, forward_thick, first_step, rest_of_loads, forward_winds, some(products, range(3)))
        run(second_step, some(products, range(3, 6)), share, inverse, neighbours)
        run(some(inside, 0, half_way), row_first, some(inside, half_way, RADIX), write_first, row_second, write_middle)

    for i, c in enumerate(pieces):
        shares[i].wait()
        below[pl.ds(pl.multiple_of(theirs + 8 * i, 8), 8), :] = shared[c, :]

    @pl.when(x == 0)
    def _():
        row_down_first.wait_recv()

    @pl.when(x == 1)
    def _():
        row_up_first.wait_recv()

    sin_center, cos_center, edge = trig[0], trig[1], trig[2]
    last_index = (lat * rows + rows + jnp.zeros((8, WIDE), jnp.int32)).astype(jnp.float32)
    last_edge = (0.25 * time_step) * jnp.sin(last_index * (math.pi / lat_total))
    minus_cut = from_minus[:, full - WIDE :][:, WIDE - 1 :]
    plus_cut = from_plus[:, full - WIDE :][:, WIDE - 1 :]
    cut2[pl.ds(rows, 8), :] = jnp.broadcast_to(minus_cut, (8, WIDE))
    cut2[pl.ds(rows + 8, 8), :] = jnp.broadcast_to(plus_cut, (8, WIDE))
    row16 = lax.broadcasted_iota(jnp.int32, (16, WIDE), 0)
    cut2[pl.ds(rows + 16, 16), :] = jnp.where(row16 == 0, minus_cut[0:1], plus_cut[0:1])
    for half in range(rows // 16):
        forward_rows(tiles_of(lambda c: below[pl.ds(half * 16, 16), c]), y2_high, y2_low, half * 16)
    forward_rows(tiles_of(lambda c: jnp.concatenate([from_minus[:, c], from_plus[:, c]], axis=0)), y2_high, y2_low, rows)
    for at in range(2):
        row_column[at] = row_upper[at] + row_lower[at] + lower * row_pair[at]

    def edge_tile(c):
        return jnp.where(row16 == 0, row_column[0, :, c], jnp.where(row16 == 1, row_column[1, :, c], 0.0))

    forward_rows(tiles_of(edge_tile), y2_high, y2_low, rows + 16)
    for k in range(6):
        filter_class(k, y2_high, y2_low, z2, cut2, wave, f_high, f_low)
    for group in range((rows + 32) // 16):
        here = pl.ds(group * 16, 16)
        parts = [(z2[k, here, :WIDE], z2[k, here, WIDE:]) for k in range(6)]
        for s, value in enumerate(inverse12(parts)):
            outer[s, here, :] = value

    eight = lax.broadcasted_iota(jnp.int32, (8, WIDE), 0)
    at_top, at_bottom = eight == 0, eight == 7
    head, tail = pl.ds(0, 8), pl.ds(rows - 8, 8)

    def patch(s, carry):
        total = outer[s, pl.ds(0, rows), :]
        sides = outer[s, pl.ds(rows, 32), :]
        grad[0, s] = -(0.5 * time_step) * (east(total) - west(total))
        grad[1, s] = -cos_center * (up(total, sides[17:18]) - down(total, sides[16:17]))
        minus_total = plus_total = jnp.zeros((1, WIDE), jnp.float32)
        for level in reversed(range(levels)):
            hm, vm = sides[level : level + 1], sides[levels + level : levels + level + 1]
            hp, vp = sides[8 + level : 9 + level], sides[8 + levels + level : 9 + levels + level]
            vi, hi = levels + level, 2 * levels + level
            geo_minus, geo_plus = minus_total + 0.5 * hm, plus_total + 0.5 * hp
            minus_total, plus_total = minus_total + hm, plus_total + hp
            result[vi, s, head, :] += jnp.where(at_top, cos_center[:8] * geo_minus, 0.0)
            result[vi, s, tail, :] -= jnp.where(at_bottom, cos_center[rows - 8 :] * geo_plus, 0.0)
            first = (field[hi, s, head, :] + hm) * (field[vi, s, head, :] + vm) * edge[:8]
            final = (field[hi, s, tail, :] + hp) * (field[vi, s, tail, :] + vp) * last_edge
            result[hi, s, head, :] += jnp.where(at_top, first, 0.0)
            result[hi, s, tail, :] -= jnp.where(at_bottom, final, 0.0)
        return carry

    lax.fori_loop(0, RADIX, patch, 0)
    write_units(levels, (0, 3))
    stores[1].start()
    write_units(2 * levels, (0, 3))
    stores[2].start()
    for which in range(2):
        write_rows(out_delta.at[which], lambda s, here: grad[which, s, here, :], range(4))
    stores[3].start()

    @pl.when(x >= 1)
    def _():
        for link in down_first:
            link.wait_send()
        row_down_first.wait_send()

    @pl.when((x == 0) | (x == 3))
    def _():
        for link in up_first:
            link.wait_send()
        row_up_first.wait_send()

    for store in stores:
        store.wait()


def step(shape, winds, thick, cutoff):
    levels, rows, lon = thick.shape
    high, low, wave = filter_tables(lon)
    full = RADIX * WIDE
    part = rows // 2
    units = 3 * levels * rows
    more = rows + 32
    f32 = lambda *dims: pltpu.VMEM(dims, jnp.float32)
    bf16 = lambda *dims: pltpu.VMEM(dims, jnp.bfloat16)
    hbm = pl.BlockSpec(memory_space=pl.ANY)
    return pl.pallas_call(
        functools.partial(step_kernel, shape["lat"], shape["lev"], 1),
        out_shape=(
            jax.ShapeDtypeStruct(winds.shape, jnp.float32),
            jax.ShapeDtypeStruct(thick.shape, jnp.float32),
            jax.ShapeDtypeStruct((2, rows, lon), jnp.float32),
        ),
        in_specs=[hbm, hbm, pl.BlockSpec(memory_space=pltpu.SMEM), pl.BlockSpec(memory_space=pltpu.VMEM), hbm, hbm],
        out_specs=(hbm, hbm, hbm),
        scratch_shapes=[
            f32(levels, rows, lon),
            f32(2, levels, rows, lon),
            bf16(*high.shape),
            bf16(*low.shape),
            bf16(6, units, 2 * WIDE),
            bf16(6, units, 2 * WIDE),
            f32(6, units, 2 * WIDE),
            f32(3 * levels, RADIX, rows, WIDE),
            f32(3 * levels, RADIX, rows, WIDE),
            f32(units, WIDE),
            bf16(6, more, 2 * WIDE),
            bf16(6, more, 2 * WIDE),
            f32(6, more, 2 * WIDE),
            f32(RADIX, more, WIDE),
            f32(2, RADIX, rows, WIDE),
            f32(more, WIDE),
            f32(3 * levels, rows, lon),
            f32(2, rows, lon),
            f32(3, rows, WIDE),
            f32(8, full),
            f32(8, full),
            f32(8, full),
            f32(8, full),
            f32(rows, full),
            f32(rows, full),
            f32(part, full),
            f32(part, full),
            f32(part, full),
            f32(part, full),
            f32(part, full),
            f32(part, full),
            f32(2, 1, full),
            f32(2, 1, full),
            f32(2, 1, full),
            f32(2, 1, full),
            f32(2, 1, full),
            f32(2, 1, full),
            pltpu.SemaphoreType.DMA((5,)),
            pltpu.SemaphoreType.DMA((4,)),
            pltpu.SemaphoreType.DMA((12,)),
            pltpu.SemaphoreType.DMA((12,)),
        ],
        compiler_params=pltpu.CompilerParams(collective_id=0, has_side_effects=True, vmem_limit_bytes=56 << 20),
    )(thick, winds, cutoff, jnp.asarray(wave), jnp.asarray(high), jnp.asarray(low))


def last_kernel(part_winds, part_thick, delta, new_winds, new_thick, w, t, d, in_sem, out_sem):
    levels = t.shape[0]
    pieces = [(part_winds.at[f, level], w.at[f, level], new_winds.at[f, level]) for f in range(2) for level in range(levels)]
    pieces.append((part_thick, t, new_thick))
    grads = [pltpu.make_async_copy(delta.at[f], d.at[f], in_sem.at[len(pieces) + f]) for f in range(2)]
    loads = [pltpu.make_async_copy(source, held, in_sem.at[i]) for i, (source, held, _) in enumerate(pieces)]
    stores = [pltpu.make_async_copy(held, target, out_sem.at[i]) for i, (_, held, target) in enumerate(pieces)]
    for f in range(2):
        grads[f].start()
        for load in loads[f * levels : (f + 1) * levels]:
            load.start()
    loads[-1].start()
    for f in range(2):
        grads[f].wait()
        for level in range(levels):
            at = f * levels + level
            loads[at].wait()
            w[f, level] = w[f, level] + d[f]
            stores[at].start()
    loads[-1].wait()
    stores[-1].start()
    for store in stores:
        store.wait()


def last(part_winds, part_thick, delta):
    hbm = pl.BlockSpec(memory_space=pl.ANY)
    count = 2 * part_thick.shape[0] + 1
    return pl.pallas_call(
        last_kernel,
        out_shape=(
            jax.ShapeDtypeStruct(part_winds.shape, jnp.float32),
            jax.ShapeDtypeStruct(part_thick.shape, jnp.float32),
        ),
        in_specs=[hbm, hbm, hbm],
        out_specs=(hbm, hbm),
        scratch_shapes=[
            pltpu.VMEM(part_winds.shape, jnp.float32),
            pltpu.VMEM(part_thick.shape, jnp.float32),
            pltpu.VMEM(delta.shape, jnp.float32),
            pltpu.SemaphoreType.DMA((count + 2,)),
            pltpu.SemaphoreType.DMA((count,)),
        ],
    )(part_winds, part_thick, delta)


def solution(mesh):
    shape = dict(mesh.shape)

    def per_device(winds, thickness, cutoff):
        return last(*step(shape, winds, thickness, cutoff))

    return jax.shard_map(
        per_device,
        mesh=mesh,
        in_specs=(P(None, "lev", "lat", None), P("lev", "lat", None), P("lat")),
        out_specs=(P(None, "lev", "lat", None), P("lev", "lat", None)),
        check_vma=False,
    )
```

```python
import functools
import math

import jax
import jax.numpy as jnp
import numpy as np
from jax import lax
from jax.experimental import pallas as pl
from jax.experimental.pallas import tpu as pltpu
from jax.sharding import PartitionSpec as P

MESH = pl.DeviceIdType.MESH
time_step = 0.2
coriolis = 1.0
RADIX = 12
HALO = 4
WIDE = 128
HALF3 = 0.5 * math.sqrt(3.0)


def filter_tables(lon):
    seg = lon // RADIX
    points = np.arange(WIDE) - HALO
    scale = math.sqrt(2.0 / lon)
    table = np.zeros((6, 2 * WIDE, 2 * WIDE))
    wave = np.full((6, 2 * WIDE), float(lon))
    turn = 2.0 * math.pi / lon
    j = np.arange(seg)
    for k in range(1, 6):
        m = RADIX * j + k
        angle = turn * ((points[:, None] * m[None, :]) % lon)
        table[k, :WIDE, :seg] = np.cos(angle) * scale
        table[k, :WIDE, WIDE : WIDE + seg] = np.sin(angle) * scale
        table[k, WIDE:, :seg] = -np.sin(angle) * scale
        table[k, WIDE:, WIDE : WIDE + seg] = np.cos(angle) * scale
        wave[k, :seg] = wave[k, WIDE : WIDE + seg] = np.minimum(m, lon - m)
    half = seg // 2
    m = RADIX * np.arange(half + 1)
    weight = np.where((m == 0) | (m == lon // 2), scale / math.sqrt(2.0), scale)
    angle = turn * ((points[:, None] * m[None, :]) % lon)
    table[0, :WIDE, : half + 1] = np.cos(angle) * weight
    table[0, :WIDE, half + 1 : seg] = np.sin(angle[:, 1:half]) * scale
    wave[0, : half + 1] = m
    wave[0, half + 1 : seg] = m[1:half]
    m = RADIX * np.arange(half) + RADIX // 2
    angle = turn * ((points[:, None] * m[None, :]) % lon)
    table[0, WIDE:, WIDE : WIDE + half] = np.cos(angle) * scale
    table[0, WIDE:, WIDE + half : WIDE + seg] = np.sin(angle) * scale
    wave[0, WIDE : WIDE + half] = wave[0, WIDE + half : WIDE + seg] = m
    table = table.astype(np.float32)
    high = table.astype(jnp.bfloat16)
    low = (table - high.astype(np.float32)).astype(jnp.bfloat16)
    return high, low, wave.astype(np.float32).reshape(1, 12 * WIDE)


def split(x):
    high = x.astype(jnp.bfloat16)
    return high, (x - high.astype(jnp.float32)).astype(jnp.bfloat16)


def forward12(x):
    e = [x[s] + x[s + 6] for s in range(6)]
    o = [x[s] - x[s + 6] for s in range(6)]
    ee = [e[s] + e[s + 3] for s in range(3)]
    eo = [e[s] - e[s + 3] for s in range(3)]
    sum12 = ee[1] + ee[2]
    d15, s15, d24, s24 = o[1] - o[5], o[1] + o[5], o[2] - o[4], o[2] + o[4]
    a, b = o[0] + 0.5 * d24, HALF3 * d15
    c, d = 0.5 * s15 + o[3], HALF3 * s24
    return [
        (ee[0] + sum12, eo[0] - eo[1] + eo[2]),
        (a + b, c + d),
        (eo[0] + 0.5 * (eo[1] - eo[2]), HALF3 * (eo[1] + eo[2])),
        (o[0] - d24, s15 - o[3]),
        (ee[0] - 0.5 * sum12, HALF3 * (ee[1] - ee[2])),
        (a - b, c - d),
    ]


def inverse12(z):
    (z0, z6), (r1, n1), (r2, n2), (r3, n3), (r4, n4), (r5, n5) = z
    a, b = HALF3 * (r1 - r5), 0.5 * (n1 + n5) + n3
    c, d = 0.5 * (r1 + r5) - r3, HALF3 * (n1 - n5)
    odd = [r1 + r3 + r5, b + a, c + d, n1 - n3 + n5, d - c, b - a]
    low, h4 = z0 - 0.5 * r4, HALF3 * n4
    ee = [z0 + r4, low + h4, low - h4]
    h2, hr = HALF3 * n2, 0.5 * r2
    eo = [z6 + r2, hr + h2 - z6, z6 - hr + h2]
    even = [ee[s] + eo[s] for s in range(3)] + [ee[s] - eo[s] for s in range(3)]
    return [even[s] + odd[s] for s in range(6)] + [even[s] - odd[s] for s in range(6)]


def lanes_of(shape):
    return lax.broadcasted_iota(jnp.int32, shape, len(shape) - 1)


def segments(tiles):
    lane = lanes_of(tiles[0].shape)
    out = [pltpu.roll(tiles[0], HALO, 1)]
    for s in range(1, RADIX):
        shift = 8 * s + HALO
        out.append(pltpu.roll(jnp.where(lane >= WIDE - shift, tiles[s - 1], tiles[s]), shift, 1))
    return out


def joined(segs):
    lane = lanes_of(segs[0].shape)
    out = []
    for t in range(RADIX):
        tile = pltpu.roll(segs[t], WIDE - (8 * t + HALO), 1)
        if t + 1 < RADIX:
            later = pltpu.roll(segs[t + 1], 116 - 8 * t, 1)
            tile = jnp.where(lane < 120 - 8 * t, tile, later)
        out.append(tile)
    return out


def forward_rows(tiles, y_high, y_low, row):
    lane = lanes_of((16, WIDE))
    inside = (lane >= HALO) & (lane < WIDE - HALO)
    classes = forward12(segments(tiles))
    for k, parts in enumerate(classes):
        for at, part in enumerate(parts):
            high, low = split(jnp.where(inside, part, 0.0))
            y_high[k, pl.ds(row, 16), at * WIDE : (at + 1) * WIDE] = high
            y_low[k, pl.ds(row, 16), at * WIDE : (at + 1) * WIDE] = low


def tiles_of(load):
    return [load(pl.ds(t * WIDE, WIDE)) for t in range(RADIX)]


def narrow_tiles(load, lon):
    last = lon - (RADIX - 1) * WIDE
    tiles = [load(pl.ds(t * WIDE, WIDE)) for t in range(RADIX - 1)]
    end = load(pl.ds((RADIX - 1) * WIDE, last))
    return tiles + [jnp.concatenate([end, jnp.zeros((end.shape[0], WIDE - last), jnp.float32)], axis=1)]


def filter_class(k, y_high, y_low, z, cut, wave, f_high, f_low):
    high, low = f_high[k], f_low[k]
    yh, yl = y_high[k], y_low[k]
    coeffs = jnp.dot(
        jnp.concatenate([yh, yl, yh], axis=1),
        jnp.concatenate([high, high, low], axis=0),
        preferred_element_type=jnp.float32,
    )
    limit = cut[...]
    wanted = wave[:, pl.ds(k * 2 * WIDE, 2 * WIDE)]
    keep = jnp.concatenate([limit >= wanted[:, :WIDE], limit >= wanted[:, WIDE:]], axis=1)
    xh, xl = split(jnp.where(keep, coeffs, 0.0))
    z[k] = lax.dot_general(
        jnp.concatenate([xh, xl, xh], axis=1),
        jnp.concatenate([high, high, low], axis=1),
        (((1,), (1,)), ((), ())),
        preferred_element_type=jnp.float32,
    )


def step_kernel(
    lat_count,
    lev_count,
    early_count,
    thick,
    winds,
    cutoff_in,
    wave_in,
    table_high,
    table_low,
    part_winds,
    new_thick,
    delta,
    cutoff,
    wave,
    h_in,
    w_in,
    f_high,
    f_low,
    y_high,
    y_low,
    z,
    field,
    result,
    cut,
    y2_high,
    y2_low,
    z2,
    outer,
    grad,
    cut2,
    out,
    out_delta,
    trig,
    send_minus,
    send_plus,
    from_minus,
    from_plus,
    column,
    below,
    pair,
    sums,
    from_upper,
    from_lower,
    relay,
    shared,
    row_column,
    row_pair,
    row_sums,
    row_upper,
    row_lower,
    row_relay,
    load_sem,
    store_sem,
    send_sem,
    recv_sem,
):
    levels, rows, lon = thick.shape
    full = RADIX * WIDE
    part = rows // 2
    fields = 3 * levels
    lat, lev = lax.axis_index("lat"), lax.axis_index("lev")
    x, core = lev // 2, lev % 2
    chips = lev_count // 2
    partner = x * 2 + (1 - core)
    x_up, x_down = ((x + 1) % chips) * 2 + core, ((x + chips - 1) % chips) * 2 + core
    has_minus, has_plus = lat > 0, lat < lat_count - 1
    lat_minus, lat_plus = jnp.maximum(lat - 1, 0), jnp.minimum(lat + 1, lat_count - 1)
    early = lat % 8 < early_count
    after_early = lat % 8 == early_count

    barrier = pltpu.get_barrier_semaphore()
    for device in ((lat, partner), (lat, x_up), (lat, x_down)):
        pl.semaphore_signal(barrier, inc=1, device_id=device, device_id_type=MESH)

    @pl.when(has_minus)
    def _():
        pl.semaphore_signal(barrier, inc=1, device_id=(lat_minus, lev), device_id_type=MESH)

    @pl.when(has_plus)
    def _():
        pl.semaphore_signal(barrier, inc=1, device_id=(lat_plus, lev), device_id_type=MESH)

    loads = [
        pltpu.make_async_copy(source, target, load_sem.at[i])
        for i, (source, target) in enumerate(
            (
                (thick, h_in),
                (winds.at[1], w_in.at[1]),
                (cutoff_in, cutoff),
                (wave_in, wave),
                (table_high, f_high),
                (table_low, f_low),
                (winds.at[0], w_in.at[0]),
            )
        )
    ]
    for load in loads[:3]:
        load.start()

    def remote(source, target, at, device):
        return pltpu.make_async_remote_copy(
            src_ref=source,
            dst_ref=target,
            send_sem=send_sem.at[at],
            recv_sem=recv_sem.at[at],
            device_id=device,
            device_id_type=MESH,
        )

    row32 = lax.broadcasted_iota(jnp.int32, (rows, WIDE), 0)

    def limits():
        limit = jnp.zeros((rows, WIDE), jnp.float32)
        for r in range(rows):
            limit = jnp.where(row32 == r, cutoff[r].astype(jnp.float32), limit)
        for unit in range(fields):
            cut[pl.ds(unit * rows, rows), :] = limit
        cut2[pl.ds(0, rows), :] = limit

    def forward_thick():
        def unit(level, carry):
            for half in range(rows // 16):
                here = pl.ds(half * 16, 16)
                tiles = narrow_tiles(lambda c: h_in[level, here, c], lon)
                forward_rows(tiles, y_high, y_low, (2 * levels + level) * rows + half * 16)
            return carry

        lax.fori_loop(0, levels, unit, 0)

    def forward_winds():
        def unit(index, carry):
            for half in range(rows // 16):
                here = pl.ds(half * 16, 16)
                tiles = narrow_tiles(lambda c: w_in[index // levels, index % levels, here, c], lon)
                forward_rows(tiles, y_high, y_low, index * rows + half * 16)
            return carry

        lax.fori_loop(0, 2 * levels, unit, 0)

    def products(classes):
        for k in classes:
            filter_class(k, y_high, y_low, z, cut, wave, f_high, f_low)

    def inverse():
        def unit(index, carry):
            for half in range(rows // 16):
                here = pl.ds(index * rows + half * 16, 16)
                parts = [(z[k, here, :WIDE], z[k, here, WIDE:]) for k in range(6)]
                for s, value in enumerate(inverse12(parts)):
                    field[index, s, pl.ds(half * 16, 16), :] = value
            return carry

        lax.fori_loop(0, fields, unit, 0)

    loads[0].wait()
    for load in loads[3:]:
        load.start()
    total = h_in[0]
    for level in range(1, levels):
        total = total + h_in[level]
    column[:, pl.ds(full - WIDE, WIDE)] = jnp.zeros((rows, WIDE), jnp.float32)
    column[:, pl.ds(0, lon)] = total
    loads[1].wait()
    loads[2].wait()
    row8 = lax.broadcasted_iota(jnp.int32, (8, lon), 0)
    for pack, row in ((send_minus, 0), (send_plus, rows - 1)):
        value = jnp.zeros((8, lon), jnp.float32)
        for level in range(levels):
            value = jnp.where(row8 == level, h_in[level, row : row + 1, :], value)
            value = jnp.where(row8 == levels + level, w_in[1, level, row : row + 1, :], value)
        pack[:, pl.ds(full - WIDE, WIDE)] = jnp.broadcast_to(cutoff[row].astype(jnp.float32), (8, WIDE))
        pack[:, pl.ds(0, lon)] = value

    one = lambda flag: jnp.where(flag, 1, 0)
    mine, theirs = pl.multiple_of(core * part, part), pl.multiple_of((1 - core) * part, part)
    upper = jnp.where(core == 0, 0.0, 1.0)
    lower = 1.0 - upper
    chunks = [(8 * r, full // 2 * c) for r in range(part // 8) for c in range(2)]
    pieces = [(pl.ds(r, 8), pl.ds(c, full // 2)) for r, c in chunks]
    places = [(pl.ds(pl.multiple_of(mine + r, 8), 8), pl.ds(c, full // 2)) for r, c in chunks]
    others = [(pl.ds(pl.multiple_of(theirs + r, 8), 8), pl.ds(c, full // 2)) for r, c in chunks]
    count = len(pieces)
    to_pair = remote(column.at[pl.ds(theirs, part), :], pair, 0, (lat, partner))
    to_minus = remote(send_minus, from_plus, 1, (lat_minus, lev))
    to_plus = remote(send_plus, from_minus, 2, (lat_plus, lev))
    down_first = [remote(sums.at[*c], from_upper.at[*c], 3 + i, (lat, x_down)) for i, c in enumerate(pieces)]
    down_later = [remote(relay.at[*c], from_upper.at[*c], 3 + i, (lat, x_down)) for i, c in enumerate(pieces)]
    up_first = [remote(sums.at[*c], from_lower.at[*c], 3 + count + i, (lat, x_up)) for i, c in enumerate(pieces)]
    up_later = [remote(from_lower.at[*c], from_lower.at[*c], 3 + count + i, (lat, x_up)) for i, c in enumerate(pieces)]
    row_pairing = remote(row_column, row_pair, 3 + 3 * count, (lat, partner))
    row_down_first = remote(row_sums, row_upper, 4 + 3 * count, (lat, x_down))
    row_down_later = remote(row_relay, row_upper, 4 + 3 * count, (lat, x_down))
    row_up_first = remote(row_sums, row_lower, 5 + 3 * count, (lat, x_up))
    row_up_later = remote(row_lower, row_lower, 5 + 3 * count, (lat, x_up))
    shares = [remote(column.at[*p], shared.at[*c], 3 + 2 * count + i, (lat, partner)) for i, (p, c) in enumerate(zip(places, pieces))]

    def enter():
        pl.semaphore_wait(barrier, 3 + one(has_minus) + one(has_plus))
        to_pair.start()

        @pl.when(has_minus)
        def _():
            to_minus.start()

        @pl.when(has_plus)
        def _():
            to_plus.start()

    def first_step():
        to_pair.wait()
        sums[...] = column[pl.ds(mine, part), :] + pair[...]
        for i in range(count):
            @pl.when(x >= 2)
            def _():
                down_first[i].start()

            @pl.when(x == 3)
            def _():
                up_first[i].start()

        @pl.when(x == chips - 1)
        def _():
            from_upper[...] = jnp.zeros_like(from_upper)
            row_upper[...] = jnp.zeros_like(row_upper)

        @pl.when(x >= chips - 2)
        def _():
            from_lower[...] = jnp.zeros_like(from_lower)
            row_lower[...] = jnp.zeros_like(row_lower)

    def second_step():
        for i, c in enumerate(pieces):
            @pl.when((x == 1) | (x == 2))
            def _():
                down_first[i].wait_recv()

            @pl.when(x == 1)
            def _():
                relay[*c] = sums[*c] + from_upper[*c]
                down_later[i].start()

            @pl.when(x == 0)
            def _():
                up_first[i].wait_recv()
                up_later[i].start()

    def share():
        for i, (p, c) in enumerate(zip(places, pieces)):
            @pl.when(x == 0)
            def _():
                down_first[i].wait_recv()

            @pl.when(x == 1)
            def _():
                up_first[i].wait_recv()

            above = from_upper[*c] + from_lower[*c]
            below[*p] = above + lower * pair[*c]
            column[*p] = above + upper * column[*p]
            shares[i].start()

    def neighbours():
        @pl.when(has_minus)
        def _():
            to_minus.wait_send()
            to_plus.wait_recv()

        @pl.when(jnp.logical_not(has_minus))
        def _():
            from_minus[...] = jnp.zeros_like(from_minus)

        @pl.when(has_plus)
        def _():
            to_plus.wait_send()
            to_minus.wait_recv()

        @pl.when(jnp.logical_not(has_plus))
        def _():
            from_plus[...] = jnp.zeros_like(from_plus)

        for at, source in enumerate((from_minus, from_plus)):
            outside = source[0:1, :]
            for level in range(1, levels):
                outside = outside + source[level : level + 1, :]
            row_column[at] = outside
        row_pairing.start()

    def row_first():
        row_pairing.wait()
        row_sums[...] = row_column[...] + row_pair[...]

        @pl.when(x >= 2)
        def _():
            row_down_first.start()

        @pl.when(x == 3)
        def _():
            row_up_first.start()

    def row_second():
        @pl.when((x == 1) | (x == 2))
        def _():
            row_down_first.wait_recv()

        @pl.when(x == 1)
        def _():
            row_relay[...] = row_sums[...] + row_upper[...]
            row_down_later.start()

        @pl.when(x == 0)
        def _():
            row_up_first.wait_recv()
            row_up_later.start()

    row_index = (lat * rows + row32).astype(jnp.float32)
    lat_total = lat_count * rows
    center = (row_index + 0.5) * (math.pi / lat_total) - 0.5 * math.pi
    trig[0] = (time_step * coriolis) * jnp.sin(center)
    trig[1] = (0.5 * time_step) * jnp.cos(center)
    trig[2] = (0.25 * time_step) * jnp.sin(row_index * (math.pi / lat_total))
    top, bottom = row32 == 0, row32 == rows - 1

    def down(x, halo):
        return jnp.where(top, halo, pltpu.roll(x, 1, 0))

    def up(x, halo):
        return jnp.where(bottom, halo, pltpu.roll(x, rows - 1, 0))

    def east(x):
        return pltpu.roll(x, WIDE - 1, 1)

    def west(x):
        return pltpu.roll(x, 1, 1)

    def inside(first, last):
        sin_center, cos_center, edge = trig[0], trig[1], trig[2]

        def one_segment(s, carry):
            total = jnp.zeros((rows, WIDE), jnp.float32)
            for level in reversed(range(levels)):
                u, v, h = field[level, s], field[levels + level, s], field[2 * levels + level, s]
                geo = total + 0.5 * h
                total = total + h
                zonal = (0.25 * time_step) * (h + east(h)) * (u + east(u))
                merid = jnp.where(top, 0.0, (h + pltpu.roll(h, 1, 0)) * (v + pltpu.roll(v, 1, 0)) * edge)
                result[2 * levels + level, s] = h - ((zonal - west(zonal)) + (up(merid, 0.0) - merid))
                result[level, s] = u - (0.5 * time_step) * (east(geo) - west(geo)) + sin_center * v
                result[levels + level, s] = v - cos_center * (up(geo, 0.0) - down(geo, 0.0)) - sin_center * u
            return carry

        lax.fori_loop(first, last, one_segment, 0)

    def write_rows(target, source, parts):
        for p in parts:
            here = pl.ds(p * 8, 8)
            tiles = joined([source(s, here) for s in range(RADIX)])
            for t in range(RADIX - 1):
                target[here, t * WIDE : (t + 1) * WIDE] = tiles[t]
            target[here, (RADIX - 1) * WIDE : lon] = tiles[RADIX - 1][:, : lon - (RADIX - 1) * WIDE]

    def write_units(first, parts):
        def unit(level, carry):
            index = first + level
            write_rows(out.at[index], lambda s, here: result[index, s, here, :], parts)
            return carry

        lax.fori_loop(0, levels, unit, 0)

    stores = [
        pltpu.make_async_copy(out.at[pl.ds(0, levels)], part_winds.at[0], store_sem.at[0]),
        pltpu.make_async_copy(out.at[pl.ds(levels, levels)], part_winds.at[1], store_sem.at[1]),
        pltpu.make_async_copy(out.at[pl.ds(2 * levels, levels)], new_thick, store_sem.at[2]),
        pltpu.make_async_copy(out_delta, delta, store_sem.at[3]),
    ]

    def write_first():
        write_units(0, range(4))
        stores[0].start()

    def write_middle():
        write_units(levels, (1, 2))
        write_units(2 * levels, (1, 2))

    def rest_of_loads():
        for load in loads[3:]:
            load.wait()

    def run(*stages):
        for stage in stages:
            stage()

    half_way = RADIX // 2
    some = lambda stage, *args: functools.partial(stage, *args)

    @pl.when(early)
    def _():
        run(rest_of_loads, limits, forward_thick, forward_winds, some(products, range(6)), inverse)
        run(some(inside, 0, RADIX), write_first, write_middle)
        run(enter, first_step, neighbours, row_first, second_step, row_second, share)

    @pl.when(after_early)
    def _():
        run(enter, limits, forward_thick, first_step, rest_of_loads, forward_winds, some(products, range(3)))
        run(second_step, some(products, range(3, 6)), share, inverse, some(inside, 0, half_way), neighbours)
        run(some(inside, half_way, RADIX), row_first, write_first, row_second, write_middle)

    @pl.when(jnp.logical_not(early | after_early))
    def _():
        run(enter, limits, forward_thick, first_step, rest_of_loads, forward_winds, neighbours)
        run(some(products, range(3)), row_first, second_step, some(products, range(3, 6)), row_second)
        run(inverse, share, some(inside, 0, RADIX), write_first, write_middle)

    for i, c in enumerate(pieces):
        shares[i].wait()
        below[*others[i]] = shared[*c]

    @pl.when(x == 0)
    def _():
        row_down_first.wait_recv()

    @pl.when(x == 1)
    def _():
        row_up_first.wait_recv()

    sin_center, cos_center, edge = trig[0], trig[1], trig[2]
    last_index = (lat * rows + rows + jnp.zeros((8, WIDE), jnp.int32)).astype(jnp.float32)
    last_edge = (0.25 * time_step) * jnp.sin(last_index * (math.pi / lat_total))
    minus_cut = from_minus[:, full - WIDE :][:, WIDE - 1 :]
    plus_cut = from_plus[:, full - WIDE :][:, WIDE - 1 :]
    cut2[pl.ds(rows, 8), :] = jnp.broadcast_to(minus_cut, (8, WIDE))
    cut2[pl.ds(rows + 8, 8), :] = jnp.broadcast_to(plus_cut, (8, WIDE))
    row16 = lax.broadcasted_iota(jnp.int32, (16, WIDE), 0)
    cut2[pl.ds(rows + 16, 16), :] = jnp.where(row16 == 0, minus_cut[0:1], plus_cut[0:1])
    for half in range(rows // 16):
        forward_rows(tiles_of(lambda c: below[pl.ds(half * 16, 16), c]), y2_high, y2_low, half * 16)
    forward_rows(tiles_of(lambda c: jnp.concatenate([from_minus[:, c], from_plus[:, c]], axis=0)), y2_high, y2_low, rows)
    for at in range(2):
        row_column[at] = row_upper[at] + row_lower[at] + lower * row_pair[at]

    def edge_tile(c):
        return jnp.where(row16 == 0, row_column[0, :, c], jnp.where(row16 == 1, row_column[1, :, c], 0.0))

    forward_rows(tiles_of(edge_tile), y2_high, y2_low, rows + 16)
    for k in range(6):
        filter_class(k, y2_high, y2_low, z2, cut2, wave, f_high, f_low)
    for group in range((rows + 32) // 16):
        here = pl.ds(group * 16, 16)
        parts = [(z2[k, here, :WIDE], z2[k, here, WIDE:]) for k in range(6)]
        for s, value in enumerate(inverse12(parts)):
            outer[s, here, :] = value

    eight = lax.broadcasted_iota(jnp.int32, (8, WIDE), 0)
    at_top, at_bottom = eight == 0, eight == 7
    head, tail = pl.ds(0, 8), pl.ds(rows - 8, 8)

    def patch(s, carry):
        total = outer[s, pl.ds(0, rows), :]
        sides = outer[s, pl.ds(rows, 32), :]
        grad[0, s] = -(0.5 * time_step) * (east(total) - west(total))
        grad[1, s] = -cos_center * (up(total, sides[17:18]) - down(total, sides[16:17]))
        minus_total = plus_total = jnp.zeros((1, WIDE), jnp.float32)
        for level in reversed(range(levels)):
            hm, vm = sides[level : level + 1], sides[levels + level : levels + level + 1]
            hp, vp = sides[8 + level : 9 + level], sides[8 + levels + level : 9 + levels + level]
            vi, hi = levels + level, 2 * levels + level
            geo_minus, geo_plus = minus_total + 0.5 * hm, plus_total + 0.5 * hp
            minus_total, plus_total = minus_total + hm, plus_total + hp
            result[vi, s, head, :] += jnp.where(at_top, cos_center[:8] * geo_minus, 0.0)
            result[vi, s, tail, :] -= jnp.where(at_bottom, cos_center[rows - 8 :] * geo_plus, 0.0)
            first = (field[hi, s, head, :] + hm) * (field[vi, s, head, :] + vm) * edge[:8]
            final = (field[hi, s, tail, :] + hp) * (field[vi, s, tail, :] + vp) * last_edge
            result[hi, s, head, :] += jnp.where(at_top, first, 0.0)
            result[hi, s, tail, :] -= jnp.where(at_bottom, final, 0.0)
        return carry

    lax.fori_loop(0, RADIX, patch, 0)
    write_units(levels, (0, 3))
    stores[1].start()
    write_units(2 * levels, (0, 3))
    stores[2].start()
    for which in range(2):
        write_rows(out_delta.at[which], lambda s, here: grad[which, s, here, :], range(4))
    stores[3].start()

    @pl.when(x >= 1)
    def _():
        for link in down_first:
            link.wait_send()
        row_down_first.wait_send()

    @pl.when((x == 0) | (x == 3))
    def _():
        for link in up_first:
            link.wait_send()
        row_up_first.wait_send()

    for store in stores:
        store.wait()


def step(shape, winds, thick, cutoff):
    levels, rows, lon = thick.shape
    high, low, wave = filter_tables(lon)
    full = RADIX * WIDE
    part = rows // 2
    units = 3 * levels * rows
    more = rows + 32
    f32 = lambda *dims: pltpu.VMEM(dims, jnp.float32)
    bf16 = lambda *dims: pltpu.VMEM(dims, jnp.bfloat16)
    hbm = pl.BlockSpec(memory_space=pltpu.HBM)
    free = pl.BlockSpec(memory_space=pl.ANY)
    return pl.pallas_call(
        functools.partial(step_kernel, shape["lat"], shape["lev"], 1),
        out_shape=(
            jax.ShapeDtypeStruct(winds.shape, jnp.float32),
            jax.ShapeDtypeStruct(thick.shape, jnp.float32),
            jax.ShapeDtypeStruct((2, rows, lon), jnp.float32),
        ),
        in_specs=[hbm] * 6,
        out_specs=(free, free, free),
        scratch_shapes=[
            pltpu.SMEM((rows,), jnp.int32),
            f32(1, RADIX * WIDE),
            f32(levels, rows, lon),
            f32(2, levels, rows, lon),
            bf16(*high.shape),
            bf16(*low.shape),
            bf16(6, units, 2 * WIDE),
            bf16(6, units, 2 * WIDE),
            f32(6, units, 2 * WIDE),
            f32(3 * levels, RADIX, rows, WIDE),
            f32(3 * levels, RADIX, rows, WIDE),
            f32(units, WIDE),
            bf16(6, more, 2 * WIDE),
            bf16(6, more, 2 * WIDE),
            f32(6, more, 2 * WIDE),
            f32(RADIX, more, WIDE),
            f32(2, RADIX, rows, WIDE),
            f32(more, WIDE),
            f32(3 * levels, rows, lon),
            f32(2, rows, lon),
            f32(3, rows, WIDE),
            f32(8, full),
            f32(8, full),
            f32(8, full),
            f32(8, full),
            f32(rows, full),
            f32(rows, full),
            f32(part, full),
            f32(part, full),
            f32(part, full),
            f32(part, full),
            f32(part, full),
            f32(part, full),
            f32(2, 1, full),
            f32(2, 1, full),
            f32(2, 1, full),
            f32(2, 1, full),
            f32(2, 1, full),
            f32(2, 1, full),
            pltpu.SemaphoreType.DMA((7,)),
            pltpu.SemaphoreType.DMA((4,)),
            pltpu.SemaphoreType.DMA((18,)),
            pltpu.SemaphoreType.DMA((18,)),
        ],
        compiler_params=pltpu.CompilerParams(collective_id=0, has_side_effects=True, vmem_limit_bytes=24 << 20),
    )(*[pltpu.with_memory_space_constraint(v, pltpu.HBM) for v in (thick, winds, cutoff, jnp.asarray(wave), jnp.asarray(high), jnp.asarray(low))])


def last_kernel(part_winds, part_thick, delta, new_winds, new_thick, w, sem):
    levels = part_thick.shape[0]
    stores = [pltpu.make_async_copy(part_thick, new_thick, sem.at[2 * levels])]
    stores[0].start()
    for f in range(2):
        for level in range(levels):
            w[f, level] = part_winds[f, level] + delta[f]
            store = pltpu.make_async_copy(w.at[f, level], new_winds.at[f, level], sem.at[f * levels + level])
            store.start()
            stores.append(store)
    for store in stores:
        store.wait()


def last(part_winds, part_thick, delta):
    hbm = pl.BlockSpec(memory_space=pltpu.HBM)
    vmem = pl.BlockSpec(memory_space=pltpu.VMEM)
    return pl.pallas_call(
        last_kernel,
        out_shape=(
            jax.ShapeDtypeStruct(part_winds.shape, jnp.float32),
            jax.ShapeDtypeStruct(part_thick.shape, jnp.float32),
        ),
        in_specs=[vmem, vmem, vmem],
        out_specs=(hbm, hbm),
        scratch_shapes=[
            pltpu.VMEM(part_winds.shape, jnp.float32),
            pltpu.SemaphoreType.DMA((2 * part_thick.shape[0] + 1,)),
        ],
        compiler_params=pltpu.CompilerParams(vmem_limit_bytes=8 << 20),
    )(part_winds, part_thick, delta)


def solution(mesh):
    shape = dict(mesh.shape)

    def per_device(winds, thickness, cutoff):
        return last(*step(shape, winds, thickness, cutoff))

    return jax.shard_map(
        per_device,
        mesh=mesh,
        in_specs=(P(None, "lev", "lat", None), P("lev", "lat", None), P("lat")),
        out_specs=(P(None, "lev", "lat", None), P("lev", "lat", None)),
        check_vma=False,
    )
```

```python
import functools
import math

import jax
import jax.numpy as jnp
import numpy as np
from jax import lax
from jax.experimental import pallas as pl
from jax.experimental.pallas import tpu as pltpu
from jax.sharding import PartitionSpec as P

MESH = pl.DeviceIdType.MESH
time_step = 0.2
coriolis = 1.0
RADIX = 12
HALO = 4
WIDE = 128
HALF3 = 0.5 * math.sqrt(3.0)


def filter_tables(lon):
    seg = lon // RADIX
    points = np.arange(WIDE) - HALO
    scale = math.sqrt(2.0 / lon)
    table = np.zeros((6, 2 * WIDE, 2 * WIDE))
    wave = np.full((6, 2 * WIDE), float(lon))
    turn = 2.0 * math.pi / lon
    j = np.arange(seg)
    for k in range(1, 6):
        m = RADIX * j + k
        angle = turn * ((points[:, None] * m[None, :]) % lon)
        table[k, :WIDE, :seg] = np.cos(angle) * scale
        table[k, :WIDE, WIDE : WIDE + seg] = np.sin(angle) * scale
        table[k, WIDE:, :seg] = -np.sin(angle) * scale
        table[k, WIDE:, WIDE : WIDE + seg] = np.cos(angle) * scale
        wave[k, :seg] = wave[k, WIDE : WIDE + seg] = np.minimum(m, lon - m)
    half = seg // 2
    m = RADIX * np.arange(half + 1)
    weight = np.where((m == 0) | (m == lon // 2), scale / math.sqrt(2.0), scale)
    angle = turn * ((points[:, None] * m[None, :]) % lon)
    table[0, :WIDE, : half + 1] = np.cos(angle) * weight
    table[0, :WIDE, half + 1 : seg] = np.sin(angle[:, 1:half]) * scale
    wave[0, : half + 1] = m
    wave[0, half + 1 : seg] = m[1:half]
    m = RADIX * np.arange(half) + RADIX // 2
    angle = turn * ((points[:, None] * m[None, :]) % lon)
    table[0, WIDE:, WIDE : WIDE + half] = np.cos(angle) * scale
    table[0, WIDE:, WIDE + half : WIDE + seg] = np.sin(angle) * scale
    wave[0, WIDE : WIDE + half] = wave[0, WIDE + half : WIDE + seg] = m
    table = table.astype(np.float32)
    high = table.astype(jnp.bfloat16)
    low = (table - high.astype(np.float32)).astype(jnp.bfloat16)
    return high, low, wave.astype(np.float32).reshape(1, 12 * WIDE)


def split(x):
    high = x.astype(jnp.bfloat16)
    return high, (x - high.astype(jnp.float32)).astype(jnp.bfloat16)


def forward12(x):
    e = [x[s] + x[s + 6] for s in range(6)]
    o = [x[s] - x[s + 6] for s in range(6)]
    ee = [e[s] + e[s + 3] for s in range(3)]
    eo = [e[s] - e[s + 3] for s in range(3)]
    sum12 = ee[1] + ee[2]
    d15, s15, d24, s24 = o[1] - o[5], o[1] + o[5], o[2] - o[4], o[2] + o[4]
    a, b = o[0] + 0.5 * d24, HALF3 * d15
    c, d = 0.5 * s15 + o[3], HALF3 * s24
    return [
        (ee[0] + sum12, eo[0] - eo[1] + eo[2]),
        (a + b, c + d),
        (eo[0] + 0.5 * (eo[1] - eo[2]), HALF3 * (eo[1] + eo[2])),
        (o[0] - d24, s15 - o[3]),
        (ee[0] - 0.5 * sum12, HALF3 * (ee[1] - ee[2])),
        (a - b, c - d),
    ]


def inverse12(z):
    (z0, z6), (r1, n1), (r2, n2), (r3, n3), (r4, n4), (r5, n5) = z
    a, b = HALF3 * (r1 - r5), 0.5 * (n1 + n5) + n3
    c, d = 0.5 * (r1 + r5) - r3, HALF3 * (n1 - n5)
    odd = [r1 + r3 + r5, b + a, c + d, n1 - n3 + n5, d - c, b - a]
    low, h4 = z0 - 0.5 * r4, HALF3 * n4
    ee = [z0 + r4, low + h4, low - h4]
    h2, hr = HALF3 * n2, 0.5 * r2
    eo = [z6 + r2, hr + h2 - z6, z6 - hr + h2]
    even = [ee[s] + eo[s] for s in range(3)] + [ee[s] - eo[s] for s in range(3)]
    return [even[s] + odd[s] for s in range(6)] + [even[s] - odd[s] for s in range(6)]


def lanes_of(shape):
    return lax.broadcasted_iota(jnp.int32, shape, len(shape) - 1)


def segments(tiles):
    lane = lanes_of(tiles[0].shape)
    out = [pltpu.roll(tiles[0], HALO, 1)]
    for s in range(1, RADIX):
        shift = 8 * s + HALO
        out.append(pltpu.roll(jnp.where(lane >= WIDE - shift, tiles[s - 1], tiles[s]), shift, 1))
    return out


def joined(segs):
    lane = lanes_of(segs[0].shape)
    out = []
    for t in range(RADIX):
        tile = pltpu.roll(segs[t], WIDE - (8 * t + HALO), 1)
        if t + 1 < RADIX:
            later = pltpu.roll(segs[t + 1], 116 - 8 * t, 1)
            tile = jnp.where(lane < 120 - 8 * t, tile, later)
        out.append(tile)
    return out


def forward_rows(tiles, y_high, y_low, row):
    lane = lanes_of((16, WIDE))
    inside = (lane >= HALO) & (lane < WIDE - HALO)
    classes = forward12(segments(tiles))
    for k, parts in enumerate(classes):
        for at, part in enumerate(parts):
            high, low = split(jnp.where(inside, part, 0.0))
            y_high[k, pl.ds(row, 16), at * WIDE : (at + 1) * WIDE] = high
            y_low[k, pl.ds(row, 16), at * WIDE : (at + 1) * WIDE] = low


def tiles_of(load):
    return [load(pl.ds(t * WIDE, WIDE)) for t in range(RADIX)]


def narrow_tiles(load, lon):
    last = lon - (RADIX - 1) * WIDE
    tiles = [load(pl.ds(t * WIDE, WIDE)) for t in range(RADIX - 1)]
    end = load(pl.ds((RADIX - 1) * WIDE, last))
    return tiles + [jnp.concatenate([end, jnp.zeros((end.shape[0], WIDE - last), jnp.float32)], axis=1)]


def filter_class(k, y_high, y_low, z, cut, wave, f_high, f_low):
    high, low = f_high[k], f_low[k]
    yh, yl = y_high[k], y_low[k]
    coeffs = jnp.dot(
        jnp.concatenate([yh, yl, yh], axis=1),
        jnp.concatenate([high, high, low], axis=0),
        preferred_element_type=jnp.float32,
    )
    limit = cut[...]
    wanted = wave[:, pl.ds(k * 2 * WIDE, 2 * WIDE)]
    keep = jnp.concatenate([limit >= wanted[:, :WIDE], limit >= wanted[:, WIDE:]], axis=1)
    xh, xl = split(jnp.where(keep, coeffs, 0.0))
    z[k] = lax.dot_general(
        jnp.concatenate([xh, xl, xh], axis=1),
        jnp.concatenate([high, high, low], axis=1),
        (((1,), (1,)), ((), ())),
        preferred_element_type=jnp.float32,
    )


def step_kernel(
    lat_count,
    lev_count,
    thick,
    winds,
    cutoff_in,
    wave_in,
    table_high,
    table_low,
    part_winds,
    new_thick,
    delta,
    cutoff,
    wave,
    h_in,
    w_in,
    f_high,
    f_low,
    y_high,
    y_low,
    z,
    field,
    result,
    cut,
    y2_high,
    y2_low,
    z2,
    outer,
    grad,
    cut2,
    out,
    out_delta,
    trig,
    send_minus,
    send_plus,
    from_minus,
    from_plus,
    column,
    below,
    pair,
    sums,
    from_upper,
    from_lower,
    relay,
    shared,
    row_column,
    row_pair,
    row_sums,
    row_slots,
    send_row,
    load_sem,
    store_sem,
    send_sem,
    recv_sem,
):
    levels, rows, lon = thick.shape
    full = RADIX * WIDE
    part = rows // 2
    fields = 3 * levels
    lat, lev = lax.axis_index("lat"), lax.axis_index("lev")
    x, core = lev // 2, lev % 2
    chips = lev_count // 2
    partner = x * 2 + (1 - core)
    chip_at = lambda other: ((other + chips) % chips) * 2 + core
    x_up, x_down = ((x + 1) % chips) * 2 + core, ((x + chips - 1) % chips) * 2 + core
    has_minus, has_plus = lat > 0, lat < lat_count - 1
    lat_minus, lat_plus = jnp.maximum(lat - 1, 0), jnp.minimum(lat + 1, lat_count - 1)
    early = (lat % 8 == 0) & (lat > 0)
    after_early = lat % 8 == 1

    barrier = pltpu.get_barrier_semaphore()
    for device in ((lat, partner), (lat, x_up), (lat, x_down), (lat, chip_at(x + 2))):
        pl.semaphore_signal(barrier, inc=1, device_id=device, device_id_type=MESH)

    @pl.when(has_minus)
    def _():
        pl.semaphore_signal(barrier, inc=1, device_id=(lat_minus, lev), device_id_type=MESH)

    @pl.when(has_plus)
    def _():
        pl.semaphore_signal(barrier, inc=1, device_id=(lat_plus, lev), device_id_type=MESH)

    loads = [
        pltpu.make_async_copy(source, target, load_sem.at[i])
        for i, (source, target) in enumerate(
            (
                (thick, h_in),
                (winds.at[1], w_in.at[1]),
                (cutoff_in, cutoff),
                (wave_in, wave),
                (table_high, f_high),
                (table_low, f_low),
                (winds.at[0], w_in.at[0]),
            )
        )
    ]
    for load in loads[:3]:
        load.start()

    def remote(source, target, at, device):
        return pltpu.make_async_remote_copy(
            src_ref=source,
            dst_ref=target,
            send_sem=send_sem.at[at],
            recv_sem=recv_sem.at[at],
            device_id=device,
            device_id_type=MESH,
        )

    row32 = lax.broadcasted_iota(jnp.int32, (rows, WIDE), 0)

    def limits():
        limit = jnp.zeros((rows, WIDE), jnp.float32)
        for r in range(rows):
            limit = jnp.where(row32 == r, cutoff[r].astype(jnp.float32), limit)
        for unit in range(fields):
            cut[pl.ds(unit * rows, rows), :] = limit
        cut2[pl.ds(0, rows), :] = limit

    def forward_thick():
        def unit(level, carry):
            for half in range(rows // 16):
                here = pl.ds(half * 16, 16)
                tiles = narrow_tiles(lambda c: h_in[level, here, c], lon)
                forward_rows(tiles, y_high, y_low, (2 * levels + level) * rows + half * 16)
            return carry

        lax.fori_loop(0, levels, unit, 0)

    def forward_winds():
        def unit(index, carry):
            for half in range(rows // 16):
                here = pl.ds(half * 16, 16)
                tiles = narrow_tiles(lambda c: w_in[index // levels, index % levels, here, c], lon)
                forward_rows(tiles, y_high, y_low, index * rows + half * 16)
            return carry

        lax.fori_loop(0, 2 * levels, unit, 0)

    def products(classes):
        for k in classes:
            filter_class(k, y_high, y_low, z, cut, wave, f_high, f_low)

    def inverse():
        def unit(index, carry):
            for half in range(rows // 16):
                here = pl.ds(index * rows + half * 16, 16)
                parts = [(z[k, here, :WIDE], z[k, here, WIDE:]) for k in range(6)]
                for s, value in enumerate(inverse12(parts)):
                    field[index, s, pl.ds(half * 16, 16), :] = value
            return carry

        lax.fori_loop(0, fields, unit, 0)

    loads[0].wait()
    for load in loads[3:]:
        load.start()
    total = h_in[0]
    for level in range(1, levels):
        total = total + h_in[level]
    column[:, pl.ds(full - WIDE, WIDE)] = jnp.zeros((rows, WIDE), jnp.float32)
    column[:, pl.ds(0, lon)] = total
    send_row[0] = column[0:1, :]
    send_row[1] = column[rows - 1 : rows, :]
    loads[1].wait()
    loads[2].wait()
    row8 = lax.broadcasted_iota(jnp.int32, (8, lon), 0)
    for pack, row in ((send_minus, 0), (send_plus, rows - 1)):
        value = jnp.zeros((8, lon), jnp.float32)
        for level in range(levels):
            value = jnp.where(row8 == level, h_in[level, row : row + 1, :], value)
            value = jnp.where(row8 == levels + level, w_in[1, level, row : row + 1, :], value)
        pack[:, pl.ds(full - WIDE, WIDE)] = jnp.broadcast_to(cutoff[row].astype(jnp.float32), (8, WIDE))
        pack[:, pl.ds(0, lon)] = value

    one = lambda flag: jnp.where(flag, 1, 0)
    mine, theirs = pl.multiple_of(core * part, part), pl.multiple_of((1 - core) * part, part)
    upper = jnp.where(core == 0, 0.0, 1.0)
    lower = 1.0 - upper
    chunks = [(8 * r, full // 2 * c) for r in range(part // 8) for c in range(2)]
    pieces = [(pl.ds(r, 8), pl.ds(c, full // 2)) for r, c in chunks]
    places = [(pl.ds(pl.multiple_of(mine + r, 8), 8), pl.ds(c, full // 2)) for r, c in chunks]
    others = [(pl.ds(pl.multiple_of(theirs + r, 8), 8), pl.ds(c, full // 2)) for r, c in chunks]
    count = len(pieces)
    to_pair = remote(column.at[pl.ds(theirs, part), :], pair, 0, (lat, partner))
    to_minus = remote(send_minus, from_plus, 1, (lat_minus, lev))
    to_plus = remote(send_plus, from_minus, 2, (lat_plus, lev))
    down_first = [remote(sums.at[*c], from_upper.at[*c], 3 + i, (lat, x_down)) for i, c in enumerate(pieces)]
    down_later = [remote(relay.at[*c], from_upper.at[*c], 3 + i, (lat, x_down)) for i, c in enumerate(pieces)]
    up_first = [remote(sums.at[*c], from_lower.at[*c], 3 + count + i, (lat, x_up)) for i, c in enumerate(pieces)]
    up_later = [remote(from_lower.at[*c], from_lower.at[*c], 3 + count + i, (lat, x_up)) for i, c in enumerate(pieces)]
    row_pairing = remote(row_column, row_pair, 3 + 3 * count, (lat, partner))
    row_minus = remote(send_row.at[0], row_column.at[1], 4 + 3 * count, (lat_minus, lev))
    row_plus = remote(send_row.at[1], row_column.at[0], 5 + 3 * count, (lat_plus, lev))
    row_links = [remote(row_sums, row_slots.at[j - 1], 5 + 3 * count + j, (lat, chip_at(x - j))) for j in range(1, 4)]
    shares = [remote(column.at[*p], shared.at[*c], 3 + 2 * count + i, (lat, partner)) for i, (p, c) in enumerate(zip(places, pieces))]

    def enter():
        pl.semaphore_wait(barrier, 4 + one(has_minus) + one(has_plus))
        @pl.when(has_minus)
        def _():
            row_minus.start()

        @pl.when(has_plus)
        def _():
            row_plus.start()

        to_pair.start()

        @pl.when(has_minus)
        def _():
            to_minus.start()

        @pl.when(has_plus)
        def _():
            to_plus.start()

    def first_step():
        to_pair.wait()
        sums[...] = column[pl.ds(mine, part), :] + pair[...]
        for i in range(count):
            @pl.when(x >= 2)
            def _():
                down_first[i].start()

            @pl.when(x == 3)
            def _():
                up_first[i].start()

        @pl.when(x == chips - 1)
        def _():
            from_upper[...] = jnp.zeros_like(from_upper)

        @pl.when(x >= chips - 2)
        def _():
            from_lower[...] = jnp.zeros_like(from_lower)

    def second_step(which):
        for i in which:
            c = pieces[i]
            @pl.when((x == 1) | (x == 2))
            def _():
                down_first[i].wait_recv()

            @pl.when(x == 1)
            def _():
                relay[*c] = sums[*c] + from_upper[*c]
                down_later[i].start()

            @pl.when(x == 0)
            def _():
                up_first[i].wait_recv()
                up_later[i].start()

    def share():
        for i, (p, c) in enumerate(zip(places, pieces)):
            @pl.when(x == 0)
            def _():
                down_first[i].wait_recv()

            @pl.when(x == 1)
            def _():
                up_first[i].wait_recv()

            above = from_upper[*c] + from_lower[*c]
            below[*p] = above + lower * pair[*c]
            column[*p] = above + upper * column[*p]
            shares[i].start()

    def rows_in():
        @pl.when(has_minus)
        def _():
            row_minus.wait_send()
            row_plus.wait_recv()

        @pl.when(jnp.logical_not(has_minus))
        def _():
            row_column[0] = jnp.zeros((1, full), jnp.float32)

        @pl.when(has_plus)
        def _():
            row_plus.wait_send()
            row_minus.wait_recv()

        @pl.when(jnp.logical_not(has_plus))
        def _():
            row_column[1] = jnp.zeros((1, full), jnp.float32)

        row_pairing.start()

    def neighbours():
        @pl.when(has_minus)
        def _():
            to_minus.wait_send()
            to_plus.wait_recv()

        @pl.when(jnp.logical_not(has_minus))
        def _():
            from_minus[...] = jnp.zeros_like(from_minus)

        @pl.when(has_plus)
        def _():
            to_plus.wait_send()
            to_minus.wait_recv()

        @pl.when(jnp.logical_not(has_plus))
        def _():
            from_plus[...] = jnp.zeros_like(from_plus)


    def row_first():
        row_pairing.wait()
        row_sums[...] = row_column[...] + row_pair[...]
        for j, link in enumerate(row_links, 1):
            @pl.when(x >= j)
            def _():
                link.start()

            @pl.when(x + j >= chips)
            def _():
                row_slots[j - 1] = jnp.zeros((2, 1, full), jnp.float32)

    row_index = (lat * rows + row32).astype(jnp.float32)
    lat_total = lat_count * rows
    center = (row_index + 0.5) * (math.pi / lat_total) - 0.5 * math.pi
    trig[0] = (time_step * coriolis) * jnp.sin(center)
    trig[1] = (0.5 * time_step) * jnp.cos(center)
    trig[2] = (0.25 * time_step) * jnp.sin(row_index * (math.pi / lat_total))
    top, bottom = row32 == 0, row32 == rows - 1

    def down(x, halo):
        return jnp.where(top, halo, pltpu.roll(x, 1, 0))

    def up(x, halo):
        return jnp.where(bottom, halo, pltpu.roll(x, rows - 1, 0))

    def east(x):
        return pltpu.roll(x, WIDE - 1, 1)

    def west(x):
        return pltpu.roll(x, 1, 1)

    def inside(first, last):
        sin_center, cos_center, edge = trig[0], trig[1], trig[2]

        def one_segment(s, carry):
            total = jnp.zeros((rows, WIDE), jnp.float32)
            for level in reversed(range(levels)):
                u, v, h = field[level, s], field[levels + level, s], field[2 * levels + level, s]
                geo = total + 0.5 * h
                total = total + h
                zonal = (0.25 * time_step) * (h + east(h)) * (u + east(u))
                merid = jnp.where(top, 0.0, (h + pltpu.roll(h, 1, 0)) * (v + pltpu.roll(v, 1, 0)) * edge)
                result[2 * levels + level, s] = h - ((zonal - west(zonal)) + (up(merid, 0.0) - merid))
                result[level, s] = u - (0.5 * time_step) * (east(geo) - west(geo)) + sin_center * v
                result[levels + level, s] = v - cos_center * (up(geo, 0.0) - down(geo, 0.0)) - sin_center * u
            return carry

        lax.fori_loop(first, last, one_segment, 0)

    def write_rows(target, source, parts):
        for p in parts:
            here = pl.ds(p * 8, 8)
            tiles = joined([source(s, here) for s in range(RADIX)])
            for t in range(RADIX - 1):
                target[here, t * WIDE : (t + 1) * WIDE] = tiles[t]
            target[here, (RADIX - 1) * WIDE : lon] = tiles[RADIX - 1][:, : lon - (RADIX - 1) * WIDE]

    def write_units(first, parts):
        def unit(level, carry):
            index = first + level
            write_rows(out.at[index], lambda s, here: result[index, s, here, :], parts)
            return carry

        lax.fori_loop(0, levels, unit, 0)

    stores = [
        pltpu.make_async_copy(out.at[pl.ds(0, levels)], part_winds.at[0], store_sem.at[0]),
        pltpu.make_async_copy(out.at[pl.ds(levels, levels)], part_winds.at[1], store_sem.at[1]),
        pltpu.make_async_copy(out.at[pl.ds(2 * levels, levels)], new_thick, store_sem.at[2]),
        pltpu.make_async_copy(out_delta, delta, store_sem.at[3]),
    ]

    def write_first():
        write_units(0, range(4))
        stores[0].start()

    def write_middle():
        write_units(levels, (1, 2))
        write_units(2 * levels, (1, 2))

    def rest_of_loads():
        for load in loads[3:]:
            load.wait()

    def run(*stages):
        for stage in stages:
            stage()

    some = lambda stage, *args: functools.partial(stage, *args)

    @pl.when(early)
    def _():
        run(rest_of_loads, limits, forward_thick, forward_winds, some(products, range(6)), inverse)
        run(some(inside, 0, RADIX), write_first, write_middle)
        run(enter, first_step, rows_in, some(second_step, range(count // 2)), row_first)
        run(some(second_step, range(count // 2, count)), share, neighbours)

    @pl.when(after_early)
    def _():
        run(enter, limits, forward_thick, first_step, rest_of_loads, forward_winds, some(products, range(3)))
        run(some(second_step, range(count)), some(products, range(3, 6)), share, inverse, some(inside, 0, RADIX))
        run(write_first, rows_in, write_middle, row_first, neighbours)

    @pl.when(jnp.logical_not(early | after_early))
    def _():
        run(enter, limits, forward_thick, first_step, rest_of_loads, forward_winds, some(products, range(3)))
        run(some(second_step, range(count)), rows_in, some(products, range(3, 6)), row_first, inverse, share)
        run(some(inside, 0, RADIX), write_first, write_middle, neighbours)

    for i, c in enumerate(pieces):
        shares[i].wait()
        below[*others[i]] = shared[*c]

    for j, link in enumerate(row_links, 1):
        @pl.when(x + j < chips)
        def _():
            link.wait_recv()

    sin_center, cos_center, edge = trig[0], trig[1], trig[2]
    last_index = (lat * rows + rows + jnp.zeros((8, WIDE), jnp.int32)).astype(jnp.float32)
    last_edge = (0.25 * time_step) * jnp.sin(last_index * (math.pi / lat_total))
    minus_cut = from_minus[:, full - WIDE :][:, WIDE - 1 :]
    plus_cut = from_plus[:, full - WIDE :][:, WIDE - 1 :]
    cut2[pl.ds(rows, 8), :] = jnp.broadcast_to(minus_cut, (8, WIDE))
    cut2[pl.ds(rows + 8, 8), :] = jnp.broadcast_to(plus_cut, (8, WIDE))
    row16 = lax.broadcasted_iota(jnp.int32, (16, WIDE), 0)
    cut2[pl.ds(rows + 16, 16), :] = jnp.where(row16 == 0, minus_cut[0:1], plus_cut[0:1])
    for half in range(rows // 16):
        forward_rows(tiles_of(lambda c: below[pl.ds(half * 16, 16), c]), y2_high, y2_low, half * 16)
    forward_rows(tiles_of(lambda c: jnp.concatenate([from_minus[:, c], from_plus[:, c]], axis=0)), y2_high, y2_low, rows)
    for at in range(2):
        row_column[at] = row_slots[0, at] + row_slots[1, at] + row_slots[2, at] + lower * row_pair[at]

    def edge_tile(c):
        return jnp.where(row16 == 0, row_column[0, :, c], jnp.where(row16 == 1, row_column[1, :, c], 0.0))

    forward_rows(tiles_of(edge_tile), y2_high, y2_low, rows + 16)
    for k in range(6):
        filter_class(k, y2_high, y2_low, z2, cut2, wave, f_high, f_low)
    for group in range((rows + 32) // 16):
        here = pl.ds(group * 16, 16)
        parts = [(z2[k, here, :WIDE], z2[k, here, WIDE:]) for k in range(6)]
        for s, value in enumerate(inverse12(parts)):
            outer[s, here, :] = value

    eight = lax.broadcasted_iota(jnp.int32, (8, WIDE), 0)
    at_top, at_bottom = eight == 0, eight == 7
    head, tail = pl.ds(0, 8), pl.ds(rows - 8, 8)

    def patch(s, carry):
        total = outer[s, pl.ds(0, rows), :]
        sides = outer[s, pl.ds(rows, 32), :]
        grad[0, s] = -(0.5 * time_step) * (east(total) - west(total))
        grad[1, s] = -cos_center * (up(total, sides[17:18]) - down(total, sides[16:17]))
        minus_total = plus_total = jnp.zeros((1, WIDE), jnp.float32)
        for level in reversed(range(levels)):
            hm, vm = sides[level : level + 1], sides[levels + level : levels + level + 1]
            hp, vp = sides[8 + level : 9 + level], sides[8 + levels + level : 9 + levels + level]
            vi, hi = levels + level, 2 * levels + level
            geo_minus, geo_plus = minus_total + 0.5 * hm, plus_total + 0.5 * hp
            minus_total, plus_total = minus_total + hm, plus_total + hp
            result[vi, s, head, :] += jnp.where(at_top, cos_center[:8] * geo_minus, 0.0)
            result[vi, s, tail, :] -= jnp.where(at_bottom, cos_center[rows - 8 :] * geo_plus, 0.0)
            first = (field[hi, s, head, :] + hm) * (field[vi, s, head, :] + vm) * edge[:8]
            final = (field[hi, s, tail, :] + hp) * (field[vi, s, tail, :] + vp) * last_edge
            result[hi, s, head, :] += jnp.where(at_top, first, 0.0)
            result[hi, s, tail, :] -= jnp.where(at_bottom, final, 0.0)
        return carry

    lax.fori_loop(0, RADIX, patch, 0)
    write_units(levels, (0, 3))
    stores[1].start()
    write_units(2 * levels, (0, 3))
    stores[2].start()
    for which in range(2):
        write_rows(out_delta.at[which], lambda s, here: grad[which, s, here, :], range(4))
    stores[3].start()

    @pl.when(x >= 1)
    def _():
        for link in down_first:
            link.wait_send()

    @pl.when((x == 0) | (x == 3))
    def _():
        for link in up_first:
            link.wait_send()

    for j, link in enumerate(row_links, 1):
        @pl.when(x >= j)
        def _():
            link.wait_send()

    for store in stores:
        store.wait()


def step(shape, winds, thick, cutoff):
    levels, rows, lon = thick.shape
    high, low, wave = filter_tables(lon)
    full = RADIX * WIDE
    part = rows // 2
    units = 3 * levels * rows
    more = rows + 32
    f32 = lambda *dims: pltpu.VMEM(dims, jnp.float32)
    bf16 = lambda *dims: pltpu.VMEM(dims, jnp.bfloat16)
    hbm = pl.BlockSpec(memory_space=pltpu.HBM)
    free = pl.BlockSpec(memory_space=pl.ANY)
    return pl.pallas_call(
        functools.partial(step_kernel, shape["lat"], shape["lev"]),
        out_shape=(
            jax.ShapeDtypeStruct(winds.shape, jnp.float32),
            jax.ShapeDtypeStruct(thick.shape, jnp.float32),
            jax.ShapeDtypeStruct((2, rows, lon), jnp.float32),
        ),
        in_specs=[hbm] * 6,
        out_specs=(free, free, free),
        scratch_shapes=[
            pltpu.SMEM((rows,), jnp.int32),
            f32(1, RADIX * WIDE),
            f32(levels, rows, lon),
            f32(2, levels, rows, lon),
            bf16(*high.shape),
            bf16(*low.shape),
            bf16(6, units, 2 * WIDE),
            bf16(6, units, 2 * WIDE),
            f32(6, units, 2 * WIDE),
            f32(3 * levels, RADIX, rows, WIDE),
            f32(3 * levels, RADIX, rows, WIDE),
            f32(units, WIDE),
            bf16(6, more, 2 * WIDE),
            bf16(6, more, 2 * WIDE),
            f32(6, more, 2 * WIDE),
            f32(RADIX, more, WIDE),
            f32(2, RADIX, rows, WIDE),
            f32(more, WIDE),
            f32(3 * levels, rows, lon),
            f32(2, rows, lon),
            f32(3, rows, WIDE),
            f32(8, full),
            f32(8, full),
            f32(8, full),
            f32(8, full),
            f32(rows, full),
            f32(rows, full),
            f32(part, full),
            f32(part, full),
            f32(part, full),
            f32(part, full),
            f32(part, full),
            f32(part, full),
            f32(2, 1, full),
            f32(2, 1, full),
            f32(2, 1, full),
            f32(3, 2, 1, full),
            f32(2, 1, full),
            pltpu.SemaphoreType.DMA((7,)),
            pltpu.SemaphoreType.DMA((4,)),
            pltpu.SemaphoreType.DMA((21,)),
            pltpu.SemaphoreType.DMA((21,)),
        ],
        compiler_params=pltpu.CompilerParams(collective_id=0, has_side_effects=True, vmem_limit_bytes=24 << 20),
    )(*[pltpu.with_memory_space_constraint(v, pltpu.HBM) for v in (thick, winds, cutoff, jnp.asarray(wave), jnp.asarray(high), jnp.asarray(low))])


def last_kernel(part_winds, part_thick, delta, new_winds, new_thick, w, sem):
    levels = part_thick.shape[0]
    stores = [pltpu.make_async_copy(part_thick, new_thick, sem.at[2 * levels])]
    stores[0].start()
    for f in range(2):
        for level in range(levels):
            w[f, level] = part_winds[f, level] + delta[f]
            store = pltpu.make_async_copy(w.at[f, level], new_winds.at[f, level], sem.at[f * levels + level])
            store.start()
            stores.append(store)
    for store in stores:
        store.wait()


def last(part_winds, part_thick, delta):
    hbm = pl.BlockSpec(memory_space=pltpu.HBM)
    vmem = pl.BlockSpec(memory_space=pltpu.VMEM)
    return pl.pallas_call(
        last_kernel,
        out_shape=(
            jax.ShapeDtypeStruct(part_winds.shape, jnp.float32),
            jax.ShapeDtypeStruct(part_thick.shape, jnp.float32),
        ),
        in_specs=[vmem, vmem, vmem],
        out_specs=(hbm, hbm),
        scratch_shapes=[
            pltpu.VMEM(part_winds.shape, jnp.float32),
            pltpu.SemaphoreType.DMA((2 * part_thick.shape[0] + 1,)),
        ],
        compiler_params=pltpu.CompilerParams(vmem_limit_bytes=8 << 20),
    )(part_winds, part_thick, delta)


def solution(mesh):
    shape = dict(mesh.shape)

    def per_device(winds, thickness, cutoff):
        return last(*step(shape, winds, thickness, cutoff))

    return jax.shard_map(
        per_device,
        mesh=mesh,
        in_specs=(P(None, "lev", "lat", None), P("lev", "lat", None), P("lat")),
        out_specs=(P(None, "lev", "lat", None), P("lev", "lat", None)),
        check_vma=False,
    )
```

```python
import functools
import math

import jax
import jax.numpy as jnp
import numpy as np
from jax import lax
from jax.experimental import pallas as pl
from jax.experimental.pallas import tpu as pltpu
from jax.sharding import PartitionSpec as P

MESH = pl.DeviceIdType.MESH
time_step = 0.2
coriolis = 1.0
RADIX = 12
HALO = 4
WIDE = 128
HALF3 = 0.5 * math.sqrt(3.0)


def filter_tables(lon):
    seg = lon // RADIX
    points = np.arange(WIDE) - HALO
    scale = math.sqrt(2.0 / lon)
    table = np.zeros((6, 2 * WIDE, 2 * WIDE))
    wave = np.full((6, 2 * WIDE), float(lon))
    turn = 2.0 * math.pi / lon
    j = np.arange(seg)
    for k in range(1, 6):
        m = RADIX * j + k
        angle = turn * ((points[:, None] * m[None, :]) % lon)
        table[k, :WIDE, :seg] = np.cos(angle) * scale
        table[k, :WIDE, WIDE : WIDE + seg] = np.sin(angle) * scale
        table[k, WIDE:, :seg] = -np.sin(angle) * scale
        table[k, WIDE:, WIDE : WIDE + seg] = np.cos(angle) * scale
        wave[k, :seg] = wave[k, WIDE : WIDE + seg] = np.minimum(m, lon - m)
    half = seg // 2
    m = RADIX * np.arange(half + 1)
    weight = np.where((m == 0) | (m == lon // 2), scale / math.sqrt(2.0), scale)
    angle = turn * ((points[:, None] * m[None, :]) % lon)
    table[0, :WIDE, : half + 1] = np.cos(angle) * weight
    table[0, :WIDE, half + 1 : seg] = np.sin(angle[:, 1:half]) * scale
    wave[0, : half + 1] = m
    wave[0, half + 1 : seg] = m[1:half]
    m = RADIX * np.arange(half) + RADIX // 2
    angle = turn * ((points[:, None] * m[None, :]) % lon)
    table[0, WIDE:, WIDE : WIDE + half] = np.cos(angle) * scale
    table[0, WIDE:, WIDE + half : WIDE + seg] = np.sin(angle) * scale
    wave[0, WIDE : WIDE + half] = wave[0, WIDE + half : WIDE + seg] = m
    table = table.astype(np.float32)
    high = table.astype(jnp.bfloat16)
    low = (table - high.astype(np.float32)).astype(jnp.bfloat16)
    return high, low, wave.astype(np.float32).reshape(1, 12 * WIDE)


def split(x):
    high = x.astype(jnp.bfloat16)
    return high, (x - high.astype(jnp.float32)).astype(jnp.bfloat16)


def forward12(x):
    e = [x[s] + x[s + 6] for s in range(6)]
    o = [x[s] - x[s + 6] for s in range(6)]
    ee = [e[s] + e[s + 3] for s in range(3)]
    eo = [e[s] - e[s + 3] for s in range(3)]
    sum12 = ee[1] + ee[2]
    d15, s15, d24, s24 = o[1] - o[5], o[1] + o[5], o[2] - o[4], o[2] + o[4]
    a, b = o[0] + 0.5 * d24, HALF3 * d15
    c, d = 0.5 * s15 + o[3], HALF3 * s24
    return [
        (ee[0] + sum12, eo[0] - eo[1] + eo[2]),
        (a + b, c + d),
        (eo[0] + 0.5 * (eo[1] - eo[2]), HALF3 * (eo[1] + eo[2])),
        (o[0] - d24, s15 - o[3]),
        (ee[0] - 0.5 * sum12, HALF3 * (ee[1] - ee[2])),
        (a - b, c - d),
    ]


def inverse12(z):
    (z0, z6), (r1, n1), (r2, n2), (r3, n3), (r4, n4), (r5, n5) = z
    a, b = HALF3 * (r1 - r5), 0.5 * (n1 + n5) + n3
    c, d = 0.5 * (r1 + r5) - r3, HALF3 * (n1 - n5)
    odd = [r1 + r3 + r5, b + a, c + d, n1 - n3 + n5, d - c, b - a]
    low, h4 = z0 - 0.5 * r4, HALF3 * n4
    ee = [z0 + r4, low + h4, low - h4]
    h2, hr = HALF3 * n2, 0.5 * r2
    eo = [z6 + r2, hr + h2 - z6, z6 - hr + h2]
    even = [ee[s] + eo[s] for s in range(3)] + [ee[s] - eo[s] for s in range(3)]
    return [even[s] + odd[s] for s in range(6)] + [even[s] - odd[s] for s in range(6)]


def lanes_of(shape):
    return lax.broadcasted_iota(jnp.int32, shape, len(shape) - 1)


def segments(tiles):
    lane = lanes_of(tiles[0].shape)
    out = [pltpu.roll(tiles[0], HALO, 1)]
    for s in range(1, RADIX):
        shift = 8 * s + HALO
        out.append(pltpu.roll(jnp.where(lane >= WIDE - shift, tiles[s - 1], tiles[s]), shift, 1))
    return out


def joined(segs):
    lane = lanes_of(segs[0].shape)
    out = []
    for t in range(RADIX):
        tile = pltpu.roll(segs[t], WIDE - (8 * t + HALO), 1)
        if t + 1 < RADIX:
            later = pltpu.roll(segs[t + 1], 116 - 8 * t, 1)
            tile = jnp.where(lane < 120 - 8 * t, tile, later)
        out.append(tile)
    return out


def forward_rows(tiles, y_high, y_low, row):
    lane = lanes_of((16, WIDE))
    inside = (lane >= HALO) & (lane < WIDE - HALO)
    classes = forward12(segments(tiles))
    for k, parts in enumerate(classes):
        for at, part in enumerate(parts):
            high, low = split(jnp.where(inside, part, 0.0))
            y_high[k, pl.ds(row, 16), at * WIDE : (at + 1) * WIDE] = high
            y_low[k, pl.ds(row, 16), at * WIDE : (at + 1) * WIDE] = low


def tiles_of(load):
    return [load(pl.ds(t * WIDE, WIDE)) for t in range(RADIX)]


def narrow_tiles(load, lon):
    last = lon - (RADIX - 1) * WIDE
    tiles = [load(pl.ds(t * WIDE, WIDE)) for t in range(RADIX - 1)]
    end = load(pl.ds((RADIX - 1) * WIDE, last))
    return tiles + [jnp.concatenate([end, jnp.zeros((end.shape[0], WIDE - last), jnp.float32)], axis=1)]


def filter_class(k, y_high, y_low, z, cut, wave, f_high, f_low):
    high, low = f_high[k], f_low[k]
    yh, yl = y_high[k], y_low[k]
    coeffs = jnp.dot(
        jnp.concatenate([yh, yl, yh], axis=1),
        jnp.concatenate([high, high, low], axis=0),
        preferred_element_type=jnp.float32,
    )
    limit = cut[...]
    wanted = wave[:, pl.ds(k * 2 * WIDE, 2 * WIDE)]
    keep = jnp.concatenate([limit >= wanted[:, :WIDE], limit >= wanted[:, WIDE:]], axis=1)
    xh, xl = split(jnp.where(keep, coeffs, 0.0))
    z[k] = lax.dot_general(
        jnp.concatenate([xh, xl, xh], axis=1),
        jnp.concatenate([high, high, low], axis=1),
        (((1,), (1,)), ((), ())),
        preferred_element_type=jnp.float32,
    )


def step_kernel(
    lat_count,
    lev_count,
    thick,
    winds,
    cutoff_in,
    wave_in,
    table_high,
    table_low,
    part_winds,
    new_thick,
    delta,
    cutoff,
    wave,
    h_in,
    w_in,
    f_high,
    f_low,
    y_high,
    y_low,
    z,
    field,
    result,
    cut,
    y2_high,
    y2_low,
    z2,
    outer,
    grad,
    cut2,
    out,
    out_delta,
    trig,
    send_minus,
    send_plus,
    from_minus,
    from_plus,
    column,
    below,
    pair,
    sums,
    from_upper,
    from_lower,
    relay,
    shared,
    row_column,
    row_pair,
    row_sums,
    row_slots,
    send_row,
    load_sem,
    store_sem,
    send_sem,
    recv_sem,
):
    levels, rows, lon = thick.shape
    full = RADIX * WIDE
    part = rows // 2
    fields = 3 * levels
    lat, lev = lax.axis_index("lat"), lax.axis_index("lev")
    x, core = lev // 2, lev % 2
    chips = lev_count // 2
    partner = x * 2 + (1 - core)
    chip_at = lambda other: ((other + chips) % chips) * 2 + core
    x_up, x_down = ((x + 1) % chips) * 2 + core, ((x + chips - 1) % chips) * 2 + core
    has_minus, has_plus = lat > 0, lat < lat_count - 1
    lat_minus, lat_plus = jnp.maximum(lat - 1, 0), jnp.minimum(lat + 1, lat_count - 1)
    follows = (lat % 8 == 0) & has_minus
    leads = (lat % 8 == 7) & has_plus

    barrier = pltpu.get_barrier_semaphore()
    for device in ((lat, partner), (lat, x_up), (lat, x_down), (lat, chip_at(x + 2))):
        pl.semaphore_signal(barrier, inc=1, device_id=device, device_id_type=MESH)

    @pl.when(has_minus)
    def _():
        pl.semaphore_signal(barrier, inc=1, device_id=(lat_minus, lev), device_id_type=MESH)

    @pl.when(has_plus & jnp.logical_not(leads))
    def _():
        pl.semaphore_signal(barrier, inc=1, device_id=(lat_plus, lev), device_id_type=MESH)

    loads = [
        pltpu.make_async_copy(source, target, load_sem.at[i])
        for i, (source, target) in enumerate(
            (
                (thick, h_in),
                (winds.at[1], w_in.at[1]),
                (cutoff_in, cutoff),
                (wave_in, wave),
                (table_high, f_high),
                (table_low, f_low),
                (winds.at[0], w_in.at[0]),
            )
        )
    ]
    for load in loads[:3]:
        load.start()

    def remote(source, target, at, device):
        return pltpu.make_async_remote_copy(
            src_ref=source,
            dst_ref=target,
            send_sem=send_sem.at[at],
            recv_sem=recv_sem.at[at],
            device_id=device,
            device_id_type=MESH,
        )

    row32 = lax.broadcasted_iota(jnp.int32, (rows, WIDE), 0)

    def limits():
        limit = jnp.zeros((rows, WIDE), jnp.float32)
        for r in range(rows):
            limit = jnp.where(row32 == r, cutoff[r].astype(jnp.float32), limit)
        for unit in range(fields):
            cut[pl.ds(unit * rows, rows), :] = limit
        cut2[pl.ds(0, rows), :] = limit

    def forward_thick():
        def unit(level, carry):
            for half in range(rows // 16):
                here = pl.ds(half * 16, 16)
                tiles = narrow_tiles(lambda c: h_in[level, here, c], lon)
                forward_rows(tiles, y_high, y_low, (2 * levels + level) * rows + half * 16)
            return carry

        lax.fori_loop(0, levels, unit, 0)

    def forward_winds():
        def unit(index, carry):
            for half in range(rows // 16):
                here = pl.ds(half * 16, 16)
                tiles = narrow_tiles(lambda c: w_in[index // levels, index % levels, here, c], lon)
                forward_rows(tiles, y_high, y_low, index * rows + half * 16)
            return carry

        lax.fori_loop(0, 2 * levels, unit, 0)

    def products(classes):
        for k in classes:
            filter_class(k, y_high, y_low, z, cut, wave, f_high, f_low)

    def inverse():
        def unit(index, carry):
            for half in range(rows // 16):
                here = pl.ds(index * rows + half * 16, 16)
                parts = [(z[k, here, :WIDE], z[k, here, WIDE:]) for k in range(6)]
                for s, value in enumerate(inverse12(parts)):
                    field[index, s, pl.ds(half * 16, 16), :] = value
            return carry

        lax.fori_loop(0, fields, unit, 0)

    loads[0].wait()
    for load in loads[3:]:
        load.start()
    total = h_in[0]
    for level in range(1, levels):
        total = total + h_in[level]
    column[:, pl.ds(full - WIDE, WIDE)] = jnp.zeros((rows, WIDE), jnp.float32)
    column[:, pl.ds(0, lon)] = total
    send_row[0] = column[0:1, :]
    send_row[1] = column[rows - 1 : rows, :]
    loads[1].wait()
    loads[2].wait()
    row8 = lax.broadcasted_iota(jnp.int32, (8, lon), 0)
    for pack, row in ((send_minus, 0), (send_plus, rows - 1)):
        value = jnp.zeros((8, lon), jnp.float32)
        for level in range(levels):
            value = jnp.where(row8 == level, h_in[level, row : row + 1, :], value)
            value = jnp.where(row8 == levels + level, w_in[1, level, row : row + 1, :], value)
        pack[:, pl.ds(full - WIDE, WIDE)] = jnp.broadcast_to(cutoff[row].astype(jnp.float32), (8, WIDE))
        pack[:, pl.ds(0, lon)] = value

    one = lambda flag: jnp.where(flag, 1, 0)
    mine, theirs = pl.multiple_of(core * part, part), pl.multiple_of((1 - core) * part, part)
    upper = jnp.where(core == 0, 0.0, 1.0)
    lower = 1.0 - upper
    chunks = [(8 * r, full // 2 * c) for r in range(part // 8) for c in range(2)]
    pieces = [(pl.ds(r, 8), pl.ds(c, full // 2)) for r, c in chunks]
    places = [(pl.ds(pl.multiple_of(mine + r, 8), 8), pl.ds(c, full // 2)) for r, c in chunks]
    others = [(pl.ds(pl.multiple_of(theirs + r, 8), 8), pl.ds(c, full // 2)) for r, c in chunks]
    count = len(pieces)
    to_pair = remote(column.at[pl.ds(theirs, part), :], pair, 0, (lat, partner))
    to_minus = remote(send_minus, from_plus, 1, (lat_minus, lev))
    to_plus = remote(send_plus, from_minus, 2, (lat_plus, lev))
    down_first = [remote(sums.at[*c], from_upper.at[*c], 3 + i, (lat, x_down)) for i, c in enumerate(pieces)]
    down_later = [remote(relay.at[*c], from_upper.at[*c], 3 + i, (lat, x_down)) for i, c in enumerate(pieces)]
    up_first = [remote(sums.at[*c], from_lower.at[*c], 3 + count + i, (lat, x_up)) for i, c in enumerate(pieces)]
    up_later = [remote(from_lower.at[*c], from_lower.at[*c], 3 + count + i, (lat, x_up)) for i, c in enumerate(pieces)]
    row_pairing = remote(row_column, row_pair, 3 + 3 * count, (lat, partner))
    row_minus = remote(send_row.at[0], row_column.at[1], 4 + 3 * count, (lat_minus, lev))
    row_plus = remote(send_row.at[1], row_column.at[0], 5 + 3 * count, (lat_plus, lev))
    row_links = [remote(row_sums, row_slots.at[j - 1], 5 + 3 * count + j, (lat, chip_at(x - j))) for j in range(1, 4)]
    shares = [remote(column.at[*p], shared.at[*c], 3 + 2 * count + i, (lat, partner)) for i, (p, c) in enumerate(zip(places, pieces))]

    def enter():
        pl.semaphore_wait(barrier, 4 + one(has_minus & jnp.logical_not(follows)) + one(has_plus))
        @pl.when(has_minus & jnp.logical_not(follows))
        def _():
            row_minus.start()

        @pl.when(has_plus)
        def _():
            row_plus.start()

        to_pair.start()

        @pl.when(has_minus & jnp.logical_not(follows))
        def _():
            to_minus.start()

        @pl.when(has_plus)
        def _():
            to_plus.start()

    def first_step():
        to_pair.wait()
        sums[...] = column[pl.ds(mine, part), :] + pair[...]
        for i in range(count):
            @pl.when(x >= 2)
            def _():
                down_first[i].start()

            @pl.when(x == 3)
            def _():
                up_first[i].start()

        @pl.when(x == chips - 1)
        def _():
            from_upper[...] = jnp.zeros_like(from_upper)

        @pl.when(x >= chips - 2)
        def _():
            from_lower[...] = jnp.zeros_like(from_lower)

    def second_step(which):
        for i in which:
            c = pieces[i]
            @pl.when((x == 1) | (x == 2))
            def _():
                down_first[i].wait_recv()

            @pl.when(x == 1)
            def _():
                relay[*c] = sums[*c] + from_upper[*c]
                down_later[i].start()

            @pl.when(x == 0)
            def _():
                up_first[i].wait_recv()
                up_later[i].start()

    def share():
        for i, (p, c) in enumerate(zip(places, pieces)):
            @pl.when(x == 0)
            def _():
                down_first[i].wait_recv()

            @pl.when(x == 1)
            def _():
                up_first[i].wait_recv()

            above = from_upper[*c] + from_lower[*c]
            below[*p] = above + lower * pair[*c]
            column[*p] = above + upper * column[*p]
            shares[i].start()

    def rows_in():
        @pl.when(has_minus)
        def _():
            row_plus.wait_recv()

        @pl.when(follows)
        def _():
            row_minus.start()
            to_minus.start()

        @pl.when(jnp.logical_not(has_minus))
        def _():
            row_column[0] = jnp.zeros((1, full), jnp.float32)

        @pl.when(has_plus)
        def _():
            row_plus.wait_send()
            row_minus.wait_recv()

        @pl.when(jnp.logical_not(has_plus))
        def _():
            row_column[1] = jnp.zeros((1, full), jnp.float32)

        row_pairing.start()

    def neighbours():
        @pl.when(has_minus)
        def _():
            row_minus.wait_send()
            to_minus.wait_send()
            to_plus.wait_recv()

        @pl.when(jnp.logical_not(has_minus))
        def _():
            from_minus[...] = jnp.zeros_like(from_minus)

        @pl.when(has_plus)
        def _():
            to_plus.wait_send()
            to_minus.wait_recv()

        @pl.when(jnp.logical_not(has_plus))
        def _():
            from_plus[...] = jnp.zeros_like(from_plus)


    def row_first():
        row_pairing.wait()
        row_sums[...] = row_column[...] + row_pair[...]
        for j, link in enumerate(row_links, 1):
            @pl.when(x >= j)
            def _():
                link.start()

            @pl.when(x + j >= chips)
            def _():
                row_slots[j - 1] = jnp.zeros((2, 1, full), jnp.float32)

    row_index = (lat * rows + row32).astype(jnp.float32)
    lat_total = lat_count * rows
    center = (row_index + 0.5) * (math.pi / lat_total) - 0.5 * math.pi
    trig[0] = (time_step * coriolis) * jnp.sin(center)
    trig[1] = (0.5 * time_step) * jnp.cos(center)
    trig[2] = (0.25 * time_step) * jnp.sin(row_index * (math.pi / lat_total))
    top, bottom = row32 == 0, row32 == rows - 1

    def down(x, halo):
        return jnp.where(top, halo, pltpu.roll(x, 1, 0))

    def up(x, halo):
        return jnp.where(bottom, halo, pltpu.roll(x, rows - 1, 0))

    def east(x):
        return pltpu.roll(x, WIDE - 1, 1)

    def west(x):
        return pltpu.roll(x, 1, 1)

    def inside(first, last):
        sin_center, cos_center, edge = trig[0], trig[1], trig[2]

        def one_segment(s, carry):
            total = jnp.zeros((rows, WIDE), jnp.float32)
            for level in reversed(range(levels)):
                u, v, h = field[level, s], field[levels + level, s], field[2 * levels + level, s]
                geo = total + 0.5 * h
                total = total + h
                zonal = (0.25 * time_step) * (h + east(h)) * (u + east(u))
                merid = jnp.where(top, 0.0, (h + pltpu.roll(h, 1, 0)) * (v + pltpu.roll(v, 1, 0)) * edge)
                result[2 * levels + level, s] = h - ((zonal - west(zonal)) + (up(merid, 0.0) - merid))
                result[level, s] = u - (0.5 * time_step) * (east(geo) - west(geo)) + sin_center * v
                result[levels + level, s] = v - cos_center * (up(geo, 0.0) - down(geo, 0.0)) - sin_center * u
            return carry

        lax.fori_loop(first, last, one_segment, 0)

    def write_rows(target, source, parts):
        for p in parts:
            here = pl.ds(p * 8, 8)
            tiles = joined([source(s, here) for s in range(RADIX)])
            for t in range(RADIX - 1):
                target[here, t * WIDE : (t + 1) * WIDE] = tiles[t]
            target[here, (RADIX - 1) * WIDE : lon] = tiles[RADIX - 1][:, : lon - (RADIX - 1) * WIDE]

    def write_units(first, parts):
        def unit(level, carry):
            index = first + level
            write_rows(out.at[index], lambda s, here: result[index, s, here, :], parts)
            return carry

        lax.fori_loop(0, levels, unit, 0)

    stores = [
        pltpu.make_async_copy(out.at[pl.ds(0, levels)], part_winds.at[0], store_sem.at[0]),
        pltpu.make_async_copy(out.at[pl.ds(levels, levels)], part_winds.at[1], store_sem.at[1]),
        pltpu.make_async_copy(out.at[pl.ds(2 * levels, levels)], new_thick, store_sem.at[2]),
        pltpu.make_async_copy(out_delta, delta, store_sem.at[3]),
    ]

    def write_first():
        write_units(0, range(4))
        stores[0].start()

    def write_middle():
        write_units(levels, (1, 2))
        write_units(2 * levels, (1, 2))

    def rest_of_loads():
        for load in loads[3:]:
            load.wait()

    def run(*stages):
        for stage in stages:
            stage()

    some = lambda stage, *args: functools.partial(stage, *args)

    turn = follows | leads

    @pl.when(turn)
    def _():
        run(enter, limits, forward_thick, first_step, rest_of_loads, forward_winds, some(products, range(3)))
        run(some(second_step, range(count)), some(products, range(3, 6)), share, inverse, some(inside, 0, RADIX))
        run(write_first, write_middle, rows_in, row_first, neighbours)

    @pl.when(jnp.logical_not(turn))
    def _():
        run(enter, limits, forward_thick, first_step, rest_of_loads, forward_winds, some(products, range(3)))
        run(some(second_step, range(count)), rows_in, some(products, range(3, 6)), row_first, inverse, share)
        run(some(inside, 0, RADIX), write_first, write_middle, neighbours)

    for i, c in enumerate(pieces):
        shares[i].wait()
        below[*others[i]] = shared[*c]

    for j, link in enumerate(row_links, 1):
        @pl.when(x + j < chips)
        def _():
            link.wait_recv()

    sin_center, cos_center, edge = trig[0], trig[1], trig[2]
    last_index = (lat * rows + rows + jnp.zeros((8, WIDE), jnp.int32)).astype(jnp.float32)
    last_edge = (0.25 * time_step) * jnp.sin(last_index * (math.pi / lat_total))
    minus_cut = from_minus[:, full - WIDE :][:, WIDE - 1 :]
    plus_cut = from_plus[:, full - WIDE :][:, WIDE - 1 :]
    cut2[pl.ds(rows, 8), :] = jnp.broadcast_to(minus_cut, (8, WIDE))
    cut2[pl.ds(rows + 8, 8), :] = jnp.broadcast_to(plus_cut, (8, WIDE))
    row16 = lax.broadcasted_iota(jnp.int32, (16, WIDE), 0)
    cut2[pl.ds(rows + 16, 16), :] = jnp.where(row16 == 0, minus_cut[0:1], plus_cut[0:1])
    for half in range(rows // 16):
        forward_rows(tiles_of(lambda c: below[pl.ds(half * 16, 16), c]), y2_high, y2_low, half * 16)
    forward_rows(tiles_of(lambda c: jnp.concatenate([from_minus[:, c], from_plus[:, c]], axis=0)), y2_high, y2_low, rows)
    for at in range(2):
        row_column[at] = row_slots[0, at] + row_slots[1, at] + row_slots[2, at] + lower * row_pair[at]

    def edge_tile(c):
        return jnp.where(row16 == 0, row_column[0, :, c], jnp.where(row16 == 1, row_column[1, :, c], 0.0))

    forward_rows(tiles_of(edge_tile), y2_high, y2_low, rows + 16)
    for k in range(6):
        filter_class(k, y2_high, y2_low, z2, cut2, wave, f_high, f_low)
    for group in range((rows + 32) // 16):
        here = pl.ds(group * 16, 16)
        parts = [(z2[k, here, :WIDE], z2[k, here, WIDE:]) for k in range(6)]
        for s, value in enumerate(inverse12(parts)):
            outer[s, here, :] = value

    eight = lax.broadcasted_iota(jnp.int32, (8, WIDE), 0)
    at_top, at_bottom = eight == 0, eight == 7
    head, tail = pl.ds(0, 8), pl.ds(rows - 8, 8)

    def patch(s, carry):
        total = outer[s, pl.ds(0, rows), :]
        sides = outer[s, pl.ds(rows, 32), :]
        grad[0, s] = -(0.5 * time_step) * (east(total) - west(total))
        grad[1, s] = -cos_center * (up(total, sides[17:18]) - down(total, sides[16:17]))
        minus_total = plus_total = jnp.zeros((1, WIDE), jnp.float32)
        for level in reversed(range(levels)):
            hm, vm = sides[level : level + 1], sides[levels + level : levels + level + 1]
            hp, vp = sides[8 + level : 9 + level], sides[8 + levels + level : 9 + levels + level]
            vi, hi = levels + level, 2 * levels + level
            geo_minus, geo_plus = minus_total + 0.5 * hm, plus_total + 0.5 * hp
            minus_total, plus_total = minus_total + hm, plus_total + hp
            result[vi, s, head, :] += jnp.where(at_top, cos_center[:8] * geo_minus, 0.0)
            result[vi, s, tail, :] -= jnp.where(at_bottom, cos_center[rows - 8 :] * geo_plus, 0.0)
            first = (field[hi, s, head, :] + hm) * (field[vi, s, head, :] + vm) * edge[:8]
            final = (field[hi, s, tail, :] + hp) * (field[vi, s, tail, :] + vp) * last_edge
            result[hi, s, head, :] += jnp.where(at_top, first, 0.0)
            result[hi, s, tail, :] -= jnp.where(at_bottom, final, 0.0)
        return carry

    lax.fori_loop(0, RADIX, patch, 0)
    write_units(levels, (0, 3))
    stores[1].start()
    write_units(2 * levels, (0, 3))
    stores[2].start()
    for which in range(2):
        write_rows(out_delta.at[which], lambda s, here: grad[which, s, here, :], range(4))
    stores[3].start()

    @pl.when(x >= 1)
    def _():
        for link in down_first:
            link.wait_send()

    @pl.when((x == 0) | (x == 3))
    def _():
        for link in up_first:
            link.wait_send()

    for j, link in enumerate(row_links, 1):
        @pl.when(x >= j)
        def _():
            link.wait_send()

    for store in stores:
        store.wait()


def step(shape, winds, thick, cutoff):
    levels, rows, lon = thick.shape
    high, low, wave = filter_tables(lon)
    full = RADIX * WIDE
    part = rows // 2
    units = 3 * levels * rows
    more = rows + 32
    f32 = lambda *dims: pltpu.VMEM(dims, jnp.float32)
    bf16 = lambda *dims: pltpu.VMEM(dims, jnp.bfloat16)
    hbm = pl.BlockSpec(memory_space=pltpu.HBM)
    free = pl.BlockSpec(memory_space=pl.ANY)
    return pl.pallas_call(
        functools.partial(step_kernel, shape["lat"], shape["lev"]),
        out_shape=(
            jax.ShapeDtypeStruct(winds.shape, jnp.float32),
            jax.ShapeDtypeStruct(thick.shape, jnp.float32),
            jax.ShapeDtypeStruct((2, rows, lon), jnp.float32),
        ),
        in_specs=[hbm] * 6,
        out_specs=(free, free, free),
        scratch_shapes=[
            pltpu.SMEM((rows,), jnp.int32),
            f32(1, RADIX * WIDE),
            f32(levels, rows, lon),
            f32(2, levels, rows, lon),
            bf16(*high.shape),
            bf16(*low.shape),
            bf16(6, units, 2 * WIDE),
            bf16(6, units, 2 * WIDE),
            f32(6, units, 2 * WIDE),
            f32(3 * levels, RADIX, rows, WIDE),
            f32(3 * levels, RADIX, rows, WIDE),
            f32(units, WIDE),
            bf16(6, more, 2 * WIDE),
            bf16(6, more, 2 * WIDE),
            f32(6, more, 2 * WIDE),
            f32(RADIX, more, WIDE),
            f32(2, RADIX, rows, WIDE),
            f32(more, WIDE),
            f32(3 * levels, rows, lon),
            f32(2, rows, lon),
            f32(3, rows, WIDE),
            f32(8, full),
            f32(8, full),
            f32(8, full),
            f32(8, full),
            f32(rows, full),
            f32(rows, full),
            f32(part, full),
            f32(part, full),
            f32(part, full),
            f32(part, full),
            f32(part, full),
            f32(part, full),
            f32(2, 1, full),
            f32(2, 1, full),
            f32(2, 1, full),
            f32(3, 2, 1, full),
            f32(2, 1, full),
            pltpu.SemaphoreType.DMA((7,)),
            pltpu.SemaphoreType.DMA((4,)),
            pltpu.SemaphoreType.DMA((21,)),
            pltpu.SemaphoreType.DMA((21,)),
        ],
        compiler_params=pltpu.CompilerParams(collective_id=0, has_side_effects=True, vmem_limit_bytes=24 << 20),
    )(*[pltpu.with_memory_space_constraint(v, pltpu.HBM) for v in (thick, winds, cutoff, jnp.asarray(wave), jnp.asarray(high), jnp.asarray(low))])


def last_kernel(part_winds, part_thick, delta, new_winds, new_thick, w, sem):
    levels = part_thick.shape[0]
    stores = [pltpu.make_async_copy(part_thick, new_thick, sem.at[2 * levels])]
    stores[0].start()
    for f in range(2):
        for level in range(levels):
            w[f, level] = part_winds[f, level] + delta[f]
            store = pltpu.make_async_copy(w.at[f, level], new_winds.at[f, level], sem.at[f * levels + level])
            store.start()
            stores.append(store)
    for store in stores:
        store.wait()


def last(part_winds, part_thick, delta):
    hbm = pl.BlockSpec(memory_space=pltpu.HBM)
    vmem = pl.BlockSpec(memory_space=pltpu.VMEM)
    return pl.pallas_call(
        last_kernel,
        out_shape=(
            jax.ShapeDtypeStruct(part_winds.shape, jnp.float32),
            jax.ShapeDtypeStruct(part_thick.shape, jnp.float32),
        ),
        in_specs=[vmem, vmem, vmem],
        out_specs=(hbm, hbm),
        scratch_shapes=[
            pltpu.VMEM(part_winds.shape, jnp.float32),
            pltpu.SemaphoreType.DMA((2 * part_thick.shape[0] + 1,)),
        ],
        compiler_params=pltpu.CompilerParams(vmem_limit_bytes=8 << 20),
    )(part_winds, part_thick, delta)


def solution(mesh):
    shape = dict(mesh.shape)

    def per_device(winds, thickness, cutoff):
        return last(*step(shape, winds, thickness, cutoff))

    return jax.shard_map(
        per_device,
        mesh=mesh,
        in_specs=(P(None, "lev", "lat", None), P("lev", "lat", None), P("lat")),
        out_specs=(P(None, "lev", "lat", None), P("lev", "lat", None)),
        check_vma=False,
    )
```

```python
import functools
import math

import jax
import jax.numpy as jnp
import numpy as np
from jax import lax
from jax.experimental import pallas as pl
from jax.experimental.pallas import tpu as pltpu
from jax.sharding import PartitionSpec as P

MESH = pl.DeviceIdType.MESH
time_step = 0.2
coriolis = 1.0
RADIX = 12
HALO = 4
WIDE = 128
HALF3 = 0.5 * math.sqrt(3.0)


def filter_tables(lon):
    seg = lon // RADIX
    points = np.arange(WIDE) - HALO
    scale = math.sqrt(2.0 / lon)
    table = np.zeros((6, 2 * WIDE, 2 * WIDE))
    wave = np.full((6, 2 * WIDE), float(lon))
    turn = 2.0 * math.pi / lon
    j = np.arange(seg)
    for k in range(1, 6):
        m = RADIX * j + k
        angle = turn * ((points[:, None] * m[None, :]) % lon)
        table[k, :WIDE, :seg] = np.cos(angle) * scale
        table[k, :WIDE, WIDE : WIDE + seg] = np.sin(angle) * scale
        table[k, WIDE:, :seg] = -np.sin(angle) * scale
        table[k, WIDE:, WIDE : WIDE + seg] = np.cos(angle) * scale
        wave[k, :seg] = wave[k, WIDE : WIDE + seg] = np.minimum(m, lon - m)
    half = seg // 2
    m = RADIX * np.arange(half + 1)
    weight = np.where((m == 0) | (m == lon // 2), scale / math.sqrt(2.0), scale)
    angle = turn * ((points[:, None] * m[None, :]) % lon)
    table[0, :WIDE, : half + 1] = np.cos(angle) * weight
    table[0, :WIDE, half + 1 : seg] = np.sin(angle[:, 1:half]) * scale
    wave[0, : half + 1] = m
    wave[0, half + 1 : seg] = m[1:half]
    m = RADIX * np.arange(half) + RADIX // 2
    angle = turn * ((points[:, None] * m[None, :]) % lon)
    table[0, WIDE:, WIDE : WIDE + half] = np.cos(angle) * scale
    table[0, WIDE:, WIDE + half : WIDE + seg] = np.sin(angle) * scale
    wave[0, WIDE : WIDE + half] = wave[0, WIDE + half : WIDE + seg] = m
    table = table.astype(np.float32)
    high = table.astype(jnp.bfloat16)
    low = (table - high.astype(np.float32)).astype(jnp.bfloat16)
    return high, low, wave.astype(np.float32).reshape(1, 12 * WIDE)


def split(x):
    high = x.astype(jnp.bfloat16)
    return high, (x - high.astype(jnp.float32)).astype(jnp.bfloat16)


def forward12(x):
    e = [x[s] + x[s + 6] for s in range(6)]
    o = [x[s] - x[s + 6] for s in range(6)]
    ee = [e[s] + e[s + 3] for s in range(3)]
    eo = [e[s] - e[s + 3] for s in range(3)]
    sum12 = ee[1] + ee[2]
    d15, s15, d24, s24 = o[1] - o[5], o[1] + o[5], o[2] - o[4], o[2] + o[4]
    a, b = o[0] + 0.5 * d24, HALF3 * d15
    c, d = 0.5 * s15 + o[3], HALF3 * s24
    return [
        (ee[0] + sum12, eo[0] - eo[1] + eo[2]),
        (a + b, c + d),
        (eo[0] + 0.5 * (eo[1] - eo[2]), HALF3 * (eo[1] + eo[2])),
        (o[0] - d24, s15 - o[3]),
        (ee[0] - 0.5 * sum12, HALF3 * (ee[1] - ee[2])),
        (a - b, c - d),
    ]


def inverse12(z):
    (z0, z6), (r1, n1), (r2, n2), (r3, n3), (r4, n4), (r5, n5) = z
    a, b = HALF3 * (r1 - r5), 0.5 * (n1 + n5) + n3
    c, d = 0.5 * (r1 + r5) - r3, HALF3 * (n1 - n5)
    odd = [r1 + r3 + r5, b + a, c + d, n1 - n3 + n5, d - c, b - a]
    low, h4 = z0 - 0.5 * r4, HALF3 * n4
    ee = [z0 + r4, low + h4, low - h4]
    h2, hr = HALF3 * n2, 0.5 * r2
    eo = [z6 + r2, hr + h2 - z6, z6 - hr + h2]
    even = [ee[s] + eo[s] for s in range(3)] + [ee[s] - eo[s] for s in range(3)]
    return [even[s] + odd[s] for s in range(6)] + [even[s] - odd[s] for s in range(6)]


def lanes_of(shape):
    return lax.broadcasted_iota(jnp.int32, shape, len(shape) - 1)


def segments(tiles):
    lane = lanes_of(tiles[0].shape)
    out = [pltpu.roll(tiles[0], HALO, 1)]
    for s in range(1, RADIX):
        shift = 8 * s + HALO
        out.append(pltpu.roll(jnp.where(lane >= WIDE - shift, tiles[s - 1], tiles[s]), shift, 1))
    return out


def joined(segs):
    lane = lanes_of(segs[0].shape)
    out = []
    for t in range(RADIX):
        tile = pltpu.roll(segs[t], WIDE - (8 * t + HALO), 1)
        if t + 1 < RADIX:
            later = pltpu.roll(segs[t + 1], 116 - 8 * t, 1)
            tile = jnp.where(lane < 120 - 8 * t, tile, later)
        out.append(tile)
    return out


def forward_rows(tiles, y_high, y_low, row):
    lane = lanes_of((16, WIDE))
    inside = (lane >= HALO) & (lane < WIDE - HALO)
    classes = forward12(segments(tiles))
    for k, parts in enumerate(classes):
        for at, part in enumerate(parts):
            high, low = split(jnp.where(inside, part, 0.0))
            y_high[k, pl.ds(row, 16), at * WIDE : (at + 1) * WIDE] = high
            y_low[k, pl.ds(row, 16), at * WIDE : (at + 1) * WIDE] = low


def tiles_of(load):
    return [load(pl.ds(t * WIDE, WIDE)) for t in range(RADIX)]


def narrow_tiles(load, lon):
    last = lon - (RADIX - 1) * WIDE
    tiles = [load(pl.ds(t * WIDE, WIDE)) for t in range(RADIX - 1)]
    end = load(pl.ds((RADIX - 1) * WIDE, last))
    return tiles + [jnp.concatenate([end, jnp.zeros((end.shape[0], WIDE - last), jnp.float32)], axis=1)]


def filter_class(k, y_high, y_low, z, cut, wave, f_high, f_low):
    high, low = f_high[k], f_low[k]
    yh, yl = y_high[k], y_low[k]
    coeffs = jnp.dot(
        jnp.concatenate([yh, yl, yh], axis=1),
        jnp.concatenate([high, high, low], axis=0),
        preferred_element_type=jnp.float32,
    )
    limit = cut[...]
    wanted = wave[:, pl.ds(k * 2 * WIDE, 2 * WIDE)]
    keep = jnp.concatenate([limit >= wanted[:, :WIDE], limit >= wanted[:, WIDE:]], axis=1)
    xh, xl = split(jnp.where(keep, coeffs, 0.0))
    z[k] = lax.dot_general(
        jnp.concatenate([xh, xl, xh], axis=1),
        jnp.concatenate([high, high, low], axis=1),
        (((1,), (1,)), ((), ())),
        preferred_element_type=jnp.float32,
    )


def step_kernel(
    lat_count,
    lev_count,
    thick,
    winds,
    cutoff_in,
    wave_in,
    table_high,
    table_low,
    part_winds,
    new_thick,
    delta,
    cutoff,
    wave,
    h_in,
    w_in,
    f_high,
    f_low,
    y_high,
    y_low,
    z,
    field,
    result,
    cut,
    y2_high,
    y2_low,
    z2,
    outer,
    grad,
    cut2,
    out,
    out_delta,
    trig,
    send_minus,
    send_plus,
    from_minus,
    from_plus,
    column,
    below,
    pair,
    sums,
    from_upper,
    from_lower,
    relay,
    shared,
    row_column,
    row_pair,
    row_sums,
    row_slots,
    send_row,
    load_sem,
    store_sem,
    send_sem,
    recv_sem,
):
    levels, rows, lon = thick.shape
    full = RADIX * WIDE
    part = rows // 2
    fields = 3 * levels
    lat, lev = lax.axis_index("lat"), lax.axis_index("lev")
    x, core = lev // 2, lev % 2
    chips = lev_count // 2
    partner = x * 2 + (1 - core)
    chip_at = lambda other: ((other + chips) % chips) * 2 + core
    x_up, x_down = ((x + 1) % chips) * 2 + core, ((x + chips - 1) % chips) * 2 + core
    has_minus, has_plus = lat > 0, lat < lat_count - 1
    lat_minus, lat_plus = jnp.maximum(lat - 1, 0), jnp.minimum(lat + 1, lat_count - 1)
    follows = (lat % 8 == 0) & has_minus
    leads = (lat % 8 == 7) & has_plus

    barrier = pltpu.get_barrier_semaphore()
    for device in ((lat, partner), (lat, x_up), (lat, x_down), (lat, chip_at(x + 2))):
        pl.semaphore_signal(barrier, inc=1, device_id=device, device_id_type=MESH)

    @pl.when(has_minus)
    def _():
        pl.semaphore_signal(barrier, inc=1, device_id=(lat_minus, lev), device_id_type=MESH)

    @pl.when(has_plus & jnp.logical_not(leads))
    def _():
        pl.semaphore_signal(barrier, inc=1, device_id=(lat_plus, lev), device_id_type=MESH)

    loads = [
        pltpu.make_async_copy(source, target, load_sem.at[i])
        for i, (source, target) in enumerate(
            (
                (thick, h_in),
                (winds.at[1], w_in.at[1]),
                (cutoff_in, cutoff),
                (wave_in, wave),
                (table_high, f_high),
                (table_low, f_low),
                (winds.at[0], w_in.at[0]),
            )
        )
    ]
    for load in loads[:3]:
        load.start()

    def remote(source, target, at, device):
        return pltpu.make_async_remote_copy(
            src_ref=source,
            dst_ref=target,
            send_sem=send_sem.at[at],
            recv_sem=recv_sem.at[at],
            device_id=device,
            device_id_type=MESH,
        )

    row32 = lax.broadcasted_iota(jnp.int32, (rows, WIDE), 0)

    def limits():
        limit = jnp.zeros((rows, WIDE), jnp.float32)
        for r in range(rows):
            limit = jnp.where(row32 == r, cutoff[r].astype(jnp.float32), limit)
        for unit in range(fields):
            cut[pl.ds(unit * rows, rows), :] = limit
        cut2[pl.ds(0, rows), :] = limit

    def forward_thick():
        def unit(level, carry):
            for half in range(rows // 16):
                here = pl.ds(half * 16, 16)
                tiles = narrow_tiles(lambda c: h_in[level, here, c], lon)
                forward_rows(tiles, y_high, y_low, (2 * levels + level) * rows + half * 16)
            return carry

        lax.fori_loop(0, levels, unit, 0)

    def forward_winds():
        def unit(index, carry):
            for half in range(rows // 16):
                here = pl.ds(half * 16, 16)
                tiles = narrow_tiles(lambda c: w_in[index // levels, index % levels, here, c], lon)
                forward_rows(tiles, y_high, y_low, index * rows + half * 16)
            return carry

        lax.fori_loop(0, 2 * levels, unit, 0)

    def products(classes):
        for k in classes:
            filter_class(k, y_high, y_low, z, cut, wave, f_high, f_low)

    def inverse():
        def unit(index, carry):
            for half in range(rows // 16):
                here = pl.ds(index * rows + half * 16, 16)
                parts = [(z[k, here, :WIDE], z[k, here, WIDE:]) for k in range(6)]
                for s, value in enumerate(inverse12(parts)):
                    field[index, s, pl.ds(half * 16, 16), :] = value
            return carry

        lax.fori_loop(0, fields, unit, 0)

    loads[0].wait()
    for load in loads[3:]:
        load.start()
    total = h_in[0]
    for level in range(1, levels):
        total = total + h_in[level]
    column[:, pl.ds(full - WIDE, WIDE)] = jnp.zeros((rows, WIDE), jnp.float32)
    column[:, pl.ds(0, lon)] = total
    send_row[0] = column[0:1, :]
    send_row[1] = column[rows - 1 : rows, :]
    loads[1].wait()
    loads[2].wait()
    row8 = lax.broadcasted_iota(jnp.int32, (8, lon), 0)
    for pack, row in ((send_minus, 0), (send_plus, rows - 1)):
        value = jnp.zeros((8, lon), jnp.float32)
        for level in range(levels):
            value = jnp.where(row8 == level, h_in[level, row : row + 1, :], value)
            value = jnp.where(row8 == levels + level, w_in[1, level, row : row + 1, :], value)
        pack[:, pl.ds(full - WIDE, WIDE)] = jnp.broadcast_to(cutoff[row].astype(jnp.float32), (8, WIDE))
        pack[:, pl.ds(0, lon)] = value

    one = lambda flag: jnp.where(flag, 1, 0)
    mine, theirs = pl.multiple_of(core * part, part), pl.multiple_of((1 - core) * part, part)
    upper = jnp.where(core == 0, 0.0, 1.0)
    lower = 1.0 - upper
    chunks = [(8 * r, full // 2 * c) for r in range(part // 8) for c in range(2)]
    pieces = [(pl.ds(r, 8), pl.ds(c, full // 2)) for r, c in chunks]
    places = [(pl.ds(pl.multiple_of(mine + r, 8), 8), pl.ds(c, full // 2)) for r, c in chunks]
    others = [(pl.ds(pl.multiple_of(theirs + r, 8), 8), pl.ds(c, full // 2)) for r, c in chunks]
    count = len(pieces)
    to_pair = remote(column.at[pl.ds(theirs, part), :], pair, 0, (lat, partner))
    to_minus = remote(send_minus, from_plus, 1, (lat_minus, lev))
    to_plus = remote(send_plus, from_minus, 2, (lat_plus, lev))
    down_first = [remote(sums.at[*c], from_upper.at[*c], 3 + i, (lat, x_down)) for i, c in enumerate(pieces)]
    down_later = [remote(relay.at[*c], from_upper.at[*c], 3 + i, (lat, x_down)) for i, c in enumerate(pieces)]
    up_first = [remote(sums.at[*c], from_lower.at[*c], 3 + count + i, (lat, x_up)) for i, c in enumerate(pieces)]
    up_later = [remote(from_lower.at[*c], from_lower.at[*c], 3 + count + i, (lat, x_up)) for i, c in enumerate(pieces)]
    row_pairing = remote(row_column, row_pair, 3 + 3 * count, (lat, partner))
    row_minus = remote(send_row.at[0], row_column.at[1], 4 + 3 * count, (lat_minus, lev))
    row_plus = remote(send_row.at[1], row_column.at[0], 5 + 3 * count, (lat_plus, lev))
    row_links = [remote(row_sums, row_slots.at[j - 1], 5 + 3 * count + j, (lat, chip_at(x - j))) for j in range(1, 4)]
    shares = [remote(column.at[*p], shared.at[*c], 3 + 2 * count + i, (lat, partner)) for i, (p, c) in enumerate(zip(places, pieces))]

    def enter():
        pl.semaphore_wait(barrier, 4 + one(has_minus & jnp.logical_not(follows)) + one(has_plus))
        @pl.when(has_minus & jnp.logical_not(follows))
        def _():
            row_minus.start()

        @pl.when(has_plus)
        def _():
            row_plus.start()

        to_pair.start()

        @pl.when(has_minus & jnp.logical_not(follows))
        def _():
            to_minus.start()

        @pl.when(has_plus)
        def _():
            to_plus.start()

    def first_step():
        to_pair.wait()
        sums[...] = column[pl.ds(mine, part), :] + pair[...]
        for i in range(count):
            @pl.when(x >= 2)
            def _():
                down_first[i].start()

            @pl.when(x == 3)
            def _():
                up_first[i].start()

        @pl.when(x == chips - 1)
        def _():
            from_upper[...] = jnp.zeros_like(from_upper)

        @pl.when(x >= chips - 2)
        def _():
            from_lower[...] = jnp.zeros_like(from_lower)

    def second_step(which):
        for i in which:
            c = pieces[i]
            @pl.when((x == 1) | (x == 2))
            def _():
                down_first[i].wait_recv()

            @pl.when(x == 1)
            def _():
                relay[*c] = sums[*c] + from_upper[*c]
                down_later[i].start()

            @pl.when(x == 0)
            def _():
                up_first[i].wait_recv()
                up_later[i].start()

    def share():
        for i, (p, c) in enumerate(zip(places, pieces)):
            @pl.when(x == 0)
            def _():
                down_first[i].wait_recv()

            @pl.when(x == 1)
            def _():
                up_first[i].wait_recv()

            above = from_upper[*c] + from_lower[*c]
            below[*p] = above + lower * pair[*c]
            column[*p] = above + upper * column[*p]
            shares[i].start()

    def rows_in():
        @pl.when(has_minus)
        def _():
            row_plus.wait_recv()

        @pl.when(follows)
        def _():
            row_minus.start()
            to_minus.start()

        @pl.when(jnp.logical_not(has_minus))
        def _():
            row_column[0] = jnp.zeros((1, full), jnp.float32)

        @pl.when(has_plus)
        def _():
            row_plus.wait_send()
            row_minus.wait_recv()

        @pl.when(jnp.logical_not(has_plus))
        def _():
            row_column[1] = jnp.zeros((1, full), jnp.float32)

        row_pairing.start()

    def neighbours():
        @pl.when(has_minus)
        def _():
            row_minus.wait_send()
            to_minus.wait_send()
            to_plus.wait_recv()

        @pl.when(jnp.logical_not(has_minus))
        def _():
            from_minus[...] = jnp.zeros_like(from_minus)

        @pl.when(has_plus)
        def _():
            to_plus.wait_send()
            to_minus.wait_recv()

        @pl.when(jnp.logical_not(has_plus))
        def _():
            from_plus[...] = jnp.zeros_like(from_plus)


    def row_first():
        row_pairing.wait()
        row_sums[...] = row_column[...] + row_pair[...]
        for j, link in enumerate(row_links, 1):
            @pl.when(x >= j)
            def _():
                link.start()

            @pl.when(x + j >= chips)
            def _():
                row_slots[j - 1] = jnp.zeros((2, 1, full), jnp.float32)

    row_index = (lat * rows + row32).astype(jnp.float32)
    lat_total = lat_count * rows
    center = (row_index + 0.5) * (math.pi / lat_total) - 0.5 * math.pi
    trig[0] = (time_step * coriolis) * jnp.sin(center)
    trig[1] = (0.5 * time_step) * jnp.cos(center)
    trig[2] = (0.25 * time_step) * jnp.sin(row_index * (math.pi / lat_total))
    top, bottom = row32 == 0, row32 == rows - 1

    def down(x, halo):
        return jnp.where(top, halo, pltpu.roll(x, 1, 0))

    def up(x, halo):
        return jnp.where(bottom, halo, pltpu.roll(x, rows - 1, 0))

    def east(x):
        return pltpu.roll(x, WIDE - 1, 1)

    def west(x):
        return pltpu.roll(x, 1, 1)

    def inside(first, last):
        sin_center, cos_center, edge = trig[0], trig[1], trig[2]

        def one_segment(s, carry):
            total = jnp.zeros((rows, WIDE), jnp.float32)
            for level in reversed(range(levels)):
                u, v, h = field[level, s], field[levels + level, s], field[2 * levels + level, s]
                geo = total + 0.5 * h
                total = total + h
                zonal = (0.25 * time_step) * (h + east(h)) * (u + east(u))
                merid = jnp.where(top, 0.0, (h + pltpu.roll(h, 1, 0)) * (v + pltpu.roll(v, 1, 0)) * edge)
                result[2 * levels + level, s] = h - ((zonal - west(zonal)) + (up(merid, 0.0) - merid))
                result[level, s] = u - (0.5 * time_step) * (east(geo) - west(geo)) + sin_center * v
                result[levels + level, s] = v - cos_center * (up(geo, 0.0) - down(geo, 0.0)) - sin_center * u
            return carry

        lax.fori_loop(first, last, one_segment, 0)

    def write_rows(target, source, parts):
        for p in parts:
            here = pl.ds(p * 8, 8)
            tiles = joined([source(s, here) for s in range(RADIX)])
            for t in range(RADIX - 1):
                target[here, t * WIDE : (t + 1) * WIDE] = tiles[t]
            target[here, (RADIX - 1) * WIDE : lon] = tiles[RADIX - 1][:, : lon - (RADIX - 1) * WIDE]

    def write_units(first, parts):
        def unit(level, carry):
            index = first + level
            write_rows(out.at[index], lambda s, here: result[index, s, here, :], parts)
            return carry

        lax.fori_loop(0, levels, unit, 0)

    stores = [
        pltpu.make_async_copy(out.at[pl.ds(0, levels)], part_winds.at[0], store_sem.at[0]),
        pltpu.make_async_copy(out.at[pl.ds(levels, levels)], part_winds.at[1], store_sem.at[1]),
        pltpu.make_async_copy(out.at[pl.ds(2 * levels, levels)], new_thick, store_sem.at[2]),
        pltpu.make_async_copy(out_delta, delta, store_sem.at[3]),
    ]

    def write_first():
        write_units(0, range(4))
        stores[0].start()

    def write_middle():
        write_units(levels, (1, 2))
        write_units(2 * levels, (1, 2))

    def rest_of_loads():
        for load in loads[3:]:
            load.wait()

    def run(*stages):
        for stage in stages:
            stage()

    some = lambda stage, *args: functools.partial(stage, *args)

    turn = follows | leads | (lat == 1)
    wait_first = (lat == 0) & (lev > 0)

    @pl.when(wait_first)
    def _():
        run(rest_of_loads, limits, forward_thick, forward_winds, some(products, range(6)))
        run(enter, first_step, rows_in, some(second_step, range(count // 2)), row_first)
        run(some(second_step, range(count // 2, count)), inverse, share)
        run(some(inside, 0, RADIX), write_first, write_middle, neighbours)

    @pl.when(turn)
    def _():
        run(enter, limits, forward_thick, first_step, rest_of_loads, forward_winds, some(products, range(3)))
        run(some(second_step, range(count)), some(products, range(3, 6)), share, inverse)
        run(some(inside, 0, RADIX // 2), rows_in, some(inside, RADIX // 2, RADIX), row_first)
        run(write_first, write_middle, neighbours)

    @pl.when(jnp.logical_not(turn | wait_first))
    def _():
        run(enter, limits, forward_thick, first_step, rest_of_loads, forward_winds, some(products, range(3)))
        run(some(second_step, range(count)), rows_in, some(products, range(3, 6)), row_first, inverse, share)
        run(some(inside, 0, RADIX), write_first, write_middle, neighbours)

    for i, c in enumerate(pieces):
        shares[i].wait()
        below[*others[i]] = shared[*c]

    for j, link in enumerate(row_links, 1):
        @pl.when(x + j < chips)
        def _():
            link.wait_recv()

    sin_center, cos_center, edge = trig[0], trig[1], trig[2]
    last_index = (lat * rows + rows + jnp.zeros((8, WIDE), jnp.int32)).astype(jnp.float32)
    last_edge = (0.25 * time_step) * jnp.sin(last_index * (math.pi / lat_total))
    minus_cut = from_minus[:, full - WIDE :][:, WIDE - 1 :]
    plus_cut = from_plus[:, full - WIDE :][:, WIDE - 1 :]
    cut2[pl.ds(rows, 8), :] = jnp.broadcast_to(minus_cut, (8, WIDE))
    cut2[pl.ds(rows + 8, 8), :] = jnp.broadcast_to(plus_cut, (8, WIDE))
    row16 = lax.broadcasted_iota(jnp.int32, (16, WIDE), 0)
    cut2[pl.ds(rows + 16, 16), :] = jnp.where(row16 == 0, minus_cut[0:1], plus_cut[0:1])
    for half in range(rows // 16):
        forward_rows(tiles_of(lambda c: below[pl.ds(half * 16, 16), c]), y2_high, y2_low, half * 16)
    forward_rows(tiles_of(lambda c: jnp.concatenate([from_minus[:, c], from_plus[:, c]], axis=0)), y2_high, y2_low, rows)
    for at in range(2):
        row_column[at] = row_slots[0, at] + row_slots[1, at] + row_slots[2, at] + lower * row_pair[at]

    def edge_tile(c):
        return jnp.where(row16 == 0, row_column[0, :, c], jnp.where(row16 == 1, row_column[1, :, c], 0.0))

    forward_rows(tiles_of(edge_tile), y2_high, y2_low, rows + 16)
    for k in range(6):
        filter_class(k, y2_high, y2_low, z2, cut2, wave, f_high, f_low)
    for group in range((rows + 32) // 16):
        here = pl.ds(group * 16, 16)
        parts = [(z2[k, here, :WIDE], z2[k, here, WIDE:]) for k in range(6)]
        for s, value in enumerate(inverse12(parts)):
            outer[s, here, :] = value

    eight = lax.broadcasted_iota(jnp.int32, (8, WIDE), 0)
    at_top, at_bottom = eight == 0, eight == 7
    head, tail = pl.ds(0, 8), pl.ds(rows - 8, 8)

    def patch(s, carry):
        total = outer[s, pl.ds(0, rows), :]
        sides = outer[s, pl.ds(rows, 32), :]
        grad[0, s] = -(0.5 * time_step) * (east(total) - west(total))
        grad[1, s] = -cos_center * (up(total, sides[17:18]) - down(total, sides[16:17]))
        minus_total = plus_total = jnp.zeros((1, WIDE), jnp.float32)
        for level in reversed(range(levels)):
            hm, vm = sides[level : level + 1], sides[levels + level : levels + level + 1]
            hp, vp = sides[8 + level : 9 + level], sides[8 + levels + level : 9 + levels + level]
            vi, hi = levels + level, 2 * levels + level
            geo_minus, geo_plus = minus_total + 0.5 * hm, plus_total + 0.5 * hp
            minus_total, plus_total = minus_total + hm, plus_total + hp
            result[vi, s, head, :] += jnp.where(at_top, cos_center[:8] * geo_minus, 0.0)
            result[vi, s, tail, :] -= jnp.where(at_bottom, cos_center[rows - 8 :] * geo_plus, 0.0)
            first = (field[hi, s, head, :] + hm) * (field[vi, s, head, :] + vm) * edge[:8]
            final = (field[hi, s, tail, :] + hp) * (field[vi, s, tail, :] + vp) * last_edge
            result[hi, s, head, :] += jnp.where(at_top, first, 0.0)
            result[hi, s, tail, :] -= jnp.where(at_bottom, final, 0.0)
        return carry

    lax.fori_loop(0, RADIX, patch, 0)
    write_units(levels, (0, 3))
    stores[1].start()
    write_units(2 * levels, (0, 3))
    stores[2].start()
    for which in range(2):
        write_rows(out_delta.at[which], lambda s, here: grad[which, s, here, :], range(4))
    stores[3].start()

    @pl.when(x >= 1)
    def _():
        for link in down_first:
            link.wait_send()

    @pl.when((x == 0) | (x == 3))
    def _():
        for link in up_first:
            link.wait_send()

    for j, link in enumerate(row_links, 1):
        @pl.when(x >= j)
        def _():
            link.wait_send()

    for store in stores:
        store.wait()


def step(shape, winds, thick, cutoff):
    levels, rows, lon = thick.shape
    high, low, wave = filter_tables(lon)
    full = RADIX * WIDE
    part = rows // 2
    units = 3 * levels * rows
    more = rows + 32
    f32 = lambda *dims: pltpu.VMEM(dims, jnp.float32)
    bf16 = lambda *dims: pltpu.VMEM(dims, jnp.bfloat16)
    hbm = pl.BlockSpec(memory_space=pltpu.HBM)
    free = pl.BlockSpec(memory_space=pl.ANY)
    return pl.pallas_call(
        functools.partial(step_kernel, shape["lat"], shape["lev"]),
        out_shape=(
            jax.ShapeDtypeStruct(winds.shape, jnp.float32),
            jax.ShapeDtypeStruct(thick.shape, jnp.float32),
            jax.ShapeDtypeStruct((2, rows, lon), jnp.float32),
        ),
        in_specs=[hbm] * 6,
        out_specs=(free, free, free),
        scratch_shapes=[
            pltpu.SMEM((rows,), jnp.int32),
            f32(1, RADIX * WIDE),
            f32(levels, rows, lon),
            f32(2, levels, rows, lon),
            bf16(*high.shape),
            bf16(*low.shape),
            bf16(6, units, 2 * WIDE),
            bf16(6, units, 2 * WIDE),
            f32(6, units, 2 * WIDE),
            f32(3 * levels, RADIX, rows, WIDE),
            f32(3 * levels, RADIX, rows, WIDE),
            f32(units, WIDE),
            bf16(6, more, 2 * WIDE),
            bf16(6, more, 2 * WIDE),
            f32(6, more, 2 * WIDE),
            f32(RADIX, more, WIDE),
            f32(2, RADIX, rows, WIDE),
            f32(more, WIDE),
            f32(3 * levels, rows, lon),
            f32(2, rows, lon),
            f32(3, rows, WIDE),
            f32(8, full),
            f32(8, full),
            f32(8, full),
            f32(8, full),
            f32(rows, full),
            f32(rows, full),
            f32(part, full),
            f32(part, full),
            f32(part, full),
            f32(part, full),
            f32(part, full),
            f32(part, full),
            f32(2, 1, full),
            f32(2, 1, full),
            f32(2, 1, full),
            f32(3, 2, 1, full),
            f32(2, 1, full),
            pltpu.SemaphoreType.DMA((7,)),
            pltpu.SemaphoreType.DMA((4,)),
            pltpu.SemaphoreType.DMA((21,)),
            pltpu.SemaphoreType.DMA((21,)),
        ],
        compiler_params=pltpu.CompilerParams(collective_id=0, has_side_effects=True, vmem_limit_bytes=24 << 20),
    )(*[pltpu.with_memory_space_constraint(v, pltpu.HBM) for v in (thick, winds, cutoff, jnp.asarray(wave), jnp.asarray(high), jnp.asarray(low))])


def last_kernel(part_winds, part_thick, delta, new_winds, new_thick, w, sem):
    levels = part_thick.shape[0]
    stores = [pltpu.make_async_copy(part_thick, new_thick, sem.at[2 * levels])]
    stores[0].start()
    for f in range(2):
        for level in range(levels):
            w[f, level] = part_winds[f, level] + delta[f]
            store = pltpu.make_async_copy(w.at[f, level], new_winds.at[f, level], sem.at[f * levels + level])
            store.start()
            stores.append(store)
    for store in stores:
        store.wait()


def last(part_winds, part_thick, delta):
    hbm = pl.BlockSpec(memory_space=pltpu.HBM)
    vmem = pl.BlockSpec(memory_space=pltpu.VMEM)
    return pl.pallas_call(
        last_kernel,
        out_shape=(
            jax.ShapeDtypeStruct(part_winds.shape, jnp.float32),
            jax.ShapeDtypeStruct(part_thick.shape, jnp.float32),
        ),
        in_specs=[vmem, vmem, vmem],
        out_specs=(hbm, hbm),
        scratch_shapes=[
            pltpu.VMEM(part_winds.shape, jnp.float32),
            pltpu.SemaphoreType.DMA((2 * part_thick.shape[0] + 1,)),
        ],
        compiler_params=pltpu.CompilerParams(vmem_limit_bytes=8 << 20),
    )(part_winds, part_thick, delta)


def solution(mesh):
    shape = dict(mesh.shape)

    def per_device(winds, thickness, cutoff):
        return last(*step(shape, winds, thickness, cutoff))

    return jax.shard_map(
        per_device,
        mesh=mesh,
        in_specs=(P(None, "lev", "lat", None), P("lev", "lat", None), P("lat")),
        out_specs=(P(None, "lev", "lat", None), P("lev", "lat", None)),
        check_vma=False,
    )
```

```python
import functools
import math

import jax
import jax.numpy as jnp
import numpy as np
from jax import lax
from jax.experimental import pallas as pl
from jax.experimental.pallas import tpu as pltpu
from jax.sharding import PartitionSpec as P

MESH = pl.DeviceIdType.MESH
time_step = 0.2
coriolis = 1.0
RADIX = 12
HALO = 4
WIDE = 128
HALF3 = 0.5 * math.sqrt(3.0)


def filter_tables(lon):
    seg = lon // RADIX
    points = np.arange(WIDE) - HALO
    scale = math.sqrt(2.0 / lon)
    table = np.zeros((6, 2 * WIDE, 2 * WIDE))
    wave = np.full((6, 2 * WIDE), float(lon))
    turn = 2.0 * math.pi / lon
    j = np.arange(seg)
    for k in range(1, 6):
        m = RADIX * j + k
        angle = turn * ((points[:, None] * m[None, :]) % lon)
        table[k, :WIDE, :seg] = np.cos(angle) * scale
        table[k, :WIDE, WIDE : WIDE + seg] = np.sin(angle) * scale
        table[k, WIDE:, :seg] = -np.sin(angle) * scale
        table[k, WIDE:, WIDE : WIDE + seg] = np.cos(angle) * scale
        wave[k, :seg] = wave[k, WIDE : WIDE + seg] = np.minimum(m, lon - m)
    half = seg // 2
    m = RADIX * np.arange(half + 1)
    weight = np.where((m == 0) | (m == lon // 2), scale / math.sqrt(2.0), scale)
    angle = turn * ((points[:, None] * m[None, :]) % lon)
    table[0, :WIDE, : half + 1] = np.cos(angle) * weight
    table[0, :WIDE, half + 1 : seg] = np.sin(angle[:, 1:half]) * scale
    wave[0, : half + 1] = m
    wave[0, half + 1 : seg] = m[1:half]
    m = RADIX * np.arange(half) + RADIX // 2
    angle = turn * ((points[:, None] * m[None, :]) % lon)
    table[0, WIDE:, WIDE : WIDE + half] = np.cos(angle) * scale
    table[0, WIDE:, WIDE + half : WIDE + seg] = np.sin(angle) * scale
    wave[0, WIDE : WIDE + half] = wave[0, WIDE + half : WIDE + seg] = m
    table = table.astype(np.float32)
    high = table.astype(jnp.bfloat16)
    low = (table - high.astype(np.float32)).astype(jnp.bfloat16)
    return high, low, wave.astype(np.float32).reshape(1, 12 * WIDE)


def split(x):
    high = x.astype(jnp.bfloat16)
    return high, (x - high.astype(jnp.float32)).astype(jnp.bfloat16)


def forward12(x):
    e = [x[s] + x[s + 6] for s in range(6)]
    o = [x[s] - x[s + 6] for s in range(6)]
    ee = [e[s] + e[s + 3] for s in range(3)]
    eo = [e[s] - e[s + 3] for s in range(3)]
    sum12 = ee[1] + ee[2]
    d15, s15, d24, s24 = o[1] - o[5], o[1] + o[5], o[2] - o[4], o[2] + o[4]
    a, b = o[0] + 0.5 * d24, HALF3 * d15
    c, d = 0.5 * s15 + o[3], HALF3 * s24
    return [
        (ee[0] + sum12, eo[0] - eo[1] + eo[2]),
        (a + b, c + d),
        (eo[0] + 0.5 * (eo[1] - eo[2]), HALF3 * (eo[1] + eo[2])),
        (o[0] - d24, s15 - o[3]),
        (ee[0] - 0.5 * sum12, HALF3 * (ee[1] - ee[2])),
        (a - b, c - d),
    ]


def inverse12(z):
    (z0, z6), (r1, n1), (r2, n2), (r3, n3), (r4, n4), (r5, n5) = z
    a, b = HALF3 * (r1 - r5), 0.5 * (n1 + n5) + n3
    c, d = 0.5 * (r1 + r5) - r3, HALF3 * (n1 - n5)
    odd = [r1 + r3 + r5, b + a, c + d, n1 - n3 + n5, d - c, b - a]
    low, h4 = z0 - 0.5 * r4, HALF3 * n4
    ee = [z0 + r4, low + h4, low - h4]
    h2, hr = HALF3 * n2, 0.5 * r2
    eo = [z6 + r2, hr + h2 - z6, z6 - hr + h2]
    even = [ee[s] + eo[s] for s in range(3)] + [ee[s] - eo[s] for s in range(3)]
    return [even[s] + odd[s] for s in range(6)] + [even[s] - odd[s] for s in range(6)]


def lanes_of(shape):
    return lax.broadcasted_iota(jnp.int32, shape, len(shape) - 1)


def segments(tiles):
    lane = lanes_of(tiles[0].shape)
    out = [pltpu.roll(tiles[0], HALO, 1)]
    for s in range(1, RADIX):
        shift = 8 * s + HALO
        out.append(pltpu.roll(jnp.where(lane >= WIDE - shift, tiles[s - 1], tiles[s]), shift, 1))
    return out


def joined(segs):
    lane = lanes_of(segs[0].shape)
    out = []
    for t in range(RADIX):
        tile = pltpu.roll(segs[t], WIDE - (8 * t + HALO), 1)
        if t + 1 < RADIX:
            later = pltpu.roll(segs[t + 1], 116 - 8 * t, 1)
            tile = jnp.where(lane < 120 - 8 * t, tile, later)
        out.append(tile)
    return out


def forward_rows(tiles, y_high, y_low, row):
    lane = lanes_of((16, WIDE))
    inside = (lane >= HALO) & (lane < WIDE - HALO)
    classes = forward12(segments(tiles))
    for k, parts in enumerate(classes):
        for at, part in enumerate(parts):
            high, low = split(jnp.where(inside, part, 0.0))
            y_high[k, pl.ds(row, 16), at * WIDE : (at + 1) * WIDE] = high
            y_low[k, pl.ds(row, 16), at * WIDE : (at + 1) * WIDE] = low


def tiles_of(load):
    return [load(pl.ds(t * WIDE, WIDE)) for t in range(RADIX)]


def narrow_tiles(load, lon):
    last = lon - (RADIX - 1) * WIDE
    tiles = [load(pl.ds(t * WIDE, WIDE)) for t in range(RADIX - 1)]
    end = load(pl.ds((RADIX - 1) * WIDE, last))
    return tiles + [jnp.concatenate([end, jnp.zeros((end.shape[0], WIDE - last), jnp.float32)], axis=1)]


def filter_class(k, y_high, y_low, z, cut, wave, f_high, f_low):
    high, low = f_high[k], f_low[k]
    yh, yl = y_high[k], y_low[k]
    coeffs = jnp.dot(
        jnp.concatenate([yh, yl, yh], axis=1),
        jnp.concatenate([high, high, low], axis=0),
        preferred_element_type=jnp.float32,
    )
    limit = cut[...]
    wanted = wave[:, pl.ds(k * 2 * WIDE, 2 * WIDE)]
    keep = jnp.concatenate([limit >= wanted[:, :WIDE], limit >= wanted[:, WIDE:]], axis=1)
    xh, xl = split(jnp.where(keep, coeffs, 0.0))
    z[k] = lax.dot_general(
        jnp.concatenate([xh, xl, xh], axis=1),
        jnp.concatenate([high, high, low], axis=1),
        (((1,), (1,)), ((), ())),
        preferred_element_type=jnp.float32,
    )


def step_kernel(
    lat_count,
    lev_count,
    thick,
    winds,
    cutoff_in,
    wave_in,
    table_high,
    table_low,
    part_winds,
    new_thick,
    delta,
    cutoff,
    wave,
    h_in,
    w_in,
    f_high,
    f_low,
    y_high,
    y_low,
    z,
    field,
    result,
    cut,
    y2_high,
    y2_low,
    z2,
    outer,
    grad,
    cut2,
    out,
    out_delta,
    trig,
    send_minus,
    send_plus,
    from_minus,
    from_plus,
    column,
    below,
    pair,
    sums,
    from_upper,
    from_lower,
    relay,
    shared,
    row_column,
    row_pair,
    row_sums,
    row_slots,
    send_row,
    load_sem,
    store_sem,
    send_sem,
    recv_sem,
):
    levels, rows, lon = thick.shape
    full = RADIX * WIDE
    part = rows // 2
    fields = 3 * levels
    lat, lev = lax.axis_index("lat"), lax.axis_index("lev")
    x, core = lev // 2, lev % 2
    chips = lev_count // 2
    partner = x * 2 + (1 - core)
    chip_at = lambda other: ((other + chips) % chips) * 2 + core
    x_up, x_down = ((x + 1) % chips) * 2 + core, ((x + chips - 1) % chips) * 2 + core
    has_minus, has_plus = lat > 0, lat < lat_count - 1
    lat_minus, lat_plus = jnp.maximum(lat - 1, 0), jnp.minimum(lat + 1, lat_count - 1)
    follows = (lat % 8 == 0) & has_minus
    leads = (lat % 8 == 7) & has_plus

    barrier = pltpu.get_barrier_semaphore()
    for device in ((lat, partner), (lat, x_up), (lat, x_down), (lat, chip_at(x + 2))):
        pl.semaphore_signal(barrier, inc=1, device_id=device, device_id_type=MESH)

    @pl.when(has_minus)
    def _():
        pl.semaphore_signal(barrier, inc=1, device_id=(lat_minus, lev), device_id_type=MESH)

    @pl.when(has_plus & jnp.logical_not(leads))
    def _():
        pl.semaphore_signal(barrier, inc=1, device_id=(lat_plus, lev), device_id_type=MESH)

    loads = [
        pltpu.make_async_copy(source, target, load_sem.at[i])
        for i, (source, target) in enumerate(
            (
                (thick, h_in),
                (winds.at[1], w_in.at[1]),
                (cutoff_in, cutoff),
                (wave_in, wave),
                (table_high, f_high),
                (table_low, f_low),
                (winds.at[0], w_in.at[0]),
            )
        )
    ]
    for load in loads[:3]:
        load.start()

    def remote(source, target, at, device):
        return pltpu.make_async_remote_copy(
            src_ref=source,
            dst_ref=target,
            send_sem=send_sem.at[at],
            recv_sem=recv_sem.at[at],
            device_id=device,
            device_id_type=MESH,
        )

    row32 = lax.broadcasted_iota(jnp.int32, (rows, WIDE), 0)

    def limits():
        limit = jnp.zeros((rows, WIDE), jnp.float32)
        for r in range(rows):
            limit = jnp.where(row32 == r, cutoff[r].astype(jnp.float32), limit)
        for unit in range(fields):
            cut[pl.ds(unit * rows, rows), :] = limit
        cut2[pl.ds(0, rows), :] = limit

    def forward_thick():
        def unit(level, carry):
            for half in range(rows // 16):
                here = pl.ds(half * 16, 16)
                tiles = narrow_tiles(lambda c: h_in[level, here, c], lon)
                forward_rows(tiles, y_high, y_low, (2 * levels + level) * rows + half * 16)
            return carry

        lax.fori_loop(0, levels, unit, 0)

    def forward_winds():
        def unit(index, carry):
            for half in range(rows // 16):
                here = pl.ds(half * 16, 16)
                tiles = narrow_tiles(lambda c: w_in[index // levels, index % levels, here, c], lon)
                forward_rows(tiles, y_high, y_low, index * rows + half * 16)
            return carry

        lax.fori_loop(0, 2 * levels, unit, 0)

    def products(classes):
        for k in classes:
            filter_class(k, y_high, y_low, z, cut, wave, f_high, f_low)

    def inverse():
        def unit(index, carry):
            for half in range(rows // 16):
                here = pl.ds(index * rows + half * 16, 16)
                parts = [(z[k, here, :WIDE], z[k, here, WIDE:]) for k in range(6)]
                for s, value in enumerate(inverse12(parts)):
                    field[index, s, pl.ds(half * 16, 16), :] = value
            return carry

        lax.fori_loop(0, fields, unit, 0)

    loads[0].wait()
    for load in loads[3:]:
        load.start()
    total = h_in[0]
    for level in range(1, levels):
        total = total + h_in[level]
    column[:, pl.ds(full - WIDE, WIDE)] = jnp.zeros((rows, WIDE), jnp.float32)
    column[:, pl.ds(0, lon)] = total
    send_row[0] = column[0:1, :]
    send_row[1] = column[rows - 1 : rows, :]
    loads[1].wait()
    loads[2].wait()
    row8 = lax.broadcasted_iota(jnp.int32, (8, lon), 0)
    for pack, row in ((send_minus, 0), (send_plus, rows - 1)):
        value = jnp.zeros((8, lon), jnp.float32)
        for level in range(levels):
            value = jnp.where(row8 == level, h_in[level, row : row + 1, :], value)
            value = jnp.where(row8 == levels + level, w_in[1, level, row : row + 1, :], value)
        pack[:, pl.ds(full - WIDE, WIDE)] = jnp.broadcast_to(cutoff[row].astype(jnp.float32), (8, WIDE))
        pack[:, pl.ds(0, lon)] = value

    one = lambda flag: jnp.where(flag, 1, 0)
    mine, theirs = pl.multiple_of(core * part, part), pl.multiple_of((1 - core) * part, part)
    upper = jnp.where(core == 0, 0.0, 1.0)
    lower = 1.0 - upper
    chunks = [(8 * r, full // 2 * c) for r in range(part // 8) for c in range(2)]
    pieces = [(pl.ds(r, 8), pl.ds(c, full // 2)) for r, c in chunks]
    places = [(pl.ds(pl.multiple_of(mine + r, 8), 8), pl.ds(c, full // 2)) for r, c in chunks]
    others = [(pl.ds(pl.multiple_of(theirs + r, 8), 8), pl.ds(c, full // 2)) for r, c in chunks]
    count = len(pieces)
    to_pair = remote(column.at[pl.ds(theirs, part), :], pair, 0, (lat, partner))
    to_minus = remote(send_minus, from_plus, 1, (lat_minus, lev))
    to_plus = remote(send_plus, from_minus, 2, (lat_plus, lev))
    down_first = [remote(sums.at[*c], from_upper.at[*c], 3 + i, (lat, x_down)) for i, c in enumerate(pieces)]
    down_later = [remote(relay.at[*c], from_upper.at[*c], 3 + i, (lat, x_down)) for i, c in enumerate(pieces)]
    up_first = [remote(sums.at[*c], from_lower.at[*c], 3 + count + i, (lat, x_up)) for i, c in enumerate(pieces)]
    up_later = [remote(from_lower.at[*c], from_lower.at[*c], 3 + count + i, (lat, x_up)) for i, c in enumerate(pieces)]
    row_pairing = remote(row_column, row_pair, 3 + 3 * count, (lat, partner))
    row_minus = remote(send_row.at[0], row_column.at[1], 4 + 3 * count, (lat_minus, lev))
    row_plus = remote(send_row.at[1], row_column.at[0], 5 + 3 * count, (lat_plus, lev))
    row_links = [remote(row_sums, row_slots.at[j - 1], 5 + 3 * count + j, (lat, chip_at(x - j))) for j in range(1, 4)]
    shares = [remote(column.at[*p], shared.at[*c], 3 + 2 * count + i, (lat, partner)) for i, (p, c) in enumerate(zip(places, pieces))]

    def enter():
        pl.semaphore_wait(barrier, 4 + one(has_minus & jnp.logical_not(follows)) + one(has_plus))
        @pl.when(has_minus & jnp.logical_not(follows))
        def _():
            row_minus.start()

        @pl.when(has_plus)
        def _():
            row_plus.start()

        to_pair.start()

        @pl.when(has_minus & jnp.logical_not(follows))
        def _():
            to_minus.start()

        @pl.when(has_plus)
        def _():
            to_plus.start()

    def first_step():
        to_pair.wait()
        sums[...] = column[pl.ds(mine, part), :] + pair[...]
        for i in range(count):
            @pl.when(x >= 2)
            def _():
                down_first[i].start()

            @pl.when(x == 3)
            def _():
                up_first[i].start()

        @pl.when(x == chips - 1)
        def _():
            from_upper[...] = jnp.zeros_like(from_upper)

        @pl.when(x >= chips - 2)
        def _():
            from_lower[...] = jnp.zeros_like(from_lower)

    def second_step(which):
        for i in which:
            c = pieces[i]
            @pl.when((x == 1) | (x == 2))
            def _():
                down_first[i].wait_recv()

            @pl.when(x == 1)
            def _():
                relay[*c] = sums[*c] + from_upper[*c]
                down_later[i].start()

            @pl.when(x == 0)
            def _():
                up_first[i].wait_recv()
                up_later[i].start()

    def share():
        for i, (p, c) in enumerate(zip(places, pieces)):
            @pl.when(x == 0)
            def _():
                down_first[i].wait_recv()

            @pl.when(x == 1)
            def _():
                up_first[i].wait_recv()

            above = from_upper[*c] + from_lower[*c]
            below[*p] = above + lower * pair[*c]
            column[*p] = above + upper * column[*p]
            shares[i].start()

    def rows_in():
        @pl.when(has_minus)
        def _():
            row_plus.wait_recv()

        @pl.when(follows)
        def _():
            row_minus.start()
            to_minus.start()

        @pl.when(jnp.logical_not(has_minus))
        def _():
            row_column[0] = jnp.zeros((1, full), jnp.float32)

        @pl.when(has_plus)
        def _():
            row_plus.wait_send()
            row_minus.wait_recv()

        @pl.when(jnp.logical_not(has_plus))
        def _():
            row_column[1] = jnp.zeros((1, full), jnp.float32)

        row_pairing.start()

    def neighbours():
        @pl.when(has_minus)
        def _():
            row_minus.wait_send()
            to_minus.wait_send()
            to_plus.wait_recv()

        @pl.when(jnp.logical_not(has_minus))
        def _():
            from_minus[...] = jnp.zeros_like(from_minus)

        @pl.when(has_plus)
        def _():
            to_plus.wait_send()
            to_minus.wait_recv()

        @pl.when(jnp.logical_not(has_plus))
        def _():
            from_plus[...] = jnp.zeros_like(from_plus)


    def row_first():
        row_pairing.wait()
        row_sums[...] = row_column[...] + row_pair[...]
        for j, link in enumerate(row_links, 1):
            @pl.when(x >= j)
            def _():
                link.start()

            @pl.when(x + j >= chips)
            def _():
                row_slots[j - 1] = jnp.zeros((2, 1, full), jnp.float32)

    row_index = (lat * rows + row32).astype(jnp.float32)
    lat_total = lat_count * rows
    center = (row_index + 0.5) * (math.pi / lat_total) - 0.5 * math.pi
    trig[0] = (time_step * coriolis) * jnp.sin(center)
    trig[1] = (0.5 * time_step) * jnp.cos(center)
    trig[2] = (0.25 * time_step) * jnp.sin(row_index * (math.pi / lat_total))
    top, bottom = row32 == 0, row32 == rows - 1

    def down(x, halo):
        return jnp.where(top, halo, pltpu.roll(x, 1, 0))

    def up(x, halo):
        return jnp.where(bottom, halo, pltpu.roll(x, rows - 1, 0))

    def east(x):
        return pltpu.roll(x, WIDE - 1, 1)

    def west(x):
        return pltpu.roll(x, 1, 1)

    def inside(first, last):
        sin_center, cos_center, edge = trig[0], trig[1], trig[2]

        def one_segment(s, carry):
            total = jnp.zeros((rows, WIDE), jnp.float32)
            for level in reversed(range(levels)):
                u, v, h = field[level, s], field[levels + level, s], field[2 * levels + level, s]
                geo = total + 0.5 * h
                total = total + h
                zonal = (0.25 * time_step) * (h + east(h)) * (u + east(u))
                merid = jnp.where(top, 0.0, (h + pltpu.roll(h, 1, 0)) * (v + pltpu.roll(v, 1, 0)) * edge)
                result[2 * levels + level, s] = h - ((zonal - west(zonal)) + (up(merid, 0.0) - merid))
                result[level, s] = u - (0.5 * time_step) * (east(geo) - west(geo)) + sin_center * v
                result[levels + level, s] = v - cos_center * (up(geo, 0.0) - down(geo, 0.0)) - sin_center * u
            return carry

        lax.fori_loop(first, last, one_segment, 0)

    def write_rows(target, source, parts):
        for p in parts:
            here = pl.ds(p * 8, 8)
            tiles = joined([source(s, here) for s in range(RADIX)])
            for t in range(RADIX - 1):
                target[here, t * WIDE : (t + 1) * WIDE] = tiles[t]
            target[here, (RADIX - 1) * WIDE : lon] = tiles[RADIX - 1][:, : lon - (RADIX - 1) * WIDE]

    def write_units(first, parts):
        def unit(level, carry):
            index = first + level
            write_rows(out.at[index], lambda s, here: result[index, s, here, :], parts)
            return carry

        lax.fori_loop(0, levels, unit, 0)

    stores = [
        pltpu.make_async_copy(out.at[pl.ds(0, levels)], part_winds.at[0], store_sem.at[0]),
        pltpu.make_async_copy(out.at[pl.ds(levels, levels)], part_winds.at[1], store_sem.at[1]),
        pltpu.make_async_copy(out.at[pl.ds(2 * levels, levels)], new_thick, store_sem.at[2]),
        pltpu.make_async_copy(out_delta, delta, store_sem.at[3]),
    ]

    def write_first():
        write_units(0, range(4))
        stores[0].start()

    def write_middle():
        write_units(levels, (1, 2))
        write_units(2 * levels, (1, 2))

    def rest_of_loads():
        for load in loads[3:]:
            load.wait()

    def run(*stages):
        for stage in stages:
            stage()

    some = lambda stage, *args: functools.partial(stage, *args)

    turn = follows | leads | (lat == 1)
    @pl.when(turn)
    def _():
        run(enter, limits, forward_thick, first_step, rest_of_loads, forward_winds, some(products, range(3)))
        run(some(second_step, range(count)), some(products, range(3, 6)), share, inverse)
        run(some(inside, 0, RADIX // 2), rows_in, some(inside, RADIX // 2, RADIX), row_first)
        run(write_first, write_middle, neighbours)

    @pl.when(jnp.logical_not(turn))
    def _():
        run(enter, limits, forward_thick, first_step, rest_of_loads, forward_winds, some(products, range(3)))
        run(some(second_step, range(count)), rows_in, some(products, range(3, 6)), row_first, inverse, share)
        run(some(inside, 0, RADIX), write_first, write_middle, neighbours)

    for i, c in enumerate(pieces):
        shares[i].wait()
        below[*others[i]] = shared[*c]

    for j, link in enumerate(row_links, 1):
        @pl.when(x + j < chips)
        def _():
            link.wait_recv()

    sin_center, cos_center, edge = trig[0], trig[1], trig[2]
    last_index = (lat * rows + rows + jnp.zeros((8, WIDE), jnp.int32)).astype(jnp.float32)
    last_edge = (0.25 * time_step) * jnp.sin(last_index * (math.pi / lat_total))
    minus_cut = from_minus[:, full - WIDE :][:, WIDE - 1 :]
    plus_cut = from_plus[:, full - WIDE :][:, WIDE - 1 :]
    cut2[pl.ds(rows, 8), :] = jnp.broadcast_to(minus_cut, (8, WIDE))
    cut2[pl.ds(rows + 8, 8), :] = jnp.broadcast_to(plus_cut, (8, WIDE))
    row16 = lax.broadcasted_iota(jnp.int32, (16, WIDE), 0)
    cut2[pl.ds(rows + 16, 16), :] = jnp.where(row16 == 0, minus_cut[0:1], plus_cut[0:1])
    for half in range(rows // 16):
        forward_rows(tiles_of(lambda c: below[pl.ds(half * 16, 16), c]), y2_high, y2_low, half * 16)
    forward_rows(tiles_of(lambda c: jnp.concatenate([from_minus[:, c], from_plus[:, c]], axis=0)), y2_high, y2_low, rows)
    for at in range(2):
        row_column[at] = row_slots[0, at] + row_slots[1, at] + row_slots[2, at] + lower * row_pair[at]

    def edge_tile(c):
        return jnp.where(row16 == 0, row_column[0, :, c], jnp.where(row16 == 1, row_column[1, :, c], 0.0))

    forward_rows(tiles_of(edge_tile), y2_high, y2_low, rows + 16)
    for k in range(6):
        filter_class(k, y2_high, y2_low, z2, cut2, wave, f_high, f_low)
    for group in range((rows + 32) // 16):
        here = pl.ds(group * 16, 16)
        parts = [(z2[k, here, :WIDE], z2[k, here, WIDE:]) for k in range(6)]
        for s, value in enumerate(inverse12(parts)):
            outer[s, here, :] = value

    eight = lax.broadcasted_iota(jnp.int32, (8, WIDE), 0)
    at_top, at_bottom = eight == 0, eight == 7
    head, tail = pl.ds(0, 8), pl.ds(rows - 8, 8)

    def patch(s, carry):
        total = outer[s, pl.ds(0, rows), :]
        sides = outer[s, pl.ds(rows, 32), :]
        grad[0, s] = -(0.5 * time_step) * (east(total) - west(total))
        grad[1, s] = -cos_center * (up(total, sides[17:18]) - down(total, sides[16:17]))
        minus_total = plus_total = jnp.zeros((1, WIDE), jnp.float32)
        for level in reversed(range(levels)):
            hm, vm = sides[level : level + 1], sides[levels + level : levels + level + 1]
            hp, vp = sides[8 + level : 9 + level], sides[8 + levels + level : 9 + levels + level]
            vi, hi = levels + level, 2 * levels + level
            geo_minus, geo_plus = minus_total + 0.5 * hm, plus_total + 0.5 * hp
            minus_total, plus_total = minus_total + hm, plus_total + hp
            result[vi, s, head, :] += jnp.where(at_top, cos_center[:8] * geo_minus, 0.0)
            result[vi, s, tail, :] -= jnp.where(at_bottom, cos_center[rows - 8 :] * geo_plus, 0.0)
            first = (field[hi, s, head, :] + hm) * (field[vi, s, head, :] + vm) * edge[:8]
            final = (field[hi, s, tail, :] + hp) * (field[vi, s, tail, :] + vp) * last_edge
            result[hi, s, head, :] += jnp.where(at_top, first, 0.0)
            result[hi, s, tail, :] -= jnp.where(at_bottom, final, 0.0)
        return carry

    lax.fori_loop(0, RADIX, patch, 0)
    write_units(levels, (0, 3))
    stores[1].start()
    write_units(2 * levels, (0, 3))
    stores[2].start()
    for which in range(2):
        write_rows(out_delta.at[which], lambda s, here: grad[which, s, here, :], range(4))
    stores[3].start()

    @pl.when(x >= 1)
    def _():
        for link in down_first:
            link.wait_send()

    @pl.when((x == 0) | (x == 3))
    def _():
        for link in up_first:
            link.wait_send()

    for j, link in enumerate(row_links, 1):
        @pl.when(x >= j)
        def _():
            link.wait_send()

    for store in stores:
        store.wait()


def step(shape, winds, thick, cutoff):
    levels, rows, lon = thick.shape
    high, low, wave = filter_tables(lon)
    full = RADIX * WIDE
    part = rows // 2
    units = 3 * levels * rows
    more = rows + 32
    f32 = lambda *dims: pltpu.VMEM(dims, jnp.float32)
    bf16 = lambda *dims: pltpu.VMEM(dims, jnp.bfloat16)
    hbm = pl.BlockSpec(memory_space=pltpu.HBM)
    free = pl.BlockSpec(memory_space=pl.ANY)
    return pl.pallas_call(
        functools.partial(step_kernel, shape["lat"], shape["lev"]),
        out_shape=(
            jax.ShapeDtypeStruct(winds.shape, jnp.float32),
            jax.ShapeDtypeStruct(thick.shape, jnp.float32),
            jax.ShapeDtypeStruct((2, rows, lon), jnp.float32),
        ),
        in_specs=[hbm] * 6,
        out_specs=(free, free, free),
        scratch_shapes=[
            pltpu.SMEM((rows,), jnp.int32),
            f32(1, RADIX * WIDE),
            f32(levels, rows, lon),
            f32(2, levels, rows, lon),
            bf16(*high.shape),
            bf16(*low.shape),
            bf16(6, units, 2 * WIDE),
            bf16(6, units, 2 * WIDE),
            f32(6, units, 2 * WIDE),
            f32(3 * levels, RADIX, rows, WIDE),
            f32(3 * levels, RADIX, rows, WIDE),
            f32(units, WIDE),
            bf16(6, more, 2 * WIDE),
            bf16(6, more, 2 * WIDE),
            f32(6, more, 2 * WIDE),
            f32(RADIX, more, WIDE),
            f32(2, RADIX, rows, WIDE),
            f32(more, WIDE),
            f32(3 * levels, rows, lon),
            f32(2, rows, lon),
            f32(3, rows, WIDE),
            f32(8, full),
            f32(8, full),
            f32(8, full),
            f32(8, full),
            f32(rows, full),
            f32(rows, full),
            f32(part, full),
            f32(part, full),
            f32(part, full),
            f32(part, full),
            f32(part, full),
            f32(part, full),
            f32(2, 1, full),
            f32(2, 1, full),
            f32(2, 1, full),
            f32(3, 2, 1, full),
            f32(2, 1, full),
            pltpu.SemaphoreType.DMA((7,)),
            pltpu.SemaphoreType.DMA((4,)),
            pltpu.SemaphoreType.DMA((21,)),
            pltpu.SemaphoreType.DMA((21,)),
        ],
        compiler_params=pltpu.CompilerParams(collective_id=0, has_side_effects=True, vmem_limit_bytes=24 << 20),
    )(*[pltpu.with_memory_space_constraint(v, pltpu.HBM) for v in (thick, winds, cutoff, jnp.asarray(wave), jnp.asarray(high), jnp.asarray(low))])


def last_kernel(part_winds, part_thick, delta, new_winds, new_thick, w, sem):
    levels = part_thick.shape[0]
    stores = [pltpu.make_async_copy(part_thick, new_thick, sem.at[2 * levels])]
    stores[0].start()
    for f in range(2):
        for level in range(levels):
            w[f, level] = part_winds[f, level] + delta[f]
            store = pltpu.make_async_copy(w.at[f, level], new_winds.at[f, level], sem.at[f * levels + level])
            store.start()
            stores.append(store)
    for store in stores:
        store.wait()


def last(part_winds, part_thick, delta):
    hbm = pl.BlockSpec(memory_space=pltpu.HBM)
    vmem = pl.BlockSpec(memory_space=pltpu.VMEM)
    return pl.pallas_call(
        last_kernel,
        out_shape=(
            jax.ShapeDtypeStruct(part_winds.shape, jnp.float32),
            jax.ShapeDtypeStruct(part_thick.shape, jnp.float32),
        ),
        in_specs=[vmem, vmem, vmem],
        out_specs=(hbm, hbm),
        scratch_shapes=[
            pltpu.VMEM(part_winds.shape, jnp.float32),
            pltpu.SemaphoreType.DMA((2 * part_thick.shape[0] + 1,)),
        ],
        compiler_params=pltpu.CompilerParams(vmem_limit_bytes=8 << 20),
    )(part_winds, part_thick, delta)


def solution(mesh):
    shape = dict(mesh.shape)

    def per_device(winds, thickness, cutoff):
        return last(*step(shape, winds, thickness, cutoff))

    return jax.shard_map(
        per_device,
        mesh=mesh,
        in_specs=(P(None, "lev", "lat", None), P("lev", "lat", None), P("lat")),
        out_specs=(P(None, "lev", "lat", None), P("lev", "lat", None)),
        check_vma=False,
    )
```
